32 devices in a mesh: gx: 4 (over y, x), gy: 8 (over z, core).
Axes of the slice: x: 2, y: 2, z: 4, core: 2. Of those that a mesh axis runs over, the one named last changes fastest.
Arguments:
- parents: bfloat16 [256, 64, 256], P(('gx', 'gy')), may hold values from -6 to 6
- parent_dest: int32 [256], P(('gx', 'gy')), may hold values from -1 to 127, as said below
- skip: bfloat16 [256, 512, 128], P(('gx', 'gy')), may hold values from -6 to 6
- skip_dest: int32 [256], P(('gx', 'gy')), may hold values from -1 to 127, as said below
- neighbours: int32 [128, 26], P(('gx', 'gy')), may hold values from -1 to 127, as said below
- up_weight: bfloat16 [8, 256, 128], replicated, may hold values from -0.375 to 0.375
- conv_weight: bfloat16 [27, 256, 128], replicated, may hold values from -0.078125 to 0.078125
Outputs:
- refined: bfloat16 [128, 512, 128], P(('gx', 'gy'))
The draws below stay inside these ranges and needn't reach their ends.
Inputs may be any that keep to these rules, and one draw needn't show every extreme that they name: `parent_dest`: each child brick index appears exactly once. Child brick c belongs to device c // 4 of the flattened axis gx+gy (gx slowest) and to its slot c % 4; it lies on a device with the same gx index as the slot that names it. One device names at most 1 child bricks of any one device, and in every draw some device names exactly 1 of one device. In every draw some device has all 8 of its slots live. `skip_dest`: each child brick index appears exactly once. Child brick c belongs to device c // 4 of the flattened axis gx+gy (gx slowest) and to its slot c % 4; it lies on a device with the same gx index as the slot that names it. One device names at most 1 child bricks of any one device, and in every draw some device names exactly 1 of one device. In every draw some device has all 8 of its slots live. Direction k = 0..25 enumerates (dx, dy, dz) in the finite set (-1,0,1)^3 with dx slowest and dz fastest, (0,0,0) left out. neighbours[c, k] is the child brick displaced from brick c by (dx, dy, dz) in the brick lattice, or -1 where no brick is there; the relation is symmetric. A brick's neighbours belong to its own device or to the devices just before and just after it on the flattened axis gx+gy.
All inputs are finite; a program needn't handle non-finite values.
Results may differ from the reference program's by a relative error of at most 0.0039.
Values may be sent and summed in bfloat16 or wider, within the bound.
A program may use at most 64 MiB of HBM per device.

```python
import jax
import jax.numpy as jnp
import numpy as np
from jax import lax

C_PARENT = 256
C_CHILD = 128
C_SKIP = 128
C_OUT = 128
BRICKS_DEV = 4
SLOTS_DEV = 8
SLOTS = 256
N_GX = 4
N_GY = 8


neighbour_steps = [(code // 9 - 1, code // 3 % 3 - 1, code % 3 - 1) for code in range(27) if code != 13]


def owner_lists(key):
    bricks_dev = BRICKS_DEV
    slot_count = SLOTS_DEV
    gy_count = N_GY
    subkeys = jax.random.split(key, 4)
    row_keys = jax.random.split(subkeys[0], N_GX)

    def row_counts(row_key):
        perm_key, move_key = jax.random.split(row_key)
        shuffled = jax.random.permutation(perm_key, gy_count)
        transfers = jax.random.randint(move_key, (gy_count,), 0, bricks_dev)
        position = jnp.arange(gy_count)
        pair_idx = jnp.maximum(position - 3, 0) // 2
        is_first = (position >= 3) & ((position - 3) % 2 == 0)
        has_partner = position + 1 < gy_count
        amount = transfers[pair_idx]
        by_pos = jnp.where(is_first, jnp.where(has_partner, bricks_dev + amount, bricks_dev), bricks_dev - amount)
        by_pos = jnp.where(position == 0, slot_count, by_pos)
        by_pos = jnp.where(position == 1, 1, by_pos)
        by_pos = jnp.where(position == 2, bricks_dev - 1, by_pos)
        return jnp.zeros((gy_count,), jnp.int32).at[shuffled].set(by_pos.astype(jnp.int32))
    counts = jax.vmap(row_counts)(row_keys)
    starts = jnp.cumsum(counts, axis=1) - counts
    rotation = jax.random.randint(subkeys[1], (N_GX, 1, 1), 0, gy_count)
    dev_keys = jax.random.split(subkeys[2], N_GX * gy_count)

    def slot_ranking(dev_key):
        return jax.random.permutation(dev_key, slot_count)
    ranking = jax.vmap(slot_ranking)(dev_keys).reshape(N_GX, gy_count, slot_count)
    order_index = starts[:, :, None] + ranking
    owners = (order_index + rotation) % gy_count
    landing = order_index // gy_count
    row_index = jnp.arange(N_GX)[:, None, None]
    child_id = (row_index * gy_count + owners) * bricks_dev + landing
    return jnp.where(ranking < counts[:, :, None], child_id, -1).reshape(-1).astype(jnp.int32)


def draw_parent_dest(key, part):
    return owner_lists(jax.random.fold_in(key, 11))


def draw_skip_dest(key, part):
    return owner_lists(jax.random.fold_in(key, 23))


def draw_neighbours(key, part):
    owner_count = N_GX * N_GY
    bricks_dev = BRICKS_DEV
    layers = bricks_dev // 2
    depth = owner_count * layers
    dev_keys = jax.random.split(jax.random.fold_in(key, 37), owner_count)

    def cell_choice(dev_key):
        return jax.random.permutation(dev_key, 2 * bricks_dev)[:bricks_dev]
    cells = jax.vmap(cell_choice)(dev_keys)
    cell_x = (cells % 2).reshape(-1)
    cell_y = (cells // 2 % 2).reshape(-1)
    cell_z = (cells // 4 + jnp.arange(owner_count)[:, None] * layers).reshape(-1)
    brick_ids = jnp.arange(owner_count * bricks_dev, dtype=jnp.int32)
    lattice = jnp.full((4 * depth,), -1, jnp.int32).at[(cell_x * 2 + cell_y) * depth + cell_z].set(brick_ids)
    steps_table = jnp.asarray(np.array(neighbour_steps, dtype=np.int32))
    near_x = cell_x[:, None] + steps_table[None, :, 0]
    near_y = cell_y[:, None] + steps_table[None, :, 1]
    near_z = cell_z[:, None] + steps_table[None, :, 2]
    inside = (near_x >= 0) & (near_x < 2) & (near_y >= 0) & (near_y < 2) & (near_z >= 0) & (near_z < depth)
    flat_cell = (jnp.clip(near_x, 0, 1) * 2 + jnp.clip(near_y, 0, 1)) * depth + jnp.clip(near_z, 0, depth - 1)
    return jnp.where(inside, lattice[flat_cell], -1).astype(jnp.int32)


def level_of(rng, shape, cuts, low, largest):
    gain, own = 1.0, jax.random.fold_in(rng, 6)
    for dim, shards_of in cuts:
        steps = jnp.exp(jax.random.uniform(jax.random.fold_in(own, dim), (shards_of,), jnp.float32, low / len(cuts), largest / len(cuts)))
        gain = gain * jnp.repeat(steps, shape[dim] // shards_of).reshape([-1 if axis == dim else 1 for axis in range(len(shape))])
    return gain


def normal_values(own_key, extent, spread, reach, cuts=(), held_as=jnp.bfloat16):
    values = spread * jax.random.normal(own_key, extent, jnp.float32)
    if cuts:
        values = values * level_of(own_key, extent, cuts, -0.22, 0.18)
    return jnp.clip(values, -reach, reach).astype(held_as)


def setup_inputs(seed: int = 0) -> dict:
    arg_keys = jax.random.split(jax.random.key(seed), 8)
    return {
        "parents": normal_values(arg_keys[0], (SLOTS, 64, C_PARENT), 1.0, 6.0, ((0, 32),)),
        "parent_dest": draw_parent_dest(jax.random.fold_in(arg_keys[7], 71), 0),
        "skip": normal_values(arg_keys[2], (SLOTS, 512, C_SKIP), 1.0, 6.0, ((0, 32),)),
        "skip_dest": draw_skip_dest(jax.random.fold_in(arg_keys[7], 71), 0),
        "neighbours": draw_neighbours(jax.random.fold_in(arg_keys[7], 71), 0),
        "up_weight": normal_values(arg_keys[5], (8, C_PARENT, C_CHILD), C_PARENT ** -0.5, 0.375),
        "conv_weight": normal_values(arg_keys[6], (27, C_CHILD + C_SKIP, C_OUT), (27 * (C_CHILD + C_SKIP)) ** -0.5, 0.078125),
    }


neighbour_steps = [(code // 9 - 1, (code // 3) % 3 - 1, code % 3 - 1) for code in range(27) if code != 13]


def edge_range(offset):
    if offset < 0:
        return slice(7, 8)
    if offset > 0:
        return slice(0, 1)
    return slice(0, 8)


def upsample(bricks_in, up_weight):
    brick_count = bricks_in.shape[0]
    product = jnp.einsum("nvc,tcd->nvtd", bricks_in.astype(jnp.float32), up_weight.astype(jnp.float32))
    product = product.reshape(brick_count, 4, 4, 4, 2, 2, 2, up_weight.shape[2])
    product = product.transpose(0, 1, 4, 2, 5, 3, 6, 7)
    return product.reshape(brick_count, 512, up_weight.shape[2]).astype(jnp.bfloat16)


def faces_of(volume):
    return jnp.stack([volume[:, 0], volume[:, 7], volume[:, :, 0], volume[:, :, 7], volume[:, :, :, 0], volume[:, :, :, 7]], axis=1)


def assemble(center, faces_pool, lookup):
    pieces = {}
    for direction, (off_x, off_y, off_z) in enumerate(neighbour_steps):
        if off_x != 0:
            surface = faces_pool[:, 1 if off_x < 0 else 0][:, edge_range(off_y), edge_range(off_z)][:, None]
        elif off_y != 0:
            surface = faces_pool[:, 3 if off_y < 0 else 2][:, edge_range(off_x), edge_range(off_z)][:, :, None]
        else:
            surface = faces_pool[:, 5 if off_z < 0 else 4][:, edge_range(off_x), edge_range(off_y)][:, :, :, None]
        column = lookup[:, direction]
        picked = jnp.take(surface, jnp.maximum(column, 0), axis=0)
        pieces[(off_x, off_y, off_z)] = jnp.where((column >= 0)[:, None, None, None, None], picked, jnp.zeros((), picked.dtype))
    pieces[(0, 0, 0)] = center
    return jnp.concatenate([jnp.concatenate([jnp.concatenate([pieces[(off_x, off_y, off_z)] for off_z in (-1, 0, 1)], axis=3) for off_y in (-1, 0, 1)], axis=2) for off_x in (-1, 0, 1)], axis=1)


def convolve(padded, conv_weight):
    brick_count = padded.shape[0]
    rows_all = brick_count * 512
    result = jnp.zeros((rows_all, conv_weight.shape[2]), jnp.float32)
    for tap_index in range(27):
        start_x, start_y, start_z = tap_index // 9, (tap_index // 3) % 3, tap_index % 3
        window = padded[:, start_x:start_x + 8, start_y:start_y + 8, start_z:start_z + 8, :].reshape(rows_all, padded.shape[-1])
        result = result + jnp.dot(window, conv_weight[tap_index], preferred_element_type=jnp.float32)
    return jnp.maximum(result, 0.0).astype(jnp.bfloat16).reshape(brick_count, 512, conv_weight.shape[2])


def reference(parents, parent_dest, skip, skip_dest, neighbours, up_weight, conv_weight):
    brick_total = neighbours.shape[0]
    slot_ids = jnp.arange(parent_dest.shape[0], dtype=jnp.int32)
    parent_of = jnp.zeros((brick_total,), jnp.int32).at[jnp.where(parent_dest >= 0, parent_dest, brick_total)].set(slot_ids, mode="drop")
    skip_of = jnp.zeros((brick_total,), jnp.int32).at[jnp.where(skip_dest >= 0, skip_dest, brick_total)].set(slot_ids, mode="drop")
    block_size = 64
    group_count = brick_total // block_size

    def build_group(group_index):
        first = (group_index * block_size).astype(jnp.int32)
        chosen = lax.dynamic_slice_in_dim(parent_of, first, block_size)
        child_block = upsample(jnp.take(parents, chosen, axis=0), up_weight)
        skip_block = jnp.take(skip, lax.dynamic_slice_in_dim(skip_of, first, block_size), axis=0)
        return jnp.concatenate([child_block, skip_block], axis=-1)

    features = lax.map(build_group, jnp.arange(group_count, dtype=jnp.int32))
    features = features.reshape(brick_total, 8, 8, 8, features.shape[-1])
    faces_pool = faces_of(features)

    def refine(inputs):
        center, lookup = inputs
        return convolve(assemble(center, faces_pool, lookup), conv_weight)

    refined = lax.map(refine, (features.reshape(group_count, block_size, 8, 8, 8, features.shape[-1]), neighbours.reshape(group_count, block_size, 26)))
    return refined.reshape(brick_total, 512, conv_weight.shape[2])
```

```python
import functools

import jax
import jax.numpy as jnp
from jax import lax
from jax.experimental import pallas as pl
from jax.experimental.pallas import tpu as pltpu
from jax.sharding import PartitionSpec as P

steps = [(code // 9 - 1, code // 3 % 3 - 1, code % 3 - 1) for code in range(27) if code != 13]
direction_of = {step: k for k, step in enumerate(steps)}
face_of = [
    (1 if x < 0 else 0) if x and not z else (5 if z < 0 else 4) if z else (3 if y < 0 else 2)
    for x, y, z in steps
]
PITCH = 24
VMEM_LIMIT = 62 * 2**20
MESH = pl.DeviceIdType.MESH


def smem():
    return pl.BlockSpec(memory_space=pltpu.SMEM)


def anywhere():
    return pl.BlockSpec(memory_space=pl.ANY)


def partner(me, step):
    other, bit = me, 1
    while bit <= step:
        if step & bit:
            other = other + bit * (1 - 2 * lax.rem(lax.div(me, bit), 2))
        bit *= 2
    return other


def kernel(
    n_gx,
    n_gy,
    pdest,
    sdest,
    near,
    parents_hbm,
    skip_hbm,
    up_hbm,
    conv_hbm,
    out_hbm,
    parents,
    skip,
    up,
    conv,
    stage_p,
    stage_s,
    recv_p,
    recv_s,
    marks,
    land,
    face_pick,
    spots,
    spread,
    whole,
    ghost,
    own,
    pool_c,
    pool_s,
    halo_c,
    halo_s,
    body,
    even,
    odd,
    right,
    acc,
    result,
    loads,
    sends,
    receives,
    halo_sends,
    halo_receives,
    own_copy,
    outs,
):
    slots = parents.shape[0]
    count = near.shape[0]
    made = whole.shape[2]
    gx, me = lax.axis_index("gx"), lax.axis_index("gy")
    flat = gx * n_gy + me
    first = flat * count
    has_ahead, has_behind = flat < n_gx * n_gy - 1, flat > 0

    def coordinates(device):
        device = lax.max(device, 0)
        return (lax.div(device, n_gy), lax.rem(device, n_gy))

    ahead, behind = coordinates(flat + 1), coordinates(flat - 1)
    order = list(range(n_gy - 1, 0, -1))
    cross = [s for s in order if s >= n_gy // 2]
    rest = [s for s in order if s < n_gy // 2]

    load = [
        pltpu.make_async_copy(parents_hbm, parents, loads.at[0]),
        pltpu.make_async_copy(skip_hbm, skip, loads.at[1]),
        pltpu.make_async_copy(up_hbm, up, loads.at[2]),
        pltpu.make_async_copy(conv_hbm, conv, loads.at[3]),
    ]
    for copy in load:
        copy.start()

    barrier = pltpu.get_barrier_semaphore()
    wraps_ahead = has_ahead & (me == n_gy - 1)
    wraps_behind = has_behind & (me == 0)

    @pl.when(wraps_ahead)
    def _():
        pl.semaphore_signal(barrier, inc=1, device_id=ahead, device_id_type=MESH)

    @pl.when(wraps_behind)
    def _():
        pl.semaphore_signal(barrier, inc=1, device_id=behind, device_id_type=MESH)

    for step in order:
        pl.semaphore_signal(
            barrier, inc=1, device_id={"gy": partner(me, step)}, device_id_type=MESH
        )

    picks = []
    for which, dest in enumerate((pdest, sdest)):
        targets = [dest[s] for s in range(slots)]
        owners = [
            jnp.where(t >= 0, lax.rem(lax.div(lax.max(t, 0), count), n_gy), -1) for t in targets
        ]
        picked = []
        for d in range(n_gy):
            slot, mark = jnp.int32(0), jnp.int32(-1)
            for s in range(slots):
                here = owners[s] == d
                slot = jnp.where(here, s, slot)
                mark = jnp.where(here, targets[s], mark)
            marks[which * n_gy + d] = mark
            picked.append(slot)
        picks.append(picked)

    load[0].wait()
    for d in range(n_gy):
        stage_p[d] = parents[picks[0][d]]
    load[1].wait()
    for d in range(n_gy):
        stage_s[d] = skip[picks[1][d]]

    pl.semaphore_wait(
        barrier, n_gy - 1 + wraps_ahead.astype(jnp.int32) + wraps_behind.astype(jnp.int32)
    )

    def remote(source, landing, kind, step):
        return pltpu.make_async_remote_copy(
            src_ref=source,
            dst_ref=landing,
            send_sem=sends.at[kind, step],
            recv_sem=receives.at[kind, step],
            device_id={"gy": partner(me, step)},
            device_id_type=MESH,
        )

    mark_copies = [remote(marks, land.at[me], 0, s) for s in order]
    parent_copies = [remote(stage_p.at[partner(me, s)], recv_p.at[me], 1, s) for s in order]
    skip_copies = [remote(stage_s.at[partner(me, s)], recv_s.at[me], 2, s) for s in order]
    mine = [
        pltpu.make_async_copy(stage_p.at[me], recv_p.at[me], own_copy.at[0]),
        pltpu.make_async_copy(stage_s.at[me], recv_s.at[me], own_copy.at[1]),
    ]
    early = max(1, len(cross) // 2)
    for copy in mark_copies + parent_copies + skip_copies[:early] + mine:
        copy.start()
    for i in range(2 * n_gy):
        land[me, i] = marks[i]

    last = 6 * count + 2 * count * count

    def tables(b, carry):
        ids = [near[b, k] for k in range(26)]
        for m in range(2 * count):
            wanted = first - count + m if m < count else first + m
            face = jnp.int32(0)
            for k in range(26):
                face = jnp.where(ids[k] == wanted, face_of[25 - k], face)
            face_pick[b * 2 * count + m] = jnp.where(wanted < 0, 0, face)
        for k in range(26):
            off = ids[k] - first
            inside = (off >= 0) & (off < count)
            before = 6 * count + (off + count) * count + b
            after = 6 * count + off * count + b
            spot = jnp.where(inside, off * 6 + face_of[k], jnp.where(off < 0, before, after))
            spot = jnp.where(ids[k] >= 0, spot, last)
            spots[b * 26 + k] = lax.min(lax.max(spot, 0), last)
        return carry

    lax.fori_loop(0, count, tables, 0)

    for copy in load[2:]:
        copy.wait()
    zero = jnp.zeros((made, made), conv.dtype)
    for half in range(2):
        rows = slice(half * made, (half + 1) * made)
        for xx in range(4):
            for yz in range(9):
                at = (xx * 9 + yz) * made
                right[half, at : at + made, 0:made] = (
                    conv[xx * 9 + yz, rows, :] if xx < 3 else zero
                )
                right[half, at : at + made, made:] = (
                    conv[(xx - 1) * 9 + yz, rows, :] if xx > 0 else zero
                )
    for pool in (pool_c, pool_s):
        pool[last] = jnp.zeros(pool.shape[1:], pool.dtype)
    spread[...] = jnp.zeros_like(spread)

    for copy in mark_copies + parent_copies:
        copy.wait_recv()
    mine[0].wait()
    sources = []
    for which in range(2):
        held = [land[d, which * n_gy + me] for d in range(n_gy)]
        of = []
        for b in range(count):
            source = jnp.int32(0)
            for d in range(n_gy):
                source = jnp.where(held[d] == first + b, d, source)
            of.append(source)
        sources.append(of)

    def faces(b, pool):
        for f in range(6):
            edge = 7 * (f % 2)
            if f < 2:
                value = whole[b, edge * 64 : edge * 64 + 64]
            elif f < 4:
                value = jnp.concatenate(
                    [whole[b, x * 64 + edge * 8 : x * 64 + edge * 8 + 8] for x in range(8)], axis=0
                )
            else:
                value = whole[b, pl.ds(edge, 64, stride=8), :]
            value = value.astype(pool.dtype)
            own[b * 6 + f] = value
            pool[b * 6 + f] = value

    def send_halo(pool, halo, kind):
        for b in range(count):
            for m in range(count):
                halo[0, b * count + m] = own[b * 6 + face_pick[b * 2 * count + m]]
                halo[1, b * count + m] = own[b * 6 + face_pick[b * 2 * count + count + m]]
        own_faces, pairs = 6 * count, count * count
        down = pltpu.make_async_remote_copy(
            src_ref=halo.at[0],
            dst_ref=pool.at[pl.ds(own_faces + pairs, pairs)],
            send_sem=halo_sends.at[kind, 0],
            recv_sem=halo_receives.at[kind, 0],
            device_id=behind,
            device_id_type=MESH,
        )
        up_copy = pltpu.make_async_remote_copy(
            src_ref=halo.at[1],
            dst_ref=pool.at[pl.ds(own_faces, pairs)],
            send_sem=halo_sends.at[kind, 1],
            recv_sem=halo_receives.at[kind, 1],
            device_id=ahead,
            device_id_type=MESH,
        )

        @pl.when(has_ahead)
        def _():
            up_copy.start()

        @pl.when(has_behind)
        def _():
            down.start()

        return down, up_copy

    def wait_halo(copies):
        down, up_copy = copies

        @pl.when(has_ahead)
        def _():
            down.wait_recv()

        @pl.when(has_behind)
        def _():
            up_copy.wait_recv()

    def finish_halo(copies):
        down, up_copy = copies

        @pl.when(has_ahead)
        def _():
            up_copy.wait_send()

        @pl.when(has_behind)
        def _():
            down.wait_send()

    def upsample(b, source):
        for half in range(2):
            values = recv_p[source, :, half * 128 : (half + 1) * 128].astype(jnp.float32)
            for c in range(2):
                spread[c * 2 + half, pl.ds(c, 64, stride=2), :] = values
        rows = jnp.concatenate([spread[p] for p in range(4)], axis=1).astype(jnp.bfloat16)
        for a in range(2):
            for e in range(2):
                tap = a * 4 + e * 2
                weight = jnp.concatenate([up[tap], up[tap + 1]], axis=0)
                value = jnp.dot(rows, weight, preferred_element_type=jnp.float32)
                for i in range(4):
                    for j in range(4):
                        at = (2 * i + a) * 64 + (2 * j + e) * 8
                        whole[b, at : at + 8] = value[(i * 4 + j) * 8 : (i * 4 + j) * 8 + 8]

    for b in range(count):
        upsample(b, sources[0][b])
        faces(b, pool_c)
    halo_copies = send_halo(pool_c, halo_c, 0)
    for copy in skip_copies[early:]:
        copy.start()

    def pad(b, pool):
        def column(u, v):
            return (u * 10 + v) * PITCH

        def taken(step):
            return pool.at[spots[b * 26 + direction_of[step]]]

        def part(step, low, high):
            return taken(step)[low:high].astype(jnp.float32)

        for x in range(8):
            for y in range(8):
                at = column(x + 1, y + 1) + 8
                body[at : at + 8] = whole[b, x * 64 + y * 8 : x * 64 + y * 8 + 8]
        for ox in (-1, 1):
            u, ex = (0, 7) if ox < 0 else (9, 0)
            value = part((ox, 0, 0), 0, 64)
            for y in range(8):
                body[column(u, y + 1) + 8 : column(u, y + 1) + 16] = value[y * 8 : y * 8 + 8]
            for oy in (-1, 1):
                v, ey = (0, 7) if oy < 0 else (9, 0)
                low = ey * 8 // 16 * 16
                value = part((ox, oy, 0), low, low + 16)
                body[column(u, v) + 8 : column(u, v) + 16] = value[ey * 8 - low : ey * 8 - low + 8]
        for oy in (-1, 1):
            v = 0 if oy < 0 else 9
            value = part((0, oy, 0), 0, 64)
            for x in range(8):
                body[column(x + 1, v) + 8 : column(x + 1, v) + 16] = value[x * 8 : x * 8 + 8]
        for p, oz in enumerate((-1, 1)):
            z = 7 if oz < 0 else 16
            value = part((0, 0, oz), 0, 64)
            for x in range(8):
                body[pl.ds(column(x + 1, 1) + z, 8, stride=PITCH), :] = value[x * 8 : x * 8 + 8]
            for ox in (-1, 1):
                u, ex = (0, 7) if ox < 0 else (9, 0)
                low = ex * 8 // 16 * 16
                value = part((ox, 0, oz), low, low + 16)
                body[pl.ds(column(u, 1) + z, 8, stride=PITCH), :] = value[
                    ex * 8 - low : ex * 8 - low + 8
                ]
                for oy in (-1, 1):
                    v, ey = (0, 7) if oy < 0 else (9, 0)
                    value = part((ox, oy, oz), low, low + 16)
                    row = ex * 8 + ey - low
                    body[column(u, v) + z : column(u, v) + z + 1] = value[row : row + 1]
            for q, oy in enumerate((-1, 1)):
                v, ey = (0, 7) if oy < 0 else (9, 0)
                ghost[p * 2 + q] = part((0, oy, oz), 0, 64)
                body[pl.ds(column(1, v) + z, 8, stride=10 * PITCH), :] = ghost[
                    p * 2 + q, pl.ds(ey, 8, stride=8), :
                ]
        for dz in range(3):
            for u in range(10):
                blocks = [
                    body[column(u, v) + 7 + dz : column(u, v) + 15 + dz] for v in range(10)
                ]
                even[dz, u * 80 : u * 80 + 80] = jnp.concatenate(blocks, axis=0).astype(even.dtype)
                odd[dz, u * 64 : u * 64 + 64] = jnp.concatenate(blocks[1:9], axis=0).astype(
                    odd.dtype
                )

    def product(half):
        parts = []
        for xx in range(4):
            for dy in range(3):
                for dz in range(3):
                    if dy == 1:
                        rows = [odd[dz, (2 * s + xx) * 64 : (2 * s + xx) * 64 + 64] for s in range(4)]
                    else:
                        at = [(2 * s + xx) * 80 + dy * 8 for s in range(4)]
                        rows = [even[dz, a : a + 64] for a in at]
                    parts.append(jnp.concatenate(rows, axis=0))
        left = jnp.concatenate(parts, axis=1)
        return jnp.dot(left, right[half], preferred_element_type=jnp.float32)

    wait_halo(halo_copies)

    def child_half(b, carry):
        pad(b, pool_c)
        acc[b] = product(0)
        return carry

    lax.fori_loop(0, count, child_half, 0)

    for copy in skip_copies:
        copy.wait_recv()
    mine[1].wait()
    for b in range(count):
        whole[b] = recv_s[sources[1][b]].astype(jnp.float32)
        faces(b, pool_s)
    skip_halo = send_halo(pool_s, halo_s, 1)
    wait_halo(skip_halo)

    def skip_half(b, carry):
        pad(b, pool_s)
        total = jnp.maximum(acc[b] + product(1), 0.0).astype(result.dtype)
        for s in range(4):
            for p in range(2):
                at = (2 * s + p) * 64
                result[b, at : at + 64] = total[s * 64 : s * 64 + 64, p * made : (p + 1) * made]
        pltpu.make_async_copy(result.at[b], out_hbm.at[b], outs.at[b]).start()
        return carry

    lax.fori_loop(0, count, skip_half, 0)

    for copy in mark_copies + parent_copies + skip_copies:
        copy.wait_send()
    finish_halo(halo_copies)
    finish_halo(skip_halo)
    for b in range(count):
        pltpu.make_async_copy(result.at[b], out_hbm.at[b], outs.at[b]).wait()


def per_device(parents, parent_dest, skip, skip_dest, neighbours, up_weight, conv_weight):
    count = neighbours.shape[0]
    n_gx, n_gy = lax.axis_size("gx"), lax.axis_size("gy")
    voxels = skip.shape[1]
    made = conv_weight.shape[2]
    bf16, f32 = jnp.bfloat16, jnp.float32
    pool = (6 * count + 2 * count * count + 1, 64, made)
    dma = pltpu.SemaphoreType.DMA
    return pl.pallas_call(
        functools.partial(kernel, n_gx, n_gy),
        out_shape=jax.ShapeDtypeStruct((count, voxels, made), bf16),
        in_specs=[smem(), smem(), smem()] + [anywhere()] * 4,
        out_specs=anywhere(),
        scratch_shapes=[
            pltpu.VMEM(parents.shape, bf16),
            pltpu.VMEM(skip.shape, bf16),
            pltpu.VMEM(up_weight.shape, bf16),
            pltpu.VMEM(conv_weight.shape, bf16),
            pltpu.VMEM((n_gy,) + parents.shape[1:], bf16),
            pltpu.VMEM((n_gy,) + skip.shape[1:], bf16),
            pltpu.VMEM((n_gy,) + parents.shape[1:], bf16),
            pltpu.VMEM((n_gy,) + skip.shape[1:], bf16),
            pltpu.SMEM((2 * n_gy,), jnp.int32),
            pltpu.SMEM((n_gy, 2 * n_gy), jnp.int32),
            pltpu.SMEM((2 * count * count,), jnp.int32),
            pltpu.SMEM((26 * count,), jnp.int32),
            pltpu.VMEM((4, 128, 128), f32),
            pltpu.VMEM((count, voxels, made), f32),
            pltpu.VMEM((4, 64, made), f32),
            pltpu.VMEM((6 * count, 64, made), bf16),
            pltpu.VMEM(pool, bf16),
            pltpu.VMEM(pool, bf16),
            pltpu.VMEM((2, count * count, 64, made), bf16),
            pltpu.VMEM((2, count * count, 64, made), bf16),
            pltpu.VMEM((100 * PITCH, made), f32),
            pltpu.VMEM((3, 800, made), bf16),
            pltpu.VMEM((3, 640, made), bf16),
            pltpu.VMEM((2, 36 * made, 2 * made), bf16),
            pltpu.VMEM((count, voxels // 2, 2 * made), f32),
            pltpu.VMEM((count, voxels, made), bf16),
            dma((4,)),
            dma((3, n_gy)),
            dma((3, n_gy)),
            dma((2, 2)),
            dma((2, 2)),
            dma((2,)),
            dma((count,)),
        ],
        compiler_params=pltpu.CompilerParams(
            collective_id=0, has_side_effects=True, vmem_limit_bytes=VMEM_LIMIT
        ),
        name="refine_level",
    )(parent_dest, skip_dest, neighbours, parents, skip, up_weight, conv_weight)


def solution(mesh):
    placed = (
        P(("gx", "gy"), None, None),
        P(("gx", "gy")),
        P(("gx", "gy"), None, None),
        P(("gx", "gy")),
        P(("gx", "gy"), None),
        P(),
        P(),
    )
    return jax.shard_map(
        per_device,
        mesh=mesh,
        in_specs=placed,
        out_specs=P(("gx", "gy"), None, None),
        check_vma=False,
    )
```

```python
import functools

import jax
import jax.numpy as jnp
from jax import lax
from jax.experimental import pallas as pl
from jax.experimental.pallas import tpu as pltpu
from jax.sharding import PartitionSpec as P

steps = [(code // 9 - 1, code // 3 % 3 - 1, code % 3 - 1) for code in range(27) if code != 13]
direction_of = {step: k for k, step in enumerate(steps)}
face_of = [
    (1 if x < 0 else 0) if x and not z else (5 if z < 0 else 4) if z else (3 if y < 0 else 2)
    for x, y, z in steps
]
PITCH = 24
VMEM_LIMIT = 62 * 2**20
MESH = pl.DeviceIdType.MESH


def smem():
    return pl.BlockSpec(memory_space=pltpu.SMEM)


def anywhere():
    return pl.BlockSpec(memory_space=pl.ANY)


def partner(me, step):
    other, bit = me, 1
    while bit <= step:
        if step & bit:
            other = other + bit * (1 - 2 * lax.rem(lax.div(me, bit), 2))
        bit *= 2
    return other


def kernel(
    n_gx,
    n_gy,
    pdest,
    sdest,
    near,
    parents_hbm,
    skip_hbm,
    up_hbm,
    conv_hbm,
    out_hbm,
    agreed,
    parents,
    skip,
    up,
    conv,
    stage_p,
    stage_s,
    recv_p,
    recv_s,
    marks,
    land,
    agree,
    agrees,
    face_pick,
    spots,
    spread,
    whole,
    ghost,
    own,
    pool_c,
    pool_s,
    halo_c,
    halo_s,
    body,
    even,
    odd,
    right,
    acc,
    result,
    loads,
    sends,
    receives,
    halo_sends,
    halo_receives,
    own_copy,
    outs,
    agree_sends,
    agree_receives,
):
    slots = parents.shape[0]
    count = near.shape[0]
    made = whole.shape[2]
    gx, me = lax.axis_index("gx"), lax.axis_index("gy")
    flat = gx * n_gy + me
    first = flat * count
    has_ahead, has_behind = flat < n_gx * n_gy - 1, flat > 0

    def coordinates(device):
        device = lax.max(device, 0)
        return (lax.div(device, n_gy), lax.rem(device, n_gy))

    ahead, behind = coordinates(flat + 1), coordinates(flat - 1)
    order = list(range(n_gy - 1, 0, -1))
    cross = [s for s in order if s >= n_gy // 2]
    rest = [s for s in order if s < n_gy // 2]

    load = [
        pltpu.make_async_copy(parents_hbm, parents, loads.at[0]),
        pltpu.make_async_copy(skip_hbm, skip, loads.at[1]),
        pltpu.make_async_copy(up_hbm, up, loads.at[2]),
        pltpu.make_async_copy(conv_hbm, conv, loads.at[3]),
    ]
    for copy in load:
        copy.start()

    barrier = pltpu.get_barrier_semaphore()
    wraps_ahead = has_ahead & (me == n_gy - 1)
    wraps_behind = has_behind & (me == 0)

    @pl.when(wraps_ahead)
    def _():
        pl.semaphore_signal(barrier, inc=1, device_id=ahead, device_id_type=MESH)

    @pl.when(wraps_behind)
    def _():
        pl.semaphore_signal(barrier, inc=1, device_id=behind, device_id_type=MESH)

    for step in order:
        pl.semaphore_signal(
            barrier, inc=1, device_id={"gy": partner(me, step)}, device_id_type=MESH
        )

    for step in range(1, n_gx):
        pl.semaphore_signal(
            barrier, inc=1, device_id={"gx": lax.rem(gx + step, n_gx)}, device_id_type=MESH
        )

    picks = []
    for which, dest in enumerate((pdest, sdest)):
        targets = [dest[s] for s in range(slots)]
        owners = [
            jnp.where(t >= 0, lax.rem(lax.div(lax.max(t, 0), count), n_gy), -1) for t in targets
        ]
        picked = []
        for d in range(n_gy):
            slot, mark = jnp.int32(0), jnp.int32(-1)
            for s in range(slots):
                here = owners[s] == d
                slot = jnp.where(here, s, slot)
                mark = jnp.where(here, targets[s], mark)
            marks[which * n_gy + d] = mark
            picked.append(slot)
        picks.append(picked)

    load[0].wait()
    for d in range(n_gy):
        stage_p[d] = parents[picks[0][d]]
    load[1].wait()
    for d in range(n_gy):
        stage_s[d] = skip[picks[1][d]]

    last = 8 * count

    def tables(b, carry):
        ids = [near[b, k] for k in range(26)]
        offs = [i - first for i in ids]
        enough = carry
        for side in range(2):
            low, high = jnp.int32(6), jnp.int32(-1)
            for k in range(26):
                off = offs[k] if side else offs[k] + 2 * count
                there = (ids[k] >= 0) & (off >= count) & (off < 2 * count)
                low = jnp.where(there, lax.min(low, face_of[25 - k]), low)
                high = jnp.where(there, lax.max(high, face_of[25 - k]), high)
            face_pick[b * 2 + side] = lax.max(high, 0)
            enough = jnp.where((high >= 0) & (low != high), 0, enough)
        for k in range(26):
            off = offs[k]
            inside = (off >= 0) & (off < count)
            spot = jnp.where(inside, off * 6 + face_of[k], 6 * count + off)
            spot = jnp.where(off < 0, 7 * count + off, spot)
            spot = jnp.where(ids[k] >= 0, spot, last)
            spots[b * 26 + k] = lax.min(lax.max(spot, 0), last)
        return enough

    marks[2 * n_gy] = lax.fori_loop(0, count, tables, jnp.int32(1))

    pl.semaphore_wait(
        barrier, n_gx + n_gy - 2 + wraps_ahead.astype(jnp.int32) + wraps_behind.astype(jnp.int32)
    )

    def remote(source, landing, kind, step):
        return pltpu.make_async_remote_copy(
            src_ref=source,
            dst_ref=landing,
            send_sem=sends.at[kind, step],
            recv_sem=receives.at[kind, step],
            device_id={"gy": partner(me, step)},
            device_id_type=MESH,
        )

    mark_copies = [remote(marks, land.at[me], 0, s) for s in order]
    parent_copies = [remote(stage_p.at[partner(me, s)], recv_p.at[me], 1, s) for s in order]
    skip_copies = [remote(stage_s.at[partner(me, s)], recv_s.at[me], 2, s) for s in order]
    mine = [
        pltpu.make_async_copy(stage_p.at[me], recv_p.at[me], own_copy.at[0]),
        pltpu.make_async_copy(stage_s.at[me], recv_s.at[me], own_copy.at[1]),
    ]
    early = max(1, len(cross) // 2)
    for copy in mark_copies + parent_copies + skip_copies[:early] + mine:
        copy.start()
    for i in range(2 * n_gy + 1):
        land[me, i] = marks[i]

    for copy in load[2:]:
        copy.wait()
    zero = jnp.zeros((made, made), conv.dtype)
    for half in range(2):
        rows = slice(half * made, (half + 1) * made)
        for xx in range(4):
            for yz in range(9):
                at = (xx * 9 + yz) * made
                right[half, at : at + made, 0:made] = (
                    conv[xx * 9 + yz, rows, :] if xx < 3 else zero
                )
                right[half, at : at + made, made:] = (
                    conv[(xx - 1) * 9 + yz, rows, :] if xx > 0 else zero
                )
    for pool in (pool_c, pool_s):
        pool[last] = jnp.zeros(pool.shape[1:], pool.dtype)
    spread[...] = jnp.zeros_like(spread)

    for copy in mark_copies + parent_copies:
        copy.wait_recv()
    mine[0].wait()
    enough = land[0, 2 * n_gy]
    for d in range(1, n_gy):
        enough = lax.min(enough, land[d, 2 * n_gy])
    agree[0] = enough
    agrees[gx, 0] = enough
    agree_copies = [
        pltpu.make_async_remote_copy(
            src_ref=agree,
            dst_ref=agrees.at[gx],
            send_sem=agree_sends.at[step],
            recv_sem=agree_receives.at[step],
            device_id={"gx": lax.rem(gx + step, n_gx)},
            device_id_type=MESH,
        )
        for step in range(1, n_gx)
    ]
    for copy in agree_copies:
        copy.start()
    sources = []
    for which in range(2):
        held = [land[d, which * n_gy + me] for d in range(n_gy)]
        of = []
        for b in range(count):
            source = jnp.int32(0)
            for d in range(n_gy):
                source = jnp.where(held[d] == first + b, d, source)
            of.append(source)
        sources.append(of)

    def faces(b, pool):
        for f in range(6):
            edge = 7 * (f % 2)
            if f < 2:
                value = whole[b, edge * 64 : edge * 64 + 64]
            elif f < 4:
                value = jnp.concatenate(
                    [whole[b, x * 64 + edge * 8 : x * 64 + edge * 8 + 8] for x in range(8)], axis=0
                )
            else:
                value = whole[b, pl.ds(edge, 64, stride=8), :]
            value = value.astype(pool.dtype)
            own[b * 6 + f] = value
            pool[b * 6 + f] = value

    def send_halo(pool, halo, kind):
        for b in range(count):
            for side in range(2):
                halo[side, b] = own[b * 6 + face_pick[b * 2 + side]]
        down = pltpu.make_async_remote_copy(
            src_ref=halo.at[0],
            dst_ref=pool.at[pl.ds(7 * count, count)],
            send_sem=halo_sends.at[kind, 0],
            recv_sem=halo_receives.at[kind, 0],
            device_id=behind,
            device_id_type=MESH,
        )
        up_copy = pltpu.make_async_remote_copy(
            src_ref=halo.at[1],
            dst_ref=pool.at[pl.ds(6 * count, count)],
            send_sem=halo_sends.at[kind, 1],
            recv_sem=halo_receives.at[kind, 1],
            device_id=ahead,
            device_id_type=MESH,
        )

        @pl.when(has_ahead)
        def _():
            up_copy.start()

        @pl.when(has_behind)
        def _():
            down.start()

        return down, up_copy

    def wait_halo(copies):
        down, up_copy = copies

        @pl.when(has_ahead)
        def _():
            down.wait_recv()

        @pl.when(has_behind)
        def _():
            up_copy.wait_recv()

    def finish_halo(copies):
        down, up_copy = copies

        @pl.when(has_ahead)
        def _():
            up_copy.wait_send()

        @pl.when(has_behind)
        def _():
            down.wait_send()

    def upsample(b, source):
        for half in range(2):
            values = recv_p[source, :, half * 128 : (half + 1) * 128].astype(jnp.float32)
            for c in range(2):
                spread[c * 2 + half, pl.ds(c, 64, stride=2), :] = values
        rows = jnp.concatenate([spread[p] for p in range(4)], axis=1).astype(jnp.bfloat16)
        for a in range(2):
            for e in range(2):
                tap = a * 4 + e * 2
                weight = jnp.concatenate([up[tap], up[tap + 1]], axis=0)
                value = jnp.dot(rows, weight, preferred_element_type=jnp.float32)
                for i in range(4):
                    for j in range(4):
                        at = (2 * i + a) * 64 + (2 * j + e) * 8
                        whole[b, at : at + 8] = value[(i * 4 + j) * 8 : (i * 4 + j) * 8 + 8]

    for b in range(count):
        upsample(b, sources[0][b])
        faces(b, pool_c)
    halo_copies = send_halo(pool_c, halo_c, 0)
    for copy in skip_copies[early:]:
        copy.start()

    def pad(b, pool):
        def column(u, v):
            return (u * 10 + v) * PITCH

        def taken(step):
            return pool.at[spots[b * 26 + direction_of[step]]]

        def part(step, low, high):
            return taken(step)[low:high].astype(jnp.float32)

        for x in range(8):
            for y in range(8):
                at = column(x + 1, y + 1) + 8
                body[at : at + 8] = whole[b, x * 64 + y * 8 : x * 64 + y * 8 + 8]
        for ox in (-1, 1):
            u, ex = (0, 7) if ox < 0 else (9, 0)
            value = part((ox, 0, 0), 0, 64)
            for y in range(8):
                body[column(u, y + 1) + 8 : column(u, y + 1) + 16] = value[y * 8 : y * 8 + 8]
            for oy in (-1, 1):
                v, ey = (0, 7) if oy < 0 else (9, 0)
                low = ey * 8 // 16 * 16
                value = part((ox, oy, 0), low, low + 16)
                body[column(u, v) + 8 : column(u, v) + 16] = value[ey * 8 - low : ey * 8 - low + 8]
        for oy in (-1, 1):
            v = 0 if oy < 0 else 9
            value = part((0, oy, 0), 0, 64)
            for x in range(8):
                body[column(x + 1, v) + 8 : column(x + 1, v) + 16] = value[x * 8 : x * 8 + 8]
        for p, oz in enumerate((-1, 1)):
            z = 7 if oz < 0 else 16
            value = part((0, 0, oz), 0, 64)
            for x in range(8):
                body[pl.ds(column(x + 1, 1) + z, 8, stride=PITCH), :] = value[x * 8 : x * 8 + 8]
            for ox in (-1, 1):
                u, ex = (0, 7) if ox < 0 else (9, 0)
                low = ex * 8 // 16 * 16
                value = part((ox, 0, oz), low, low + 16)
                body[pl.ds(column(u, 1) + z, 8, stride=PITCH), :] = value[
                    ex * 8 - low : ex * 8 - low + 8
                ]
                for oy in (-1, 1):
                    v, ey = (0, 7) if oy < 0 else (9, 0)
                    value = part((ox, oy, oz), low, low + 16)
                    row = ex * 8 + ey - low
                    body[column(u, v) + z : column(u, v) + z + 1] = value[row : row + 1]
            for q, oy in enumerate((-1, 1)):
                v, ey = (0, 7) if oy < 0 else (9, 0)
                ghost[p * 2 + q] = part((0, oy, oz), 0, 64)
                body[pl.ds(column(1, v) + z, 8, stride=10 * PITCH), :] = ghost[
                    p * 2 + q, pl.ds(ey, 8, stride=8), :
                ]
        for dz in range(3):
            for u in range(10):
                blocks = [
                    body[column(u, v) + 7 + dz : column(u, v) + 15 + dz] for v in range(10)
                ]
                even[dz, u * 80 : u * 80 + 80] = jnp.concatenate(blocks, axis=0).astype(even.dtype)
                odd[dz, u * 64 : u * 64 + 64] = jnp.concatenate(blocks[1:9], axis=0).astype(
                    odd.dtype
                )

    def product(half):
        parts = []
        for xx in range(4):
            for dy in range(3):
                for dz in range(3):
                    if dy == 1:
                        rows = [odd[dz, (2 * s + xx) * 64 : (2 * s + xx) * 64 + 64] for s in range(4)]
                    else:
                        at = [(2 * s + xx) * 80 + dy * 8 for s in range(4)]
                        rows = [even[dz, a : a + 64] for a in at]
                    parts.append(jnp.concatenate(rows, axis=0))
        left = jnp.concatenate(parts, axis=1)
        return jnp.dot(left, right[half], preferred_element_type=jnp.float32)

    wait_halo(halo_copies)

    def child_half(b, carry):
        pad(b, pool_c)
        acc[b] = product(0)
        return carry

    lax.fori_loop(0, count, child_half, 0)

    for copy in skip_copies:
        copy.wait_recv()
    mine[1].wait()
    for b in range(count):
        whole[b] = recv_s[sources[1][b]].astype(jnp.float32)
        faces(b, pool_s)
    skip_halo = send_halo(pool_s, halo_s, 1)
    wait_halo(skip_halo)

    def skip_half(b, carry):
        pad(b, pool_s)
        total = jnp.maximum(acc[b] + product(1), 0.0).astype(result.dtype)
        for s in range(4):
            for p in range(2):
                at = (2 * s + p) * 64
                result[b, at : at + 64] = total[s * 64 : s * 64 + 64, p * made : (p + 1) * made]
        pltpu.make_async_copy(result.at[b], out_hbm.at[b], outs.at[b]).start()
        return carry

    lax.fori_loop(0, count, skip_half, 0)

    for copy in mark_copies + parent_copies + skip_copies:
        copy.wait_send()
    finish_halo(halo_copies)
    finish_halo(skip_halo)
    for copy in agree_copies:
        copy.wait()
    for x in range(n_gx):
        enough = lax.min(enough, agrees[x, 0])
    agreed[0] = enough
    for b in range(count):
        pltpu.make_async_copy(result.at[b], out_hbm.at[b], outs.at[b]).wait()


META = 8


def vmem():
    return pl.BlockSpec(memory_space=pltpu.VMEM)


def pack_kernel(
    gy_count, bricks_dev, pdest, sdest, parents, skip, out_p, out_s, land, sem_p, sem_s
):
    slots, voxels = parents.shape[0], parents.shape[1]
    for d in range(gy_count):
        land[0, d] = -1
        land[1, d] = -1

    def copies(s):
        tp, ts = pdest[s], sdest[s]
        op = lax.rem(lax.div(jnp.maximum(tp, 0), bricks_dev), gy_count)
        os = lax.rem(lax.div(jnp.maximum(ts, 0), bricks_dev), gy_count)
        cp = pltpu.make_async_copy(parents.at[s], out_p.at[op, pl.ds(0, voxels)], sem_p.at[s])
        cs = pltpu.make_async_copy(skip.at[s], out_s.at[os], sem_s.at[s])
        return (tp, op, cp), (ts, os, cs)

    for s in range(slots):
        for which, (t, o, c) in enumerate(copies(s)):

            @pl.when(t >= 0)
            def _():
                land[which, o] = lax.rem(t, bricks_dev)
                c.start()

    for d in range(gy_count):
        half = parents.shape[2] // 2
        for which in range(2):
            mark = jnp.full((META, half), land[which, d], jnp.int32).astype(jnp.float32)
            out_p[d, voxels : voxels + META, which * half : (which + 1) * half] = mark.astype(
                jnp.bfloat16
            )
    for s in range(slots):
        for t, o, c in copies(s):

            @pl.when(t >= 0)
            def _():
                c.wait()


def pack(parent_dest, skip_dest, parents, skip, bricks_dev, gy_count):
    slots, voxels, channels = parents.shape
    return pl.pallas_call(
        functools.partial(pack_kernel, gy_count, bricks_dev),
        out_shape=(
            jax.ShapeDtypeStruct((gy_count, voxels + META, channels), parents.dtype),
            jax.ShapeDtypeStruct((gy_count,) + skip.shape[1:], skip.dtype),
        ),
        in_specs=[smem(), smem(), anywhere(), anywhere()],
        out_specs=(vmem(), vmem()),
        scratch_shapes=[
            pltpu.SMEM((2, gy_count), jnp.int32),
            pltpu.SemaphoreType.DMA((slots,)),
            pltpu.SemaphoreType.DMA((slots,)),
        ],
        compiler_params=pltpu.CompilerParams(vmem_limit_bytes=VMEM_LIMIT),
        name="pack",
    )(parent_dest, skip_dest, parents, skip)


def exchange_kernel(gy_count, in_p, in_s, out_p, out_s, sends, receives, own):
    me = lax.axis_index("gy")
    mine = [
        pltpu.make_async_copy(in_p.at[me], out_p.at[me], own.at[0]),
        pltpu.make_async_copy(in_s.at[me], out_s.at[me], own.at[1]),
    ]
    for copy in mine:
        copy.start()
    barrier = pltpu.get_barrier_semaphore()
    shifts = sorted(range(1, gy_count), key=lambda s: abs(s - gy_count // 2))
    for shift in shifts:
        pl.semaphore_signal(
            barrier,
            inc=1,
            device_id={"gy": lax.rem(me + shift, gy_count)},
            device_id_type=pl.DeviceIdType.MESH,
        )
    pl.semaphore_wait(barrier, gy_count - 1)
    copies = []
    for which, (source, landing) in enumerate(((in_p, out_p), (in_s, out_s))):
        for shift in shifts:
            there = lax.rem(me + shift, gy_count)
            copy = pltpu.make_async_remote_copy(
                src_ref=source.at[there],
                dst_ref=landing.at[me],
                send_sem=sends.at[which, shift],
                recv_sem=receives.at[which, shift],
                device_id={"gy": there},
                device_id_type=pl.DeviceIdType.MESH,
            )
            copy.start()
            copies.append(copy)
    for copy in copies:
        copy.wait()
    for copy in mine:
        copy.wait()


def exchange(in_p, in_s):
    gy_count = in_p.shape[0]
    return pl.pallas_call(
        functools.partial(exchange_kernel, gy_count),
        out_shape=tuple(jax.ShapeDtypeStruct(a.shape, a.dtype) for a in (in_p, in_s)),
        in_specs=[anywhere(), anywhere()],
        out_specs=(anywhere(), anywhere()),
        scratch_shapes=[
            pltpu.SemaphoreType.DMA((2, gy_count)),
            pltpu.SemaphoreType.DMA((2, gy_count)),
            pltpu.SemaphoreType.DMA((2,)),
        ],
        compiler_params=pltpu.CompilerParams(collective_id=2, has_side_effects=True),
        name="exchange",
    )(in_p, in_s)


def halo_kernel(size, inner, to_before, to_after, from_before, from_after, sends, receives):
    me = lax.axis_index("gx") * inner + lax.axis_index("gy")

    def coordinates(device):
        device = lax.max(device, 0)
        return (lax.div(device, inner), lax.rem(device, inner))

    ahead, behind = coordinates(me + 1), coordinates(me - 1)
    has_ahead, has_behind = me < size - 1, me > 0
    barrier = pltpu.get_barrier_semaphore()
    mesh_id = pl.DeviceIdType.MESH

    @pl.when(has_ahead)
    def _():
        pl.semaphore_signal(barrier, inc=1, device_id=ahead, device_id_type=mesh_id)

    @pl.when(has_behind)
    def _():
        pl.semaphore_signal(barrier, inc=1, device_id=behind, device_id_type=mesh_id)

    pl.semaphore_wait(barrier, has_ahead.astype(jnp.int32) + has_behind.astype(jnp.int32))
    up = pltpu.make_async_remote_copy(
        src_ref=to_after,
        dst_ref=from_before,
        send_sem=sends.at[0],
        recv_sem=receives.at[0],
        device_id=ahead,
        device_id_type=mesh_id,
    )
    down = pltpu.make_async_remote_copy(
        src_ref=to_before,
        dst_ref=from_after,
        send_sem=sends.at[1],
        recv_sem=receives.at[1],
        device_id=behind,
        device_id_type=mesh_id,
    )

    @pl.when(has_ahead)
    def _():
        up.start()

    @pl.when(has_behind)
    def _():
        down.start()

    @pl.when(has_ahead)
    def _():
        up.wait_send()
        down.wait_recv()

    @pl.when(has_behind)
    def _():
        down.wait_send()
        up.wait_recv()


def halo(to_before, to_after):
    inner = lax.axis_size("gy")
    size = lax.axis_size("gx") * inner
    return pl.pallas_call(
        functools.partial(halo_kernel, size, inner),
        out_shape=(
            jax.ShapeDtypeStruct(to_after.shape, to_after.dtype),
            jax.ShapeDtypeStruct(to_before.shape, to_before.dtype),
        ),
        in_specs=[anywhere(), anywhere()],
        out_specs=(anywhere(), anywhere()),
        scratch_shapes=[pltpu.SemaphoreType.DMA((2,)), pltpu.SemaphoreType.DMA((2,))],
        compiler_params=pltpu.CompilerParams(collective_id=1, has_side_effects=True),
        name="halo",
    )(to_before, to_after)


def build_kernel(
    source, near, pay, skip, up, feats, faces, before, after, spread, whole, sent
):
    channels = up.shape[1]
    made = up.shape[2]

    @pl.when(pl.program_id(0) == 0)
    def _():
        spread[...] = jnp.zeros_like(spread)

    for half in range(channels // 128):
        values = pay[0, 0:64, half * 128 : (half + 1) * 128].astype(jnp.float32)
        for c in range(2):
            spread[c * (channels // 128) + half, pl.ds(c, 64, stride=2), :] = values
    rows = jnp.concatenate([spread[p] for p in range(spread.shape[0])], axis=1).astype(jnp.bfloat16)
    for a in range(2):
        for b in range(2):
            tap = a * 4 + b * 2
            weight = jnp.concatenate([up[tap], up[tap + 1]], axis=0)
            value = jnp.dot(rows, weight, preferred_element_type=jnp.float32)
            for i in range(4):
                for j in range(4):
                    at = (2 * i + a) * 64 + (2 * j + b) * 8
                    for p in range(made // 128):
                        whole[p, at : at + 8] = value[
                            (i * 4 + j) * 8 : (i * 4 + j) * 8 + 8, p * 128 : (p + 1) * 128
                        ]
    for p in range(made // 128, whole.shape[0]):
        at = p * 128 - made
        whole[p] = skip[0, :, at : at + 128].astype(jnp.float32)
    for p in range(whole.shape[0]):
        lanes = slice(p * 128, (p + 1) * 128)
        feats[0, :, lanes] = whole[p].astype(jnp.bfloat16)
        for side in range(2):
            edge = 7 * side
            faces[0, side, :, lanes] = whole[p, edge * 64 : edge * 64 + 64].astype(jnp.bfloat16)
            faces[0, 2 + side, :, lanes] = jnp.concatenate(
                [whole[p, x * 64 + edge * 8 : x * 64 + edge * 8 + 8] for x in range(8)], axis=0
            ).astype(jnp.bfloat16)
            faces[0, 4 + side, :, lanes] = whole[p, pl.ds(edge, 64, stride=8), :].astype(
                jnp.bfloat16
            )
    brick = pl.program_id(0)
    count = before.shape[1]
    first = (lax.axis_index("gx") * lax.axis_size("gy") + lax.axis_index("gy")) * count
    for m in range(2 * count):
        sent[m] = 0
    for k, face in enumerate(face_of[::-1]):
        n = near[brick, k]
        off = n - first
        spot = jnp.where(off < 0, off + count, jnp.where(off >= count, off, 2 * count))
        sent[jnp.where(n >= 0, spot, 2 * count)] = face
    for m in range(count):
        before[0, m] = faces[0, sent[m]]
        after[0, m] = faces[0, sent[count + m]]


def build(source, near, pay, skip, up_weight, bricks_dev):
    channels, made = up_weight.shape[1:]
    joined = made + skip.shape[2]
    return pl.pallas_call(
        build_kernel,
        out_shape=(
            jax.ShapeDtypeStruct((bricks_dev, 512, joined), jnp.bfloat16),
            jax.ShapeDtypeStruct((bricks_dev, 6, 64, joined), jnp.bfloat16),
            jax.ShapeDtypeStruct((bricks_dev, bricks_dev, 64, joined), jnp.bfloat16),
            jax.ShapeDtypeStruct((bricks_dev, bricks_dev, 64, joined), jnp.bfloat16),
        ),
        grid_spec=pltpu.PrefetchScalarGridSpec(
            num_scalar_prefetch=2,
            grid=(bricks_dev,),
            in_specs=[
                pl.BlockSpec((1,) + pay.shape[1:], lambda b, s, t: (s[0, b], 0, 0)),
                pl.BlockSpec((1,) + skip.shape[1:], lambda b, s, t: (s[1, b], 0, 0)),
                pl.BlockSpec(up_weight.shape, lambda b, s, t: (0, 0, 0)),
            ],
            out_specs=(
                pl.BlockSpec((1, 512, joined), lambda b, s, t: (b, 0, 0)),
                pl.BlockSpec((1, 6, 64, joined), lambda b, s, t: (b, 0, 0, 0)),
                pl.BlockSpec((1, bricks_dev, 64, joined), lambda b, s, t: (b, 0, 0, 0)),
                pl.BlockSpec((1, bricks_dev, 64, joined), lambda b, s, t: (b, 0, 0, 0)),
            ),
            scratch_shapes=[
                pltpu.VMEM((2 * channels // 128, 128, 128), jnp.float32),
                pltpu.VMEM((joined // 128, 512, 128), jnp.float32),
                pltpu.SMEM((2 * bricks_dev + 1,), jnp.int32),
            ],
        ),
        compiler_params=pltpu.CompilerParams(vmem_limit_bytes=VMEM_LIMIT),
        name="build",
    )(source, near, pay, skip, up_weight)


def refine_kernel(
    near,
    feats,
    own,
    before,
    after,
    weight,
    out,
    pool,
    sems,
    body,
    plane,
    left,
    right,
    early,
    late,
):
    brick = pl.program_id(0)
    joined, made = weight.shape[1:]

    @pl.when(brick == 0)
    def _():
        copies, first = [], 0
        for i, part in enumerate((own, before, after)):
            length = part.shape[0]
            copies.append(pltpu.make_async_copy(part, pool.at[pl.ds(first, length)], sems.at[i]))
            copies[-1].start()
            first += length
        for tap in range(9):
            for dz in range(3):
                right[tap * joined : (tap + 1) * joined, dz * made : (dz + 1) * made] = weight[
                    tap * 3 + dz
                ]
        for copy in copies:
            copy.wait()

    count = pl.num_programs(0)
    first = (lax.axis_index("gx") * lax.axis_size("gy") + lax.axis_index("gy")) * count
    ahead = own.shape[0] + count * count + brick
    behind = before.shape[0] - 2 * count * count

    def taken(step, start, length):
        k = direction_of[step]
        n = near[brick, k]
        off = n - first
        spot = jnp.where(off < 0, ahead + off * count, ahead + behind + off * count)
        spot = jnp.where((off >= 0) & (off < count), off * 6 + face_of[k], spot)
        spot = jnp.where(n >= 0, spot, 0)
        low = start // 16 * 16
        high = -(-(start + length) // 16) * 16
        value = pool[spot, low:high, :].astype(jnp.float32)
        return jnp.where(n >= 0, value[start - low : start - low + length], 0.0)

    body[1:9, 1:9] = feats[0].astype(jnp.float32).reshape(8, 8, 8, joined)
    for ox in (-1, 1):
        u = 0 if ox < 0 else 9
        body[u, 1:9] = taken((ox, 0, 0), 0, 64).reshape(8, 8, joined)
        for oy in (-1, 1):
            v, ey = (0, 7) if oy < 0 else (9, 0)
            body[u, v] = taken((ox, oy, 0), ey * 8, 8)
    for oy in (-1, 1):
        v = 0 if oy < 0 else 9
        body[1:9, v] = taken((0, oy, 0), 0, 64).reshape(8, 8, joined)
    for p, oz in enumerate((-1, 1)):
        plane[p, 1:9, 1:9] = taken((0, 0, oz), 0, 64).reshape(8, 8, joined)
        for ox in (-1, 1):
            u, ex = (0, 7) if ox < 0 else (9, 0)
            plane[p, u, 1:9] = taken((ox, 0, oz), ex * 8, 8)
            for oy in (-1, 1):
                v, ey = (0, 7) if oy < 0 else (9, 0)
                row = taken((ox, oy, oz), ex * 8, 8)
                plane[p, u, v : v + 1] = row[ey : ey + 1]
        for oy in (-1, 1):
            v, ey = (0, 7) if oy < 0 else (9, 0)
            value = taken((0, oy, oz), 0, 64).reshape(8, 8, joined)
            plane[p, 1:9, v : v + 1] = value[:, ey : ey + 1]

    for tap in range(9):
        dx, dy = tap // 3, tap % 3
        lanes = slice(tap * joined, (tap + 1) * joined)
        left[0:512, lanes] = (
            body[dx : dx + 8, dy : dy + 8].reshape(512, joined).astype(jnp.bfloat16)
        )
        for p in range(2):
            left[512 + 64 * p : 576 + 64 * p, lanes] = (
                plane[p, dx : dx + 8, dy : dy + 8].reshape(64, joined).astype(jnp.bfloat16)
            )
    total = jnp.dot(left[...], right[...], preferred_element_type=jnp.float32)
    early[1:513] = total[0:512, 0:made]
    early[pl.ds(0, 64, stride=8), :] = total[512:576, 0:made]
    late[7:519] = total[0:512, 2 * made : 3 * made]
    late[pl.ds(15, 64, stride=8), :] = total[576:640, 2 * made : 3 * made]
    result = early[0:512] + total[0:512, made : 2 * made] + late[8:520]
    out[0] = jnp.maximum(result, 0.0).astype(jnp.bfloat16)


def refine(near, feats, own, before, after, conv_weight):
    bricks_dev, voxels, joined = feats.shape
    made = conv_weight.shape[2]
    return pl.pallas_call(
        refine_kernel,
        out_shape=jax.ShapeDtypeStruct((bricks_dev, voxels, made), jnp.bfloat16),
        grid_spec=pltpu.PrefetchScalarGridSpec(
            num_scalar_prefetch=1,
            grid=(bricks_dev,),
            in_specs=[
                pl.BlockSpec((1, voxels, joined), lambda b, s: (b, 0, 0)),
                anywhere(),
                anywhere(),
                anywhere(),
                pl.BlockSpec(conv_weight.shape, lambda b, s: (0, 0, 0)),
            ],
            out_specs=pl.BlockSpec((1, voxels, made), lambda b, s: (b, 0, 0)),
            scratch_shapes=[
                pltpu.VMEM((sum(a.shape[0] for a in (own, before, after)), 64, joined), own.dtype),
                pltpu.SemaphoreType.DMA((3,)),
                pltpu.VMEM((10, 10, 8, joined), jnp.float32),
                pltpu.VMEM((2, 10, 16, joined), jnp.float32),
                pltpu.VMEM((640, 9 * joined), jnp.bfloat16),
                pltpu.VMEM((9 * joined, 3 * made), jnp.bfloat16),
                pltpu.VMEM((520, made), jnp.float32),
                pltpu.VMEM((520, made), jnp.float32),
            ],
        ),
        compiler_params=pltpu.CompilerParams(vmem_limit_bytes=VMEM_LIMIT),
        name="refine",
    )(near, feats, own, before, after, conv_weight)


def general(parents, parent_dest, skip, skip_dest, neighbours, up_weight, conv_weight):
    bricks_dev = neighbours.shape[0]
    gy_count = lax.axis_size("gy")
    sent_p, sent_s = pack(parent_dest, skip_dest, parents, skip, bricks_dev, gy_count)
    came_p, came_s = exchange(sent_p, sent_s)
    voxels, channels = parents.shape[1:]
    spots = jnp.stack([came_p[:, voxels, 0], came_p[:, voxels, channels // 2]]).astype(jnp.int32)
    matches = spots[:, None, :] == jnp.arange(bricks_dev)[None, :, None]
    source = jnp.sum(jnp.where(matches, jnp.arange(gy_count)[None, None, :], 0), axis=2)
    feats, faces, to_before, to_after = build(
        source.astype(jnp.int32), neighbours, came_p, came_s, up_weight, bricks_dev
    )
    flat = (-1,) + faces.shape[2:]
    before, after = halo(to_before.reshape(flat), to_after.reshape(flat))
    return refine(neighbours, feats, faces.reshape(flat), before, after, conv_weight)


def per_device(parents, parent_dest, skip, skip_dest, neighbours, up_weight, conv_weight):
    count = neighbours.shape[0]
    n_gx, n_gy = lax.axis_size("gx"), lax.axis_size("gy")
    voxels = skip.shape[1]
    made = conv_weight.shape[2]
    bf16, f32 = jnp.bfloat16, jnp.float32
    pool = (8 * count + 1, 64, made)
    dma = pltpu.SemaphoreType.DMA
    refined, agreed = pl.pallas_call(
        functools.partial(kernel, n_gx, n_gy),
        out_shape=(
            jax.ShapeDtypeStruct((count, voxels, made), bf16),
            jax.ShapeDtypeStruct((1,), jnp.int32),
        ),
        in_specs=[smem(), smem(), smem()] + [anywhere()] * 4,
        out_specs=(anywhere(), smem()),
        scratch_shapes=[
            pltpu.VMEM(parents.shape, bf16),
            pltpu.VMEM(skip.shape, bf16),
            pltpu.VMEM(up_weight.shape, bf16),
            pltpu.VMEM(conv_weight.shape, bf16),
            pltpu.VMEM((n_gy,) + parents.shape[1:], bf16),
            pltpu.VMEM((n_gy,) + skip.shape[1:], bf16),
            pltpu.VMEM((n_gy,) + parents.shape[1:], bf16),
            pltpu.VMEM((n_gy,) + skip.shape[1:], bf16),
            pltpu.SMEM((2 * n_gy + 1,), jnp.int32),
            pltpu.SMEM((n_gy, 2 * n_gy + 1), jnp.int32),
            pltpu.SMEM((1,), jnp.int32),
            pltpu.SMEM((n_gx, 1), jnp.int32),
            pltpu.SMEM((2 * count,), jnp.int32),
            pltpu.SMEM((26 * count,), jnp.int32),
            pltpu.VMEM((4, 128, 128), f32),
            pltpu.VMEM((count, voxels, made), f32),
            pltpu.VMEM((4, 64, made), f32),
            pltpu.VMEM((6 * count, 64, made), bf16),
            pltpu.VMEM(pool, bf16),
            pltpu.VMEM(pool, bf16),
            pltpu.VMEM((2, count, 64, made), bf16),
            pltpu.VMEM((2, count, 64, made), bf16),
            pltpu.VMEM((100 * PITCH, made), f32),
            pltpu.VMEM((3, 800, made), bf16),
            pltpu.VMEM((3, 640, made), bf16),
            pltpu.VMEM((2, 36 * made, 2 * made), bf16),
            pltpu.VMEM((count, voxels // 2, 2 * made), f32),
            pltpu.VMEM((count, voxels, made), bf16),
            dma((4,)),
            dma((3, n_gy)),
            dma((3, n_gy)),
            dma((2, 2)),
            dma((2, 2)),
            dma((2,)),
            dma((count,)),
            dma((n_gx,)),
            dma((n_gx,)),
        ],
        compiler_params=pltpu.CompilerParams(
            collective_id=0, has_side_effects=True, vmem_limit_bytes=VMEM_LIMIT
        ),
        name="refine_level",
    )(parent_dest, skip_dest, neighbours, parents, skip, up_weight, conv_weight)
    return lax.cond(
        agreed[0] > 0,
        lambda: refined,
        lambda: general(
            parents, parent_dest, skip, skip_dest, neighbours, up_weight, conv_weight
        ),
    )


def solution(mesh):
    placed = (
        P(("gx", "gy"), None, None),
        P(("gx", "gy")),
        P(("gx", "gy"), None, None),
        P(("gx", "gy")),
        P(("gx", "gy"), None),
        P(),
        P(),
    )
    return jax.shard_map(
        per_device,
        mesh=mesh,
        in_specs=placed,
        out_specs=P(("gx", "gy"), None, None),
        check_vma=False,
    )
```

```python
import functools

import jax
import jax.numpy as jnp
from jax import lax
from jax.experimental import pallas as pl
from jax.experimental.pallas import tpu as pltpu
from jax.sharding import PartitionSpec as P

steps = [(code // 9 - 1, code // 3 % 3 - 1, code % 3 - 1) for code in range(27) if code != 13]
direction_of = {step: k for k, step in enumerate(steps)}
face_of = [
    (1 if x < 0 else 0) if x and not z else (5 if z < 0 else 4) if z else (3 if y < 0 else 2)
    for x, y, z in steps
]
PITCH = 24
VMEM_LIMIT = 24 * 2**20
SHELL, INSIDE = 296, 216
MESH = pl.DeviceIdType.MESH


def smem():
    return pl.BlockSpec(memory_space=pltpu.SMEM)


def anywhere():
    return pl.BlockSpec(memory_space=pl.ANY)


def partner(me, step):
    other, bit = me, 1
    while bit <= step:
        if step & bit:
            other = other + bit * (1 - 2 * lax.rem(lax.div(me, bit), 2))
        bit *= 2
    return other


def column(u, v):
    return (u * 10 + v) * PITCH


def product(even, odd, right):
    parts = []
    for xx in range(4):
        for dy in range(3):
            for dz in range(3):
                if dy == 1:
                    rows = [odd[dz, (2 * s + xx) * 64 : (2 * s + xx) * 64 + 64] for s in range(4)]
                else:
                    at = [(2 * s + xx) * 80 + dy * 8 for s in range(4)]
                    rows = [even[dz, a : a + 64] for a in at]
                parts.append(jnp.concatenate(rows, axis=0))
    left = jnp.concatenate(parts, axis=1)
    return jnp.dot(left, right[...], preferred_element_type=jnp.float32)


def kernel(
    n_gx,
    n_gy,
    pdest,
    sdest,
    near,
    parents_hbm,
    skip_hbm,
    up_hbm,
    conv_hbm,
    acc,
    even_s,
    odd_s,
    right_s,
    agreed,
    parents,
    skip,
    up,
    conv,
    stage_p,
    stage_shell,
    stage_inside,
    recv_p,
    recv_shell,
    recv_inside,
    marks,
    land,
    chosen,
    flag,
    flags,
    wide,
    strip,
    agree,
    agrees,
    face_pick,
    spots,
    spread,
    whole,
    ghost,
    own,
    pool_c,
    pool_s,
    halo_c,
    halo_s,
    body,
    body_s,
    even,
    odd,
    right,
    loads,
    sends,
    receives,
    halo_sends,
    halo_receives,
    own_copy,
    agree_sends,
    agree_receives,
):
    slots = parents.shape[0]
    count = near.shape[0]
    made = whole.shape[2]
    gx, me = lax.axis_index("gx"), lax.axis_index("gy")
    flat = gx * n_gy + me
    first = flat * count
    has_ahead, has_behind = flat < n_gx * n_gy - 1, flat > 0

    def coordinates(device):
        device = lax.max(device, 0)
        return (lax.div(device, n_gy), lax.rem(device, n_gy))

    ahead, behind = coordinates(flat + 1), coordinates(flat - 1)
    order = list(range(n_gy - 1, 0, -1))
    cross = [s for s in order if s >= n_gy // 2]
    rest = [s for s in order if s < n_gy // 2]

    load = [
        pltpu.make_async_copy(parents_hbm, parents, loads.at[0]),
        pltpu.make_async_copy(skip_hbm, skip, loads.at[1]),
        pltpu.make_async_copy(up_hbm, up, loads.at[2]),
        pltpu.make_async_copy(conv_hbm, conv, loads.at[3]),
    ]
    for copy in load:
        copy.start()

    barrier = pltpu.get_barrier_semaphore()
    wraps_ahead = has_ahead & (me == n_gy - 1)
    wraps_behind = has_behind & (me == 0)

    @pl.when(wraps_ahead)
    def _():
        pl.semaphore_signal(barrier, inc=1, device_id=ahead, device_id_type=MESH)

    @pl.when(wraps_behind)
    def _():
        pl.semaphore_signal(barrier, inc=1, device_id=behind, device_id_type=MESH)

    for step in order:
        pl.semaphore_signal(
            barrier, inc=1, device_id={"gy": partner(me, step)}, device_id_type=MESH
        )

    for step in range(1, n_gx):
        pl.semaphore_signal(
            barrier, inc=1, device_id={"gx": lax.rem(gx + step, n_gx)}, device_id_type=MESH
        )

    for which, dest in enumerate((pdest, sdest)):
        targets = [dest[s] for s in range(slots)]
        owners = [
            jnp.where(t >= 0, lax.rem(lax.div(lax.max(t, 0), count), n_gy), -1) for t in targets
        ]
        for d in range(n_gy):
            slot, mark = jnp.int32(0), jnp.int32(-1)
            for s in range(slots):
                here = owners[s] == d
                slot = jnp.where(here, s, slot)
                mark = jnp.where(here, targets[s], mark)
            marks[which * n_gy + d] = mark
            chosen[which * n_gy + d] = slot

    load[0].wait()
    for d in range(n_gy):
        stage_p[d] = parents[chosen[d]]
    load[1].wait()

    def split(d, carry):
        wide[...] = skip[chosen[n_gy + d]].astype(jnp.float32)
        columns = [wide[0:64], wide[448:512]]
        for x in range(1, 7):
            columns += [wide[x * 64 : x * 64 + 8], wide[x * 64 + 56 : x * 64 + 64]]
        stage_shell[d, 0:224] = jnp.concatenate(columns, axis=0).astype(stage_shell.dtype)
        for i in range(12):
            z, x = i // 6 * 7, i % 6 + 1
            strip[6 * i : 6 * i + 8] = wide[pl.ds(x * 64 + 8 + z, 8, stride=8), :]
        stage_shell[d, 224:304] = strip[0:80].astype(stage_shell.dtype)
        for i in range(36):
            at = (i // 6 + 1) * 64 + (i % 6 + 1) * 8 + 1
            strip[80 + 6 * i : 88 + 6 * i] = wide[at : at + 8]
        stage_inside[d] = strip[80:304].astype(stage_inside.dtype)
        return carry

    lax.fori_loop(0, n_gy, split, 0)

    pl.semaphore_wait(
        barrier, n_gx + n_gy - 2 + wraps_ahead.astype(jnp.int32) + wraps_behind.astype(jnp.int32)
    )

    def remote(source, landing, kind, step):
        return pltpu.make_async_remote_copy(
            src_ref=source,
            dst_ref=landing,
            send_sem=sends.at[kind, step],
            recv_sem=receives.at[kind, step],
            device_id={"gy": partner(me, step)},
            device_id_type=MESH,
        )

    mark_copies = [remote(marks, land.at[me], 0, s) for s in order]
    parent_copies = [remote(stage_p.at[partner(me, s)], recv_p.at[me], 1, s) for s in order]
    shell_copies, inside_copies = [
        [remote(stage.at[partner(me, s), pl.ds(0, size)], recv.at[me, pl.ds(0, size)], kind, s) for s in order]
        for kind, stage, recv, size in (
            (2, stage_shell, recv_shell, SHELL),
            (3, stage_inside, recv_inside, INSIDE),
        )
    ]
    flag_copies = [remote(flag, flags.at[me], 4, s) for s in order]
    mine = [
        pltpu.make_async_copy(stage.at[me], recv.at[me], own_copy.at[i])
        for i, (stage, recv) in enumerate(
            ((stage_p, recv_p), (stage_shell, recv_shell), (stage_inside, recv_inside))
        )
    ]
    early = max(1, len(cross) // 2)
    for copy in mark_copies + parent_copies + shell_copies[:early] + mine:
        copy.start()
    for i in range(2 * n_gy):
        land[me, i] = marks[i]

    last = 8 * count

    def tables(b, carry):
        ids = [near[b, k] for k in range(26)]
        offs = [i - first for i in ids]
        enough = carry
        for side in range(2):
            low, high = jnp.int32(6), jnp.int32(-1)
            for k in range(26):
                off = offs[k] if side else offs[k] + 2 * count
                there = (ids[k] >= 0) & (off >= count) & (off < 2 * count)
                low = jnp.where(there, lax.min(low, face_of[25 - k]), low)
                high = jnp.where(there, lax.max(high, face_of[25 - k]), high)
            face_pick[b * 2 + side] = lax.max(high, 0)
            enough = jnp.where((high >= 0) & (low != high), 0, enough)
        for k in range(26):
            off = offs[k]
            inside = (off >= 0) & (off < count)
            spot = jnp.where(inside, off * 6 + face_of[k], 6 * count + off)
            spot = jnp.where(off < 0, 7 * count + off, spot)
            spot = jnp.where(ids[k] >= 0, spot, last)
            spots[b * 26 + k] = lax.min(lax.max(spot, 0), last)
        return enough

    flag[0] = lax.fori_loop(0, count, tables, jnp.int32(1))
    for copy in flag_copies:
        copy.start()
    flags[me, 0] = flag[0]


    for copy in load[2:]:
        copy.wait()
    zero = jnp.zeros((made, made), conv.dtype)
    for half, into in enumerate((right, right_s)):
        rows = slice(half * made, (half + 1) * made)
        for xx in range(4):
            for yz in range(9):
                at = (xx * 9 + yz) * made
                into[at : at + made, 0:made] = conv[xx * 9 + yz, rows, :] if xx < 3 else zero
                into[at : at + made, made:] = conv[(xx - 1) * 9 + yz, rows, :] if xx > 0 else zero
    for pool in (pool_c, pool_s):
        pool[last] = jnp.zeros(pool.shape[1:], pool.dtype)
    spread[...] = jnp.zeros_like(spread)

    for copy in mark_copies + parent_copies:
        copy.wait_recv()
    mine[0].wait()
    sources = []
    for which in range(2):
        held = [land[d, which * n_gy + me] for d in range(n_gy)]
        of = []
        for b in range(count):
            source = jnp.int32(0)
            for d in range(n_gy):
                source = jnp.where(held[d] == first + b, d, source)
            of.append(source)
        sources.append(of)

    def faces(b, pool):
        for f in range(6):
            edge = 7 * (f % 2)
            if f < 2:
                value = whole[b, edge * 64 : edge * 64 + 64]
            elif f < 4:
                value = jnp.concatenate(
                    [whole[b, x * 64 + edge * 8 : x * 64 + edge * 8 + 8] for x in range(8)], axis=0
                )
            else:
                value = whole[b, pl.ds(edge, 64, stride=8), :]
            value = value.astype(pool.dtype)
            own[b * 6 + f] = value
            pool[b * 6 + f] = value

    def faces_of_body(b, pool):
        for f in range(6):
            edge = 7 * (f % 2)
            if f < 2:
                rows = [body_s[b, pl.ds(column(edge + 1, y + 1) + 8, 8), :] for y in range(8)]
            elif f < 4:
                rows = [body_s[b, pl.ds(column(x + 1, edge + 1) + 8, 8), :] for x in range(8)]
            else:
                rows = [
                    body_s[b, pl.ds(column(x + 1, 1) + 8 + edge, 8, stride=PITCH), :]
                    for x in range(8)
                ]
            value = jnp.concatenate(rows, axis=0).astype(pool.dtype)
            own[b * 6 + f] = value
            pool[b * 6 + f] = value

    def send_halo(pool, halo, kind):
        for b in range(count):
            for side in range(2):
                halo[side, b] = own[b * 6 + face_pick[b * 2 + side]]
        down = pltpu.make_async_remote_copy(
            src_ref=halo.at[0],
            dst_ref=pool.at[pl.ds(7 * count, count)],
            send_sem=halo_sends.at[kind, 0],
            recv_sem=halo_receives.at[kind, 0],
            device_id=behind,
            device_id_type=MESH,
        )
        up_copy = pltpu.make_async_remote_copy(
            src_ref=halo.at[1],
            dst_ref=pool.at[pl.ds(6 * count, count)],
            send_sem=halo_sends.at[kind, 1],
            recv_sem=halo_receives.at[kind, 1],
            device_id=ahead,
            device_id_type=MESH,
        )

        @pl.when(has_ahead)
        def _():
            up_copy.start()

        @pl.when(has_behind)
        def _():
            down.start()

        return down, up_copy

    def wait_halo(copies):
        down, up_copy = copies

        @pl.when(has_ahead)
        def _():
            down.wait_recv()

        @pl.when(has_behind)
        def _():
            up_copy.wait_recv()

    def finish_halo(copies):
        down, up_copy = copies

        @pl.when(has_ahead)
        def _():
            up_copy.wait_send()

        @pl.when(has_behind)
        def _():
            down.wait_send()

    def upsample(b, source):
        for half in range(2):
            values = recv_p[source, :, half * 128 : (half + 1) * 128].astype(jnp.float32)
            for c in range(2):
                spread[c * 2 + half, pl.ds(c, 64, stride=2), :] = values
        rows = jnp.concatenate([spread[p] for p in range(4)], axis=1).astype(jnp.bfloat16)
        for a in range(2):
            for e in range(2):
                tap = a * 4 + e * 2
                weight = jnp.concatenate([up[tap], up[tap + 1]], axis=0)
                value = jnp.dot(rows, weight, preferred_element_type=jnp.float32)
                for i in range(4):
                    for j in range(4):
                        at = (2 * i + a) * 64 + (2 * j + e) * 8
                        whole[b, at : at + 8] = value[(i * 4 + j) * 8 : (i * 4 + j) * 8 + 8]

    for b in range(count):
        upsample(b, sources[0][b])
        faces(b, pool_c)
    halo_copies = send_halo(pool_c, halo_c, 0)
    for copy in shell_copies[early:] + inside_copies[:early]:
        copy.start()

    def surround(b, pool, body):
        def taken(step):
            return pool.at[spots[b * 26 + direction_of[step]]]

        def part(step, low, high):
            return taken(step)[low:high].astype(jnp.float32)

        for ox in (-1, 1):
            u, ex = (0, 7) if ox < 0 else (9, 0)
            value = part((ox, 0, 0), 0, 64)
            for y in range(8):
                body[column(u, y + 1) + 8 : column(u, y + 1) + 16] = value[y * 8 : y * 8 + 8]
            for oy in (-1, 1):
                v, ey = (0, 7) if oy < 0 else (9, 0)
                low = ey * 8 // 16 * 16
                value = part((ox, oy, 0), low, low + 16)
                body[column(u, v) + 8 : column(u, v) + 16] = value[ey * 8 - low : ey * 8 - low + 8]
        for oy in (-1, 1):
            v = 0 if oy < 0 else 9
            value = part((0, oy, 0), 0, 64)
            for x in range(8):
                body[column(x + 1, v) + 8 : column(x + 1, v) + 16] = value[x * 8 : x * 8 + 8]
        for p, oz in enumerate((-1, 1)):
            z = 7 if oz < 0 else 16
            value = part((0, 0, oz), 0, 64)
            for x in range(8):
                body[pl.ds(column(x + 1, 1) + z, 8, stride=PITCH), :] = value[x * 8 : x * 8 + 8]
            for ox in (-1, 1):
                u, ex = (0, 7) if ox < 0 else (9, 0)
                low = ex * 8 // 16 * 16
                value = part((ox, 0, oz), low, low + 16)
                body[pl.ds(column(u, 1) + z, 8, stride=PITCH), :] = value[
                    ex * 8 - low : ex * 8 - low + 8
                ]
                for oy in (-1, 1):
                    v, ey = (0, 7) if oy < 0 else (9, 0)
                    value = part((ox, oy, oz), low, low + 16)
                    row = ex * 8 + ey - low
                    body[column(u, v) + z : column(u, v) + z + 1] = value[row : row + 1]
            for q, oy in enumerate((-1, 1)):
                v, ey = (0, 7) if oy < 0 else (9, 0)
                ghost[p * 2 + q] = part((0, oy, oz), 0, 64)
                body[pl.ds(column(1, v) + z, 8, stride=10 * PITCH), :] = ghost[
                    p * 2 + q, pl.ds(ey, 8, stride=8), :
                ]
    def shifts(body, even, odd):
        for dz in range(3):
            for u in range(10):
                blocks = [
                    body[column(u, v) + 7 + dz : column(u, v) + 15 + dz] for v in range(10)
                ]
                even[dz, u * 80 : u * 80 + 80] = jnp.concatenate(blocks, axis=0).astype(even.dtype)
                odd[dz, u * 64 : u * 64 + 64] = jnp.concatenate(blocks[1:9], axis=0).astype(
                    odd.dtype
                )

    wait_halo(halo_copies)

    def child_half(b, carry):
        for x in range(8):
            for y in range(8):
                at = column(x + 1, y + 1) + 8
                body[at : at + 8] = whole[b, x * 64 + y * 8 : x * 64 + y * 8 + 8]
        surround(b, pool_c, body)
        shifts(body, even, odd)
        acc[b] = product(even, odd, right)
        return carry

    lax.fori_loop(0, count, child_half, 0)

    for copy in shell_copies:
        copy.wait_recv()
    mine[1].wait()
    for b in range(count):
        outer = recv_shell[sources[1][b]].astype(jnp.float32)
        padded = body_s.at[b]
        for y in range(8):
            padded[column(1, y + 1) + 8 : column(1, y + 1) + 16] = outer[y * 8 : y * 8 + 8]
            padded[column(8, y + 1) + 8 : column(8, y + 1) + 16] = outer[64 + y * 8 : 72 + y * 8]
        for x in range(1, 7):
            at = 112 + x * 16
            padded[column(x + 1, 1) + 8 : column(x + 1, 1) + 16] = outer[at : at + 8]
            padded[column(x + 1, 8) + 8 : column(x + 1, 8) + 16] = outer[at + 8 : at + 16]
        strip[0:80] = outer[224:304]
        for i in range(12):
            at = column(i % 6 + 2, 2) + 8 + i // 6 * 7
            padded[pl.ds(at, 6, stride=PITCH), :] = strip[6 * i : 6 * i + 6]
        faces_of_body(b, pool_s)
    skip_halo = send_halo(pool_s, halo_s, 1)
    for copy in inside_copies[early:]:
        copy.start()
    for copy in flag_copies:
        copy.wait_recv()
    enough = flags[0, 0]
    for d in range(1, n_gy):
        enough = lax.min(enough, flags[d, 0])
    agree[0] = enough
    agrees[gx, 0] = enough
    agree_copies = [
        pltpu.make_async_remote_copy(
            src_ref=agree,
            dst_ref=agrees.at[gx],
            send_sem=agree_sends.at[step],
            recv_sem=agree_receives.at[step],
            device_id={"gx": lax.rem(gx + step, n_gx)},
            device_id_type=MESH,
        )
        for step in range(1, n_gx)
    ]
    for copy in agree_copies:
        copy.start()
    wait_halo(skip_halo)
    for b in range(count):
        surround(b, pool_s, body_s.at[b])

    for copy in inside_copies:
        copy.wait_recv()
    mine[2].wait()
    for b in range(count):
        padded = body_s.at[b]
        strip[80:304] = recv_inside[sources[1][b]].astype(jnp.float32)
        for i in range(36):
            at = column(i // 6 + 2, i % 6 + 2) + 9
            padded[at : at + 6] = strip[80 + 6 * i : 86 + 6 * i]
        shifts(padded, even_s.at[b], odd_s.at[b])

    for copy in mark_copies + parent_copies + shell_copies + inside_copies + flag_copies:
        copy.wait_send()
    finish_halo(halo_copies)
    finish_halo(skip_halo)
    for copy in agree_copies:
        copy.wait()
    for x in range(n_gx):
        enough = lax.min(enough, agrees[x, 0])
    agreed[0] = enough

def finish_kernel(acc, even, odd, right, out, result, sems):
    copies = []
    for b in range(acc.shape[0]):
        made = acc.shape[2] // 2
        total = acc[b] + product(even.at[b], odd.at[b], right)
        total = jnp.maximum(total, 0.0).astype(result.dtype)
        for s in range(4):
            for p in range(2):
                at = (2 * s + p) * 64
                result[b, at : at + 64] = total[s * 64 : s * 64 + 64, p * made : (p + 1) * made]
        copies.append(pltpu.make_async_copy(result.at[b], out.at[b], sems.at[b]))
        copies[-1].start()
    for copy in copies:
        copy.wait()


def finish(acc, even, odd, right):
    count, made = acc.shape[0], acc.shape[2] // 2
    shape = (count, 2 * acc.shape[1], made)
    return pl.pallas_call(
        finish_kernel,
        out_shape=pltpu.HBM(shape, jnp.bfloat16),
        in_specs=[vmem()] * 4,
        out_specs=pl.BlockSpec(memory_space=pltpu.HBM),
        scratch_shapes=[
            pltpu.VMEM(shape, jnp.bfloat16),
            pltpu.SemaphoreType.DMA((count,)),
        ],
        compiler_params=pltpu.CompilerParams(vmem_limit_bytes=24 * 2**20),
        name="finish",
    )(acc, even, odd, right)


META = 8


def vmem():
    return pl.BlockSpec(memory_space=pltpu.VMEM)


def pack_kernel(
    gy_count, bricks_dev, pdest, sdest, parents, skip, out_p, out_s, land, sem_p, sem_s
):
    slots, voxels = parents.shape[0], parents.shape[1]
    for d in range(gy_count):
        land[0, d] = -1
        land[1, d] = -1

    def copies(s):
        tp, ts = pdest[s], sdest[s]
        op = lax.rem(lax.div(jnp.maximum(tp, 0), bricks_dev), gy_count)
        os = lax.rem(lax.div(jnp.maximum(ts, 0), bricks_dev), gy_count)
        cp = pltpu.make_async_copy(parents.at[s], out_p.at[op, pl.ds(0, voxels)], sem_p.at[s])
        cs = pltpu.make_async_copy(skip.at[s], out_s.at[os], sem_s.at[s])
        return (tp, op, cp), (ts, os, cs)

    for s in range(slots):
        for which, (t, o, c) in enumerate(copies(s)):

            @pl.when(t >= 0)
            def _():
                land[which, o] = lax.rem(t, bricks_dev)
                c.start()

    for d in range(gy_count):
        half = parents.shape[2] // 2
        for which in range(2):
            mark = jnp.full((META, half), land[which, d], jnp.int32).astype(jnp.float32)
            out_p[d, voxels : voxels + META, which * half : (which + 1) * half] = mark.astype(
                jnp.bfloat16
            )
    for s in range(slots):
        for t, o, c in copies(s):

            @pl.when(t >= 0)
            def _():
                c.wait()


def pack(parent_dest, skip_dest, parents, skip, bricks_dev, gy_count):
    slots, voxels, channels = parents.shape
    return pl.pallas_call(
        functools.partial(pack_kernel, gy_count, bricks_dev),
        out_shape=(
            jax.ShapeDtypeStruct((gy_count, voxels + META, channels), parents.dtype),
            jax.ShapeDtypeStruct((gy_count,) + skip.shape[1:], skip.dtype),
        ),
        in_specs=[smem(), smem(), anywhere(), anywhere()],
        out_specs=(vmem(), vmem()),
        scratch_shapes=[
            pltpu.SMEM((2, gy_count), jnp.int32),
            pltpu.SemaphoreType.DMA((slots,)),
            pltpu.SemaphoreType.DMA((slots,)),
        ],
        compiler_params=pltpu.CompilerParams(vmem_limit_bytes=VMEM_LIMIT),
        name="pack",
    )(parent_dest, skip_dest, parents, skip)


def exchange_kernel(gy_count, in_p, in_s, out_p, out_s, sends, receives, own):
    me = lax.axis_index("gy")
    mine = [
        pltpu.make_async_copy(in_p.at[me], out_p.at[me], own.at[0]),
        pltpu.make_async_copy(in_s.at[me], out_s.at[me], own.at[1]),
    ]
    for copy in mine:
        copy.start()
    barrier = pltpu.get_barrier_semaphore()
    shifts = sorted(range(1, gy_count), key=lambda s: abs(s - gy_count // 2))
    for shift in shifts:
        pl.semaphore_signal(
            barrier,
            inc=1,
            device_id={"gy": lax.rem(me + shift, gy_count)},
            device_id_type=pl.DeviceIdType.MESH,
        )
    pl.semaphore_wait(barrier, gy_count - 1)
    copies = []
    for which, (source, landing) in enumerate(((in_p, out_p), (in_s, out_s))):
        for shift in shifts:
            there = lax.rem(me + shift, gy_count)
            copy = pltpu.make_async_remote_copy(
                src_ref=source.at[there],
                dst_ref=landing.at[me],
                send_sem=sends.at[which, shift],
                recv_sem=receives.at[which, shift],
                device_id={"gy": there},
                device_id_type=pl.DeviceIdType.MESH,
            )
            copy.start()
            copies.append(copy)
    for copy in copies:
        copy.wait()
    for copy in mine:
        copy.wait()


def exchange(in_p, in_s):
    gy_count = in_p.shape[0]
    return pl.pallas_call(
        functools.partial(exchange_kernel, gy_count),
        out_shape=tuple(jax.ShapeDtypeStruct(a.shape, a.dtype) for a in (in_p, in_s)),
        in_specs=[anywhere(), anywhere()],
        out_specs=(anywhere(), anywhere()),
        scratch_shapes=[
            pltpu.SemaphoreType.DMA((2, gy_count)),
            pltpu.SemaphoreType.DMA((2, gy_count)),
            pltpu.SemaphoreType.DMA((2,)),
        ],
        compiler_params=pltpu.CompilerParams(
            collective_id=2, has_side_effects=True, vmem_limit_bytes=2**20
        ),
        name="exchange",
    )(in_p, in_s)


def halo_kernel(size, inner, to_before, to_after, from_before, from_after, sends, receives):
    me = lax.axis_index("gx") * inner + lax.axis_index("gy")

    def coordinates(device):
        device = lax.max(device, 0)
        return (lax.div(device, inner), lax.rem(device, inner))

    ahead, behind = coordinates(me + 1), coordinates(me - 1)
    has_ahead, has_behind = me < size - 1, me > 0
    barrier = pltpu.get_barrier_semaphore()
    mesh_id = pl.DeviceIdType.MESH

    @pl.when(has_ahead)
    def _():
        pl.semaphore_signal(barrier, inc=1, device_id=ahead, device_id_type=mesh_id)

    @pl.when(has_behind)
    def _():
        pl.semaphore_signal(barrier, inc=1, device_id=behind, device_id_type=mesh_id)

    pl.semaphore_wait(barrier, has_ahead.astype(jnp.int32) + has_behind.astype(jnp.int32))
    up = pltpu.make_async_remote_copy(
        src_ref=to_after,
        dst_ref=from_before,
        send_sem=sends.at[0],
        recv_sem=receives.at[0],
        device_id=ahead,
        device_id_type=mesh_id,
    )
    down = pltpu.make_async_remote_copy(
        src_ref=to_before,
        dst_ref=from_after,
        send_sem=sends.at[1],
        recv_sem=receives.at[1],
        device_id=behind,
        device_id_type=mesh_id,
    )

    @pl.when(has_ahead)
    def _():
        up.start()

    @pl.when(has_behind)
    def _():
        down.start()

    @pl.when(has_ahead)
    def _():
        up.wait_send()
        down.wait_recv()

    @pl.when(has_behind)
    def _():
        down.wait_send()
        up.wait_recv()


def halo(to_before, to_after):
    inner = lax.axis_size("gy")
    size = lax.axis_size("gx") * inner
    return pl.pallas_call(
        functools.partial(halo_kernel, size, inner),
        out_shape=(
            jax.ShapeDtypeStruct(to_after.shape, to_after.dtype),
            jax.ShapeDtypeStruct(to_before.shape, to_before.dtype),
        ),
        in_specs=[anywhere(), anywhere()],
        out_specs=(anywhere(), anywhere()),
        scratch_shapes=[pltpu.SemaphoreType.DMA((2,)), pltpu.SemaphoreType.DMA((2,))],
        compiler_params=pltpu.CompilerParams(
            collective_id=1, has_side_effects=True, vmem_limit_bytes=2**20
        ),
        name="halo",
    )(to_before, to_after)


def build_kernel(
    source, near, pay, skip, up, feats, faces, before, after, spread, whole, sent
):
    channels = up.shape[1]
    made = up.shape[2]

    @pl.when(pl.program_id(0) == 0)
    def _():
        spread[...] = jnp.zeros_like(spread)

    for half in range(channels // 128):
        values = pay[0, 0:64, half * 128 : (half + 1) * 128].astype(jnp.float32)
        for c in range(2):
            spread[c * (channels // 128) + half, pl.ds(c, 64, stride=2), :] = values
    rows = jnp.concatenate([spread[p] for p in range(spread.shape[0])], axis=1).astype(jnp.bfloat16)
    for a in range(2):
        for b in range(2):
            tap = a * 4 + b * 2
            weight = jnp.concatenate([up[tap], up[tap + 1]], axis=0)
            value = jnp.dot(rows, weight, preferred_element_type=jnp.float32)
            for i in range(4):
                for j in range(4):
                    at = (2 * i + a) * 64 + (2 * j + b) * 8
                    for p in range(made // 128):
                        whole[p, at : at + 8] = value[
                            (i * 4 + j) * 8 : (i * 4 + j) * 8 + 8, p * 128 : (p + 1) * 128
                        ]
    for p in range(made // 128, whole.shape[0]):
        at = p * 128 - made
        whole[p] = skip[0, :, at : at + 128].astype(jnp.float32)
    for p in range(whole.shape[0]):
        lanes = slice(p * 128, (p + 1) * 128)
        feats[0, :, lanes] = whole[p].astype(jnp.bfloat16)
        for side in range(2):
            edge = 7 * side
            faces[0, side, :, lanes] = whole[p, edge * 64 : edge * 64 + 64].astype(jnp.bfloat16)
            faces[0, 2 + side, :, lanes] = jnp.concatenate(
                [whole[p, x * 64 + edge * 8 : x * 64 + edge * 8 + 8] for x in range(8)], axis=0
            ).astype(jnp.bfloat16)
            faces[0, 4 + side, :, lanes] = whole[p, pl.ds(edge, 64, stride=8), :].astype(
                jnp.bfloat16
            )
    brick = pl.program_id(0)
    count = before.shape[1]
    first = (lax.axis_index("gx") * lax.axis_size("gy") + lax.axis_index("gy")) * count
    for m in range(2 * count):
        sent[m] = 0
    for k, face in enumerate(face_of[::-1]):
        n = near[brick, k]
        off = n - first
        spot = jnp.where(off < 0, off + count, jnp.where(off >= count, off, 2 * count))
        sent[jnp.where(n >= 0, spot, 2 * count)] = face
    for m in range(count):
        before[0, m] = faces[0, sent[m]]
        after[0, m] = faces[0, sent[count + m]]


def build(source, near, pay, skip, up_weight, bricks_dev):
    channels, made = up_weight.shape[1:]
    joined = made + skip.shape[2]
    return pl.pallas_call(
        build_kernel,
        out_shape=(
            jax.ShapeDtypeStruct((bricks_dev, 512, joined), jnp.bfloat16),
            jax.ShapeDtypeStruct((bricks_dev, 6, 64, joined), jnp.bfloat16),
            jax.ShapeDtypeStruct((bricks_dev, bricks_dev, 64, joined), jnp.bfloat16),
            jax.ShapeDtypeStruct((bricks_dev, bricks_dev, 64, joined), jnp.bfloat16),
        ),
        grid_spec=pltpu.PrefetchScalarGridSpec(
            num_scalar_prefetch=2,
            grid=(bricks_dev,),
            in_specs=[
                pl.BlockSpec((1,) + pay.shape[1:], lambda b, s, t: (s[0, b], 0, 0)),
                pl.BlockSpec((1,) + skip.shape[1:], lambda b, s, t: (s[1, b], 0, 0)),
                pl.BlockSpec(up_weight.shape, lambda b, s, t: (0, 0, 0)),
            ],
            out_specs=(
                pl.BlockSpec((1, 512, joined), lambda b, s, t: (b, 0, 0)),
                pl.BlockSpec((1, 6, 64, joined), lambda b, s, t: (b, 0, 0, 0)),
                pl.BlockSpec((1, bricks_dev, 64, joined), lambda b, s, t: (b, 0, 0, 0)),
                pl.BlockSpec((1, bricks_dev, 64, joined), lambda b, s, t: (b, 0, 0, 0)),
            ),
            scratch_shapes=[
                pltpu.VMEM((2 * channels // 128, 128, 128), jnp.float32),
                pltpu.VMEM((joined // 128, 512, 128), jnp.float32),
                pltpu.SMEM((2 * bricks_dev + 1,), jnp.int32),
            ],
        ),
        compiler_params=pltpu.CompilerParams(vmem_limit_bytes=VMEM_LIMIT),
        name="build",
    )(source, near, pay, skip, up_weight)


def refine_kernel(
    near,
    feats,
    own,
    before,
    after,
    weight,
    out,
    pool,
    sems,
    body,
    plane,
    left,
    right,
    early,
    late,
):
    brick = pl.program_id(0)
    joined, made = weight.shape[1:]

    @pl.when(brick == 0)
    def _():
        copies, first = [], 0
        for i, part in enumerate((own, before, after)):
            length = part.shape[0]
            copies.append(pltpu.make_async_copy(part, pool.at[pl.ds(first, length)], sems.at[i]))
            copies[-1].start()
            first += length
        for tap in range(9):
            for dz in range(3):
                right[tap * joined : (tap + 1) * joined, dz * made : (dz + 1) * made] = weight[
                    tap * 3 + dz
                ]
        for copy in copies:
            copy.wait()

    count = pl.num_programs(0)
    first = (lax.axis_index("gx") * lax.axis_size("gy") + lax.axis_index("gy")) * count
    ahead = own.shape[0] + count * count + brick
    behind = before.shape[0] - 2 * count * count

    def taken(step, start, length):
        k = direction_of[step]
        n = near[brick, k]
        off = n - first
        spot = jnp.where(off < 0, ahead + off * count, ahead + behind + off * count)
        spot = jnp.where((off >= 0) & (off < count), off * 6 + face_of[k], spot)
        spot = jnp.where(n >= 0, spot, 0)
        low = start // 16 * 16
        high = -(-(start + length) // 16) * 16
        value = pool[spot, low:high, :].astype(jnp.float32)
        return jnp.where(n >= 0, value[start - low : start - low + length], 0.0)

    body[1:9, 1:9] = feats[0].astype(jnp.float32).reshape(8, 8, 8, joined)
    for ox in (-1, 1):
        u = 0 if ox < 0 else 9
        body[u, 1:9] = taken((ox, 0, 0), 0, 64).reshape(8, 8, joined)
        for oy in (-1, 1):
            v, ey = (0, 7) if oy < 0 else (9, 0)
            body[u, v] = taken((ox, oy, 0), ey * 8, 8)
    for oy in (-1, 1):
        v = 0 if oy < 0 else 9
        body[1:9, v] = taken((0, oy, 0), 0, 64).reshape(8, 8, joined)
    for p, oz in enumerate((-1, 1)):
        plane[p, 1:9, 1:9] = taken((0, 0, oz), 0, 64).reshape(8, 8, joined)
        for ox in (-1, 1):
            u, ex = (0, 7) if ox < 0 else (9, 0)
            plane[p, u, 1:9] = taken((ox, 0, oz), ex * 8, 8)
            for oy in (-1, 1):
                v, ey = (0, 7) if oy < 0 else (9, 0)
                row = taken((ox, oy, oz), ex * 8, 8)
                plane[p, u, v : v + 1] = row[ey : ey + 1]
        for oy in (-1, 1):
            v, ey = (0, 7) if oy < 0 else (9, 0)
            value = taken((0, oy, oz), 0, 64).reshape(8, 8, joined)
            plane[p, 1:9, v : v + 1] = value[:, ey : ey + 1]

    for tap in range(9):
        dx, dy = tap // 3, tap % 3
        lanes = slice(tap * joined, (tap + 1) * joined)
        left[0:512, lanes] = (
            body[dx : dx + 8, dy : dy + 8].reshape(512, joined).astype(jnp.bfloat16)
        )
        for p in range(2):
            left[512 + 64 * p : 576 + 64 * p, lanes] = (
                plane[p, dx : dx + 8, dy : dy + 8].reshape(64, joined).astype(jnp.bfloat16)
            )
    total = jnp.dot(left[...], right[...], preferred_element_type=jnp.float32)
    early[1:513] = total[0:512, 0:made]
    early[pl.ds(0, 64, stride=8), :] = total[512:576, 0:made]
    late[7:519] = total[0:512, 2 * made : 3 * made]
    late[pl.ds(15, 64, stride=8), :] = total[576:640, 2 * made : 3 * made]
    result = early[0:512] + total[0:512, made : 2 * made] + late[8:520]
    out[0] = jnp.maximum(result, 0.0).astype(jnp.bfloat16)


def refine(near, feats, own, before, after, conv_weight):
    bricks_dev, voxels, joined = feats.shape
    made = conv_weight.shape[2]
    return pl.pallas_call(
        refine_kernel,
        out_shape=jax.ShapeDtypeStruct((bricks_dev, voxels, made), jnp.bfloat16),
        grid_spec=pltpu.PrefetchScalarGridSpec(
            num_scalar_prefetch=1,
            grid=(bricks_dev,),
            in_specs=[
                pl.BlockSpec((1, voxels, joined), lambda b, s: (b, 0, 0)),
                anywhere(),
                anywhere(),
                anywhere(),
                pl.BlockSpec(conv_weight.shape, lambda b, s: (0, 0, 0)),
            ],
            out_specs=pl.BlockSpec((1, voxels, made), lambda b, s: (b, 0, 0)),
            scratch_shapes=[
                pltpu.VMEM((sum(a.shape[0] for a in (own, before, after)), 64, joined), own.dtype),
                pltpu.SemaphoreType.DMA((3,)),
                pltpu.VMEM((10, 10, 8, joined), jnp.float32),
                pltpu.VMEM((2, 10, 16, joined), jnp.float32),
                pltpu.VMEM((640, 9 * joined), jnp.bfloat16),
                pltpu.VMEM((9 * joined, 3 * made), jnp.bfloat16),
                pltpu.VMEM((520, made), jnp.float32),
                pltpu.VMEM((520, made), jnp.float32),
            ],
        ),
        compiler_params=pltpu.CompilerParams(vmem_limit_bytes=VMEM_LIMIT),
        name="refine",
    )(near, feats, own, before, after, conv_weight)


def general(parents, parent_dest, skip, skip_dest, neighbours, up_weight, conv_weight):
    bricks_dev = neighbours.shape[0]
    gy_count = lax.axis_size("gy")
    sent_p, sent_s = pack(parent_dest, skip_dest, parents, skip, bricks_dev, gy_count)
    came_p, came_s = exchange(sent_p, sent_s)
    voxels, channels = parents.shape[1:]
    spots = jnp.stack([came_p[:, voxels, 0], came_p[:, voxels, channels // 2]]).astype(jnp.int32)
    matches = spots[:, None, :] == jnp.arange(bricks_dev)[None, :, None]
    source = jnp.sum(jnp.where(matches, jnp.arange(gy_count)[None, None, :], 0), axis=2)
    feats, faces, to_before, to_after = build(
        source.astype(jnp.int32), neighbours, came_p, came_s, up_weight, bricks_dev
    )
    flat = (-1,) + faces.shape[2:]
    before, after = halo(to_before.reshape(flat), to_after.reshape(flat))
    return refine(neighbours, feats, faces.reshape(flat), before, after, conv_weight)


def per_device(parents, parent_dest, skip, skip_dest, neighbours, up_weight, conv_weight):
    count = neighbours.shape[0]
    n_gx, n_gy = lax.axis_size("gx"), lax.axis_size("gy")
    voxels = skip.shape[1]
    made = conv_weight.shape[2]
    bf16, f32 = jnp.bfloat16, jnp.float32
    pool = (8 * count + 1, 64, made)
    dma = pltpu.SemaphoreType.DMA
    width = 2 * made
    acc, even, odd, right, agreed = pl.pallas_call(
        functools.partial(kernel, n_gx, n_gy),
        out_shape=(
            pltpu.VMEM((count, voxels // 2, width), f32),
            pltpu.VMEM((count, 3, 800, made), bf16),
            pltpu.VMEM((count, 3, 640, made), bf16),
            pltpu.VMEM((36 * made, width), bf16),
            jax.ShapeDtypeStruct((1,), jnp.int32),
        ),
        in_specs=[smem(), smem(), smem()] + [anywhere()] * 4,
        out_specs=(vmem(), vmem(), vmem(), vmem(), smem()),
        scratch_shapes=[
            pltpu.VMEM(parents.shape, bf16),
            pltpu.VMEM(skip.shape, bf16),
            pltpu.VMEM(up_weight.shape, bf16),
            pltpu.VMEM(conv_weight.shape, bf16),
            pltpu.VMEM((n_gy,) + parents.shape[1:], bf16),
            pltpu.VMEM((n_gy, 304, skip.shape[2]), bf16),
            pltpu.VMEM((n_gy, 224, skip.shape[2]), bf16),
            pltpu.VMEM((n_gy,) + parents.shape[1:], bf16),
            pltpu.VMEM((n_gy, 304, skip.shape[2]), bf16),
            pltpu.VMEM((n_gy, 224, skip.shape[2]), bf16),
            pltpu.SMEM((2 * n_gy,), jnp.int32),
            pltpu.SMEM((n_gy, 2 * n_gy), jnp.int32),
            pltpu.SMEM((2 * n_gy,), jnp.int32),
            pltpu.SMEM((1,), jnp.int32),
            pltpu.SMEM((n_gy, 1), jnp.int32),
            pltpu.VMEM((voxels, skip.shape[2]), f32),
            pltpu.VMEM((304, skip.shape[2]), f32),
            pltpu.SMEM((1,), jnp.int32),
            pltpu.SMEM((n_gx, 1), jnp.int32),
            pltpu.SMEM((2 * count,), jnp.int32),
            pltpu.SMEM((26 * count,), jnp.int32),
            pltpu.VMEM((4, 128, 128), f32),
            pltpu.VMEM((count, voxels, made), f32),
            pltpu.VMEM((4, 64, made), f32),
            pltpu.VMEM((6 * count, 64, made), bf16),
            pltpu.VMEM(pool, bf16),
            pltpu.VMEM(pool, bf16),
            pltpu.VMEM((2, count, 64, made), bf16),
            pltpu.VMEM((2, count, 64, made), bf16),
            pltpu.VMEM((100 * PITCH, made), f32),
            pltpu.VMEM((count, 100 * PITCH, made), f32),
            pltpu.VMEM((3, 800, made), bf16),
            pltpu.VMEM((3, 640, made), bf16),
            pltpu.VMEM((36 * made, width), bf16),
            dma((4,)),
            dma((5, n_gy)),
            dma((5, n_gy)),
            dma((2, 2)),
            dma((2, 2)),
            dma((3,)),
            dma((n_gx,)),
            dma((n_gx,)),
        ],
        compiler_params=pltpu.CompilerParams(
            collective_id=0, has_side_effects=True, vmem_limit_bytes=40 * 2**20
        ),
        name="refine_level",
    )(parent_dest, skip_dest, neighbours, parents, skip, up_weight, conv_weight)
    return lax.switch(
        agreed[0],
        [
            lambda: general(
                parents, parent_dest, skip, skip_dest, neighbours, up_weight, conv_weight
            ),
            lambda: finish(acc, even, odd, right),
        ],
    )


def solution(mesh):
    placed = (
        P(("gx", "gy"), None, None),
        P(("gx", "gy")),
        P(("gx", "gy"), None, None),
        P(("gx", "gy")),
        P(("gx", "gy"), None),
        P(),
        P(),
    )
    return jax.shard_map(
        per_device,
        mesh=mesh,
        in_specs=placed,
        out_specs=P(("gx", "gy"), None, None),
        check_vma=False,
    )
```

```python
import functools

import jax
import jax.numpy as jnp
from jax import lax
from jax.experimental import pallas as pl
from jax.experimental.pallas import tpu as pltpu
from jax.sharding import PartitionSpec as P

steps = [(code // 9 - 1, code // 3 % 3 - 1, code % 3 - 1) for code in range(27) if code != 13]
direction_of = {step: k for k, step in enumerate(steps)}
face_of = [
    (1 if x < 0 else 0) if x and not z else (5 if z < 0 else 4) if z else (3 if y < 0 else 2)
    for x, y, z in steps
]
PITCH = 24
VMEM_LIMIT = 24 * 2**20
SHELL, INSIDE = 296, 216
MESH = pl.DeviceIdType.MESH


def smem():
    return pl.BlockSpec(memory_space=pltpu.SMEM)


def anywhere():
    return pl.BlockSpec(memory_space=pl.ANY)


def partner(me, step):
    other, bit = me, 1
    while bit <= step:
        if step & bit:
            other = other + bit * (1 - 2 * lax.rem(lax.div(me, bit), 2))
        bit *= 2
    return other


def column(u, v):
    return (u * 10 + v) * PITCH


def product(even, odd, right):
    parts = []
    for xx in range(4):
        for dy in range(3):
            for dz in range(3):
                if dy == 1:
                    rows = [odd[dz, (2 * s + xx) * 64 : (2 * s + xx) * 64 + 64] for s in range(4)]
                else:
                    at = [(2 * s + xx) * 80 + dy * 8 for s in range(4)]
                    rows = [even[dz, a : a + 64] for a in at]
                parts.append(jnp.concatenate(rows, axis=0))
    left = jnp.concatenate(parts, axis=1)
    return jnp.dot(left, right[...], preferred_element_type=jnp.float32)


def kernel(
    n_gx,
    n_gy,
    pdest,
    sdest,
    near,
    parents_hbm,
    skip_hbm,
    up_hbm,
    conv_hbm,
    acc,
    even_s,
    odd_s,
    right_s,
    agreed,
    parents,
    skip,
    up,
    conv,
    stage_p,
    stage_shell,
    stage_inside,
    recv_p,
    recv_shell,
    recv_inside,
    marks,
    land,
    chosen,
    flag,
    flags,
    wide,
    strip,
    agree,
    agrees,
    face_pick,
    spots,
    spread,
    whole,
    ghost,
    own,
    pool_c,
    pool_s,
    halo_c,
    halo_s,
    body,
    body_s,
    even,
    odd,
    right,
    loads,
    sends,
    receives,
    halo_sends,
    halo_receives,
    own_copy,
    agree_sends,
    agree_receives,
):
    slots = parents.shape[0]
    count = near.shape[0]
    made = whole.shape[2]
    gx, me = lax.axis_index("gx"), lax.axis_index("gy")
    flat = gx * n_gy + me
    first = flat * count
    has_ahead, has_behind = flat < n_gx * n_gy - 1, flat > 0

    def coordinates(device):
        device = lax.max(device, 0)
        return (lax.div(device, n_gy), lax.rem(device, n_gy))

    ahead, behind = coordinates(flat + 1), coordinates(flat - 1)
    cross = list(range(n_gy // 2, n_gy))
    rest = list(range(2, n_gy // 2)) + [1]
    order = cross + rest

    load = [
        pltpu.make_async_copy(parents_hbm, parents, loads.at[0]),
        pltpu.make_async_copy(skip_hbm, skip, loads.at[1]),
        pltpu.make_async_copy(up_hbm, up, loads.at[2]),
        pltpu.make_async_copy(conv_hbm, conv, loads.at[3]),
    ]
    for copy in load:
        copy.start()

    barrier = pltpu.get_barrier_semaphore()
    wraps_ahead = has_ahead & (me == n_gy - 1)
    wraps_behind = has_behind & (me == 0)

    @pl.when(wraps_ahead)
    def _():
        pl.semaphore_signal(barrier, inc=1, device_id=ahead, device_id_type=MESH)

    @pl.when(wraps_behind)
    def _():
        pl.semaphore_signal(barrier, inc=1, device_id=behind, device_id_type=MESH)

    for step in order:
        pl.semaphore_signal(
            barrier, inc=1, device_id={"gy": partner(me, step)}, device_id_type=MESH
        )

    for step in range(1, n_gx):
        pl.semaphore_signal(
            barrier, inc=1, device_id={"gx": lax.rem(gx + step, n_gx)}, device_id_type=MESH
        )

    for which, dest in enumerate((pdest, sdest)):
        targets = [dest[s] for s in range(slots)]
        owners = [
            jnp.where(t >= 0, lax.rem(lax.div(lax.max(t, 0), count), n_gy), -1) for t in targets
        ]
        for d in range(n_gy):
            slot, mark = jnp.int32(0), jnp.int32(-1)
            for s in range(slots):
                here = owners[s] == d
                slot = jnp.where(here, s, slot)
                mark = jnp.where(here, targets[s], mark)
            marks[which * n_gy + d] = mark
            chosen[which * n_gy + d] = slot

    load[0].wait()
    for d in range(n_gy):
        stage_p[d] = parents[chosen[d]]
    load[1].wait()

    def split(d, carry):
        wide[...] = skip[chosen[n_gy + d]].astype(jnp.float32)
        columns = [wide[0:64], wide[448:512]]
        for x in range(1, 7):
            columns += [wide[x * 64 : x * 64 + 8], wide[x * 64 + 56 : x * 64 + 64]]
        stage_shell[d, 0:224] = jnp.concatenate(columns, axis=0).astype(stage_shell.dtype)
        for i in range(12):
            z, x = i // 6 * 7, i % 6 + 1
            strip[6 * i : 6 * i + 8] = wide[pl.ds(x * 64 + 8 + z, 8, stride=8), :]
        stage_shell[d, 224:304] = strip[0:80].astype(stage_shell.dtype)
        for i in range(36):
            at = (i // 6 + 1) * 64 + (i % 6 + 1) * 8 + 1
            strip[80 + 6 * i : 88 + 6 * i] = wide[at : at + 8]
        stage_inside[d] = strip[80:304].astype(stage_inside.dtype)
        return carry

    lax.fori_loop(0, n_gy, split, 0)

    pl.semaphore_wait(
        barrier, n_gx + n_gy - 2 + wraps_ahead.astype(jnp.int32) + wraps_behind.astype(jnp.int32)
    )

    def remote(source, landing, kind, step):
        return pltpu.make_async_remote_copy(
            src_ref=source,
            dst_ref=landing,
            send_sem=sends.at[kind, step],
            recv_sem=receives.at[kind, step],
            device_id={"gy": partner(me, step)},
            device_id_type=MESH,
        )

    mark_copies = [remote(marks, land.at[me], 0, s) for s in order]
    parent_copies = [remote(stage_p.at[partner(me, s)], recv_p.at[me], 1, s) for s in order]
    shell_copies, inside_copies = [
        [remote(stage.at[partner(me, s), pl.ds(0, size)], recv.at[me, pl.ds(0, size)], kind, s) for s in order]
        for kind, stage, recv, size in (
            (2, stage_shell, recv_shell, SHELL),
            (3, stage_inside, recv_inside, INSIDE),
        )
    ]
    flag_copies = [remote(flag, flags.at[me], 4, s) for s in order]
    mine = [
        pltpu.make_async_copy(stage.at[me], recv.at[me], own_copy.at[i])
        for i, (stage, recv) in enumerate(
            ((stage_p, recv_p), (stage_shell, recv_shell), (stage_inside, recv_inside))
        )
    ]
    early = max(1, len(cross) // 2)
    for copy in mark_copies + parent_copies + shell_copies[:early] + mine:
        copy.start()
    for i in range(2 * n_gy):
        land[me, i] = marks[i]

    last = 8 * count

    def tables(b, carry):
        ids = [near[b, k] for k in range(26)]
        offs = [i - first for i in ids]
        enough = carry
        for side in range(2):
            low, high = jnp.int32(6), jnp.int32(-1)
            for k in range(26):
                off = offs[k] if side else offs[k] + 2 * count
                there = (ids[k] >= 0) & (off >= count) & (off < 2 * count)
                low = jnp.where(there, lax.min(low, face_of[25 - k]), low)
                high = jnp.where(there, lax.max(high, face_of[25 - k]), high)
            face_pick[b * 2 + side] = lax.max(high, 0)
            enough = jnp.where((high >= 0) & (low != high), 0, enough)
        for k in range(26):
            off = offs[k]
            inside = (off >= 0) & (off < count)
            spot = jnp.where(inside, off * 6 + face_of[k], 6 * count + off)
            spot = jnp.where(off < 0, 7 * count + off, spot)
            spot = jnp.where(ids[k] >= 0, spot, last)
            spots[b * 26 + k] = lax.min(lax.max(spot, 0), last)
        return enough

    flag[0] = lax.fori_loop(0, count, tables, jnp.int32(1))
    for copy in flag_copies:
        copy.start()
    flags[me, 0] = flag[0]


    for copy in load[2:]:
        copy.wait()
    zero = jnp.zeros((made, made), conv.dtype)
    for half, into in enumerate((right, right_s)):
        rows = slice(half * made, (half + 1) * made)
        for xx in range(4):
            for yz in range(9):
                at = (xx * 9 + yz) * made
                into[at : at + made, 0:made] = conv[xx * 9 + yz, rows, :] if xx < 3 else zero
                into[at : at + made, made:] = conv[(xx - 1) * 9 + yz, rows, :] if xx > 0 else zero
    for pool in (pool_c, pool_s):
        pool[last] = jnp.zeros(pool.shape[1:], pool.dtype)
    spread[...] = jnp.zeros_like(spread)

    for copy in mark_copies + parent_copies:
        copy.wait_recv()
    mine[0].wait()
    sources = []
    for which in range(2):
        held = [land[d, which * n_gy + me] for d in range(n_gy)]
        of = []
        for b in range(count):
            source = jnp.int32(0)
            for d in range(n_gy):
                source = jnp.where(held[d] == first + b, d, source)
            of.append(source)
        sources.append(of)

    def faces(b, pool):
        for f in range(6):
            edge = 7 * (f % 2)
            if f < 2:
                value = whole[b, edge * 64 : edge * 64 + 64]
            elif f < 4:
                value = jnp.concatenate(
                    [whole[b, x * 64 + edge * 8 : x * 64 + edge * 8 + 8] for x in range(8)], axis=0
                )
            else:
                value = whole[b, pl.ds(edge, 64, stride=8), :]
            value = value.astype(pool.dtype)
            own[b * 6 + f] = value
            pool[b * 6 + f] = value

    def faces_of_body(b, pool):
        for f in range(6):
            edge = 7 * (f % 2)
            if f < 2:
                rows = [body_s[b, pl.ds(column(edge + 1, y + 1) + 8, 8), :] for y in range(8)]
            elif f < 4:
                rows = [body_s[b, pl.ds(column(x + 1, edge + 1) + 8, 8), :] for x in range(8)]
            else:
                rows = [
                    body_s[b, pl.ds(column(x + 1, 1) + 8 + edge, 8, stride=PITCH), :]
                    for x in range(8)
                ]
            value = jnp.concatenate(rows, axis=0).astype(pool.dtype)
            own[b * 6 + f] = value
            pool[b * 6 + f] = value

    def send_halo(pool, halo, kind):
        for b in range(count):
            for side in range(2):
                halo[side, b] = own[b * 6 + face_pick[b * 2 + side]]
        down = pltpu.make_async_remote_copy(
            src_ref=halo.at[0],
            dst_ref=pool.at[pl.ds(7 * count, count)],
            send_sem=halo_sends.at[kind, 0],
            recv_sem=halo_receives.at[kind, 0],
            device_id=behind,
            device_id_type=MESH,
        )
        up_copy = pltpu.make_async_remote_copy(
            src_ref=halo.at[1],
            dst_ref=pool.at[pl.ds(6 * count, count)],
            send_sem=halo_sends.at[kind, 1],
            recv_sem=halo_receives.at[kind, 1],
            device_id=ahead,
            device_id_type=MESH,
        )

        @pl.when(has_ahead)
        def _():
            up_copy.start()

        @pl.when(has_behind)
        def _():
            down.start()

        return down, up_copy

    def wait_halo(copies):
        down, up_copy = copies

        @pl.when(has_ahead)
        def _():
            down.wait_recv()

        @pl.when(has_behind)
        def _():
            up_copy.wait_recv()

    def finish_halo(copies):
        down, up_copy = copies

        @pl.when(has_ahead)
        def _():
            up_copy.wait_send()

        @pl.when(has_behind)
        def _():
            down.wait_send()

    def upsample(b, source):
        for half in range(2):
            values = recv_p[source, :, half * 128 : (half + 1) * 128].astype(jnp.float32)
            for c in range(2):
                spread[c * 2 + half, pl.ds(c, 64, stride=2), :] = values
        rows = jnp.concatenate([spread[p] for p in range(4)], axis=1).astype(jnp.bfloat16)
        for a in range(2):
            for e in range(2):
                tap = a * 4 + e * 2
                weight = jnp.concatenate([up[tap], up[tap + 1]], axis=0)
                value = jnp.dot(rows, weight, preferred_element_type=jnp.float32)
                for i in range(4):
                    for j in range(4):
                        at = (2 * i + a) * 64 + (2 * j + e) * 8
                        whole[b, at : at + 8] = value[(i * 4 + j) * 8 : (i * 4 + j) * 8 + 8]

    for b in range(count):
        upsample(b, sources[0][b])
        faces(b, pool_c)
    halo_copies = send_halo(pool_c, halo_c, 0)
    for copy in shell_copies[early:] + inside_copies:
        copy.start()

    def surround(b, pool, body):
        def taken(step):
            return pool.at[spots[b * 26 + direction_of[step]]]

        def part(step, low, high):
            return taken(step)[low:high].astype(jnp.float32)

        for ox in (-1, 1):
            u, ex = (0, 7) if ox < 0 else (9, 0)
            value = part((ox, 0, 0), 0, 64)
            for y in range(8):
                body[column(u, y + 1) + 8 : column(u, y + 1) + 16] = value[y * 8 : y * 8 + 8]
            for oy in (-1, 1):
                v, ey = (0, 7) if oy < 0 else (9, 0)
                low = ey * 8 // 16 * 16
                value = part((ox, oy, 0), low, low + 16)
                body[column(u, v) + 8 : column(u, v) + 16] = value[ey * 8 - low : ey * 8 - low + 8]
        for oy in (-1, 1):
            v = 0 if oy < 0 else 9
            value = part((0, oy, 0), 0, 64)
            for x in range(8):
                body[column(x + 1, v) + 8 : column(x + 1, v) + 16] = value[x * 8 : x * 8 + 8]
        for p, oz in enumerate((-1, 1)):
            z = 7 if oz < 0 else 16
            value = part((0, 0, oz), 0, 64)
            for x in range(8):
                body[pl.ds(column(x + 1, 1) + z, 8, stride=PITCH), :] = value[x * 8 : x * 8 + 8]
            for ox in (-1, 1):
                u, ex = (0, 7) if ox < 0 else (9, 0)
                low = ex * 8 // 16 * 16
                value = part((ox, 0, oz), low, low + 16)
                body[pl.ds(column(u, 1) + z, 8, stride=PITCH), :] = value[
                    ex * 8 - low : ex * 8 - low + 8
                ]
                for oy in (-1, 1):
                    v, ey = (0, 7) if oy < 0 else (9, 0)
                    value = part((ox, oy, oz), low, low + 16)
                    row = ex * 8 + ey - low
                    body[column(u, v) + z : column(u, v) + z + 1] = value[row : row + 1]
            for q, oy in enumerate((-1, 1)):
                v, ey = (0, 7) if oy < 0 else (9, 0)
                ghost[p * 2 + q] = part((0, oy, oz), 0, 64)
                body[pl.ds(column(1, v) + z, 8, stride=10 * PITCH), :] = ghost[
                    p * 2 + q, pl.ds(ey, 8, stride=8), :
                ]
    def shifts(body, even, odd):
        for dz in range(3):
            for u in range(10):
                blocks = [
                    body[column(u, v) + 7 + dz : column(u, v) + 15 + dz] for v in range(10)
                ]
                even[dz, u * 80 : u * 80 + 80] = jnp.concatenate(blocks, axis=0).astype(even.dtype)
                odd[dz, u * 64 : u * 64 + 64] = jnp.concatenate(blocks[1:9], axis=0).astype(
                    odd.dtype
                )

    wait_halo(halo_copies)

    def child_half(b, carry):
        for x in range(8):
            for y in range(8):
                at = column(x + 1, y + 1) + 8
                body[at : at + 8] = whole[b, x * 64 + y * 8 : x * 64 + y * 8 + 8]
        surround(b, pool_c, body)
        shifts(body, even, odd)
        acc[b] = product(even, odd, right)
        return carry

    lax.fori_loop(0, count, child_half, 0)

    for copy in shell_copies:
        copy.wait_recv()
    mine[1].wait()
    for b in range(count):
        outer = recv_shell[sources[1][b]].astype(jnp.float32)
        padded = body_s.at[b]
        for y in range(8):
            padded[column(1, y + 1) + 8 : column(1, y + 1) + 16] = outer[y * 8 : y * 8 + 8]
            padded[column(8, y + 1) + 8 : column(8, y + 1) + 16] = outer[64 + y * 8 : 72 + y * 8]
        for x in range(1, 7):
            at = 112 + x * 16
            padded[column(x + 1, 1) + 8 : column(x + 1, 1) + 16] = outer[at : at + 8]
            padded[column(x + 1, 8) + 8 : column(x + 1, 8) + 16] = outer[at + 8 : at + 16]
        strip[0:80] = outer[224:304]
        for i in range(12):
            at = column(i % 6 + 2, 2) + 8 + i // 6 * 7
            padded[pl.ds(at, 6, stride=PITCH), :] = strip[6 * i : 6 * i + 6]
        faces_of_body(b, pool_s)
    skip_halo = send_halo(pool_s, halo_s, 1)
    for copy in flag_copies:
        copy.wait_recv()
    enough = flags[0, 0]
    for d in range(1, n_gy):
        enough = lax.min(enough, flags[d, 0])
    agree[0] = enough
    agrees[gx, 0] = enough
    agree_copies = [
        pltpu.make_async_remote_copy(
            src_ref=agree,
            dst_ref=agrees.at[gx],
            send_sem=agree_sends.at[step],
            recv_sem=agree_receives.at[step],
            device_id={"gx": lax.rem(gx + step, n_gx)},
            device_id_type=MESH,
        )
        for step in range(1, n_gx)
    ]
    for copy in agree_copies:
        copy.start()
    wait_halo(skip_halo)
    for b in range(count):
        surround(b, pool_s, body_s.at[b])

    for copy in inside_copies:
        copy.wait_recv()
    mine[2].wait()
    for b in range(count):
        padded = body_s.at[b]
        strip[80:304] = recv_inside[sources[1][b]].astype(jnp.float32)
        for i in range(36):
            at = column(i // 6 + 2, i % 6 + 2) + 9
            padded[at : at + 6] = strip[80 + 6 * i : 86 + 6 * i]
        shifts(padded, even_s.at[b], odd_s.at[b])

    for copy in mark_copies + parent_copies + shell_copies + inside_copies + flag_copies:
        copy.wait_send()
    finish_halo(halo_copies)
    finish_halo(skip_halo)
    for copy in agree_copies:
        copy.wait()
    for x in range(n_gx):
        enough = lax.min(enough, agrees[x, 0])
    agreed[0] = enough

def finish_kernel(acc, even, odd, right, out, result, sems):
    copies = []
    for b in range(acc.shape[0]):
        made = acc.shape[2] // 2
        total = acc[b] + product(even.at[b], odd.at[b], right)
        total = jnp.maximum(total, 0.0).astype(result.dtype)
        for s in range(4):
            for p in range(2):
                at = (2 * s + p) * 64
                result[b, at : at + 64] = total[s * 64 : s * 64 + 64, p * made : (p + 1) * made]
        copies.append(pltpu.make_async_copy(result.at[b], out.at[b], sems.at[b]))
        copies[-1].start()
    for copy in copies:
        copy.wait()


def finish(acc, even, odd, right):
    count, made = acc.shape[0], acc.shape[2] // 2
    shape = (count, 2 * acc.shape[1], made)
    return pl.pallas_call(
        finish_kernel,
        out_shape=pltpu.HBM(shape, jnp.bfloat16),
        in_specs=[vmem()] * 4,
        out_specs=pl.BlockSpec(memory_space=pltpu.HBM),
        scratch_shapes=[
            pltpu.VMEM(shape, jnp.bfloat16),
            pltpu.SemaphoreType.DMA((count,)),
        ],
        compiler_params=pltpu.CompilerParams(vmem_limit_bytes=24 * 2**20),
        name="finish",
    )(acc, even, odd, right)


META = 8


def vmem():
    return pl.BlockSpec(memory_space=pltpu.VMEM)


def pack_kernel(
    gy_count, bricks_dev, pdest, sdest, parents, skip, out_p, out_s, land, sem_p, sem_s
):
    slots, voxels = parents.shape[0], parents.shape[1]
    for d in range(gy_count):
        land[0, d] = -1
        land[1, d] = -1

    def copies(s):
        tp, ts = pdest[s], sdest[s]
        op = lax.rem(lax.div(jnp.maximum(tp, 0), bricks_dev), gy_count)
        os = lax.rem(lax.div(jnp.maximum(ts, 0), bricks_dev), gy_count)
        cp = pltpu.make_async_copy(parents.at[s], out_p.at[op, pl.ds(0, voxels)], sem_p.at[s])
        cs = pltpu.make_async_copy(skip.at[s], out_s.at[os], sem_s.at[s])
        return (tp, op, cp), (ts, os, cs)

    for s in range(slots):
        for which, (t, o, c) in enumerate(copies(s)):

            @pl.when(t >= 0)
            def _():
                land[which, o] = lax.rem(t, bricks_dev)
                c.start()

    for d in range(gy_count):
        half = parents.shape[2] // 2
        for which in range(2):
            mark = jnp.full((META, half), land[which, d], jnp.int32).astype(jnp.float32)
            out_p[d, voxels : voxels + META, which * half : (which + 1) * half] = mark.astype(
                jnp.bfloat16
            )
    for s in range(slots):
        for t, o, c in copies(s):

            @pl.when(t >= 0)
            def _():
                c.wait()


def pack(parent_dest, skip_dest, parents, skip, bricks_dev, gy_count):
    slots, voxels, channels = parents.shape
    return pl.pallas_call(
        functools.partial(pack_kernel, gy_count, bricks_dev),
        out_shape=(
            jax.ShapeDtypeStruct((gy_count, voxels + META, channels), parents.dtype),
            jax.ShapeDtypeStruct((gy_count,) + skip.shape[1:], skip.dtype),
        ),
        in_specs=[smem(), smem(), anywhere(), anywhere()],
        out_specs=(vmem(), vmem()),
        scratch_shapes=[
            pltpu.SMEM((2, gy_count), jnp.int32),
            pltpu.SemaphoreType.DMA((slots,)),
            pltpu.SemaphoreType.DMA((slots,)),
        ],
        compiler_params=pltpu.CompilerParams(vmem_limit_bytes=VMEM_LIMIT),
        name="pack",
    )(parent_dest, skip_dest, parents, skip)


def exchange_kernel(gy_count, in_p, in_s, out_p, out_s, sends, receives, own):
    me = lax.axis_index("gy")
    mine = [
        pltpu.make_async_copy(in_p.at[me], out_p.at[me], own.at[0]),
        pltpu.make_async_copy(in_s.at[me], out_s.at[me], own.at[1]),
    ]
    for copy in mine:
        copy.start()
    barrier = pltpu.get_barrier_semaphore()
    shifts = sorted(range(1, gy_count), key=lambda s: abs(s - gy_count // 2))
    for shift in shifts:
        pl.semaphore_signal(
            barrier,
            inc=1,
            device_id={"gy": lax.rem(me + shift, gy_count)},
            device_id_type=pl.DeviceIdType.MESH,
        )
    pl.semaphore_wait(barrier, gy_count - 1)
    copies = []
    for which, (source, landing) in enumerate(((in_p, out_p), (in_s, out_s))):
        for shift in shifts:
            there = lax.rem(me + shift, gy_count)
            copy = pltpu.make_async_remote_copy(
                src_ref=source.at[there],
                dst_ref=landing.at[me],
                send_sem=sends.at[which, shift],
                recv_sem=receives.at[which, shift],
                device_id={"gy": there},
                device_id_type=pl.DeviceIdType.MESH,
            )
            copy.start()
            copies.append(copy)
    for copy in copies:
        copy.wait()
    for copy in mine:
        copy.wait()


def exchange(in_p, in_s):
    gy_count = in_p.shape[0]
    return pl.pallas_call(
        functools.partial(exchange_kernel, gy_count),
        out_shape=tuple(jax.ShapeDtypeStruct(a.shape, a.dtype) for a in (in_p, in_s)),
        in_specs=[anywhere(), anywhere()],
        out_specs=(anywhere(), anywhere()),
        scratch_shapes=[
            pltpu.SemaphoreType.DMA((2, gy_count)),
            pltpu.SemaphoreType.DMA((2, gy_count)),
            pltpu.SemaphoreType.DMA((2,)),
        ],
        compiler_params=pltpu.CompilerParams(
            collective_id=2, has_side_effects=True, vmem_limit_bytes=2**20
        ),
        name="exchange",
    )(in_p, in_s)


def halo_kernel(size, inner, to_before, to_after, from_before, from_after, sends, receives):
    me = lax.axis_index("gx") * inner + lax.axis_index("gy")

    def coordinates(device):
        device = lax.max(device, 0)
        return (lax.div(device, inner), lax.rem(device, inner))

    ahead, behind = coordinates(me + 1), coordinates(me - 1)
    has_ahead, has_behind = me < size - 1, me > 0
    barrier = pltpu.get_barrier_semaphore()
    mesh_id = pl.DeviceIdType.MESH

    @pl.when(has_ahead)
    def _():
        pl.semaphore_signal(barrier, inc=1, device_id=ahead, device_id_type=mesh_id)

    @pl.when(has_behind)
    def _():
        pl.semaphore_signal(barrier, inc=1, device_id=behind, device_id_type=mesh_id)

    pl.semaphore_wait(barrier, has_ahead.astype(jnp.int32) + has_behind.astype(jnp.int32))
    up = pltpu.make_async_remote_copy(
        src_ref=to_after,
        dst_ref=from_before,
        send_sem=sends.at[0],
        recv_sem=receives.at[0],
        device_id=ahead,
        device_id_type=mesh_id,
    )
    down = pltpu.make_async_remote_copy(
        src_ref=to_before,
        dst_ref=from_after,
        send_sem=sends.at[1],
        recv_sem=receives.at[1],
        device_id=behind,
        device_id_type=mesh_id,
    )

    @pl.when(has_ahead)
    def _():
        up.start()

    @pl.when(has_behind)
    def _():
        down.start()

    @pl.when(has_ahead)
    def _():
        up.wait_send()
        down.wait_recv()

    @pl.when(has_behind)
    def _():
        down.wait_send()
        up.wait_recv()


def halo(to_before, to_after):
    inner = lax.axis_size("gy")
    size = lax.axis_size("gx") * inner
    return pl.pallas_call(
        functools.partial(halo_kernel, size, inner),
        out_shape=(
            jax.ShapeDtypeStruct(to_after.shape, to_after.dtype),
            jax.ShapeDtypeStruct(to_before.shape, to_before.dtype),
        ),
        in_specs=[anywhere(), anywhere()],
        out_specs=(anywhere(), anywhere()),
        scratch_shapes=[pltpu.SemaphoreType.DMA((2,)), pltpu.SemaphoreType.DMA((2,))],
        compiler_params=pltpu.CompilerParams(
            collective_id=1, has_side_effects=True, vmem_limit_bytes=2**20
        ),
        name="halo",
    )(to_before, to_after)


def build_kernel(
    source, near, pay, skip, up, feats, faces, before, after, spread, whole, sent
):
    channels = up.shape[1]
    made = up.shape[2]

    @pl.when(pl.program_id(0) == 0)
    def _():
        spread[...] = jnp.zeros_like(spread)

    for half in range(channels // 128):
        values = pay[0, 0:64, half * 128 : (half + 1) * 128].astype(jnp.float32)
        for c in range(2):
            spread[c * (channels // 128) + half, pl.ds(c, 64, stride=2), :] = values
    rows = jnp.concatenate([spread[p] for p in range(spread.shape[0])], axis=1).astype(jnp.bfloat16)
    for a in range(2):
        for b in range(2):
            tap = a * 4 + b * 2
            weight = jnp.concatenate([up[tap], up[tap + 1]], axis=0)
            value = jnp.dot(rows, weight, preferred_element_type=jnp.float32)
            for i in range(4):
                for j in range(4):
                    at = (2 * i + a) * 64 + (2 * j + b) * 8
                    for p in range(made // 128):
                        whole[p, at : at + 8] = value[
                            (i * 4 + j) * 8 : (i * 4 + j) * 8 + 8, p * 128 : (p + 1) * 128
                        ]
    for p in range(made // 128, whole.shape[0]):
        at = p * 128 - made
        whole[p] = skip[0, :, at : at + 128].astype(jnp.float32)
    for p in range(whole.shape[0]):
        lanes = slice(p * 128, (p + 1) * 128)
        feats[0, :, lanes] = whole[p].astype(jnp.bfloat16)
        for side in range(2):
            edge = 7 * side
            faces[0, side, :, lanes] = whole[p, edge * 64 : edge * 64 + 64].astype(jnp.bfloat16)
            faces[0, 2 + side, :, lanes] = jnp.concatenate(
                [whole[p, x * 64 + edge * 8 : x * 64 + edge * 8 + 8] for x in range(8)], axis=0
            ).astype(jnp.bfloat16)
            faces[0, 4 + side, :, lanes] = whole[p, pl.ds(edge, 64, stride=8), :].astype(
                jnp.bfloat16
            )
    brick = pl.program_id(0)
    count = before.shape[1]
    first = (lax.axis_index("gx") * lax.axis_size("gy") + lax.axis_index("gy")) * count
    for m in range(2 * count):
        sent[m] = 0
    for k, face in enumerate(face_of[::-1]):
        n = near[brick, k]
        off = n - first
        spot = jnp.where(off < 0, off + count, jnp.where(off >= count, off, 2 * count))
        sent[jnp.where(n >= 0, spot, 2 * count)] = face
    for m in range(count):
        before[0, m] = faces[0, sent[m]]
        after[0, m] = faces[0, sent[count + m]]


def build(source, near, pay, skip, up_weight, bricks_dev):
    channels, made = up_weight.shape[1:]
    joined = made + skip.shape[2]
    return pl.pallas_call(
        build_kernel,
        out_shape=(
            jax.ShapeDtypeStruct((bricks_dev, 512, joined), jnp.bfloat16),
            jax.ShapeDtypeStruct((bricks_dev, 6, 64, joined), jnp.bfloat16),
            jax.ShapeDtypeStruct((bricks_dev, bricks_dev, 64, joined), jnp.bfloat16),
            jax.ShapeDtypeStruct((bricks_dev, bricks_dev, 64, joined), jnp.bfloat16),
        ),
        grid_spec=pltpu.PrefetchScalarGridSpec(
            num_scalar_prefetch=2,
            grid=(bricks_dev,),
            in_specs=[
                pl.BlockSpec((1,) + pay.shape[1:], lambda b, s, t: (s[0, b], 0, 0)),
                pl.BlockSpec((1,) + skip.shape[1:], lambda b, s, t: (s[1, b], 0, 0)),
                pl.BlockSpec(up_weight.shape, lambda b, s, t: (0, 0, 0)),
            ],
            out_specs=(
                pl.BlockSpec((1, 512, joined), lambda b, s, t: (b, 0, 0)),
                pl.BlockSpec((1, 6, 64, joined), lambda b, s, t: (b, 0, 0, 0)),
                pl.BlockSpec((1, bricks_dev, 64, joined), lambda b, s, t: (b, 0, 0, 0)),
                pl.BlockSpec((1, bricks_dev, 64, joined), lambda b, s, t: (b, 0, 0, 0)),
            ),
            scratch_shapes=[
                pltpu.VMEM((2 * channels // 128, 128, 128), jnp.float32),
                pltpu.VMEM((joined // 128, 512, 128), jnp.float32),
                pltpu.SMEM((2 * bricks_dev + 1,), jnp.int32),
            ],
        ),
        compiler_params=pltpu.CompilerParams(vmem_limit_bytes=VMEM_LIMIT),
        name="build",
    )(source, near, pay, skip, up_weight)


def refine_kernel(
    near,
    feats,
    own,
    before,
    after,
    weight,
    out,
    pool,
    sems,
    body,
    plane,
    left,
    right,
    early,
    late,
):
    brick = pl.program_id(0)
    joined, made = weight.shape[1:]

    @pl.when(brick == 0)
    def _():
        copies, first = [], 0
        for i, part in enumerate((own, before, after)):
            length = part.shape[0]
            copies.append(pltpu.make_async_copy(part, pool.at[pl.ds(first, length)], sems.at[i]))
            copies[-1].start()
            first += length
        for tap in range(9):
            for dz in range(3):
                right[tap * joined : (tap + 1) * joined, dz * made : (dz + 1) * made] = weight[
                    tap * 3 + dz
                ]
        for copy in copies:
            copy.wait()

    count = pl.num_programs(0)
    first = (lax.axis_index("gx") * lax.axis_size("gy") + lax.axis_index("gy")) * count
    ahead = own.shape[0] + count * count + brick
    behind = before.shape[0] - 2 * count * count

    def taken(step, start, length):
        k = direction_of[step]
        n = near[brick, k]
        off = n - first
        spot = jnp.where(off < 0, ahead + off * count, ahead + behind + off * count)
        spot = jnp.where((off >= 0) & (off < count), off * 6 + face_of[k], spot)
        spot = jnp.where(n >= 0, spot, 0)
        low = start // 16 * 16
        high = -(-(start + length) // 16) * 16
        value = pool[spot, low:high, :].astype(jnp.float32)
        return jnp.where(n >= 0, value[start - low : start - low + length], 0.0)

    body[1:9, 1:9] = feats[0].astype(jnp.float32).reshape(8, 8, 8, joined)
    for ox in (-1, 1):
        u = 0 if ox < 0 else 9
        body[u, 1:9] = taken((ox, 0, 0), 0, 64).reshape(8, 8, joined)
        for oy in (-1, 1):
            v, ey = (0, 7) if oy < 0 else (9, 0)
            body[u, v] = taken((ox, oy, 0), ey * 8, 8)
    for oy in (-1, 1):
        v = 0 if oy < 0 else 9
        body[1:9, v] = taken((0, oy, 0), 0, 64).reshape(8, 8, joined)
    for p, oz in enumerate((-1, 1)):
        plane[p, 1:9, 1:9] = taken((0, 0, oz), 0, 64).reshape(8, 8, joined)
        for ox in (-1, 1):
            u, ex = (0, 7) if ox < 0 else (9, 0)
            plane[p, u, 1:9] = taken((ox, 0, oz), ex * 8, 8)
            for oy in (-1, 1):
                v, ey = (0, 7) if oy < 0 else (9, 0)
                row = taken((ox, oy, oz), ex * 8, 8)
                plane[p, u, v : v + 1] = row[ey : ey + 1]
        for oy in (-1, 1):
            v, ey = (0, 7) if oy < 0 else (9, 0)
            value = taken((0, oy, oz), 0, 64).reshape(8, 8, joined)
            plane[p, 1:9, v : v + 1] = value[:, ey : ey + 1]

    for tap in range(9):
        dx, dy = tap // 3, tap % 3
        lanes = slice(tap * joined, (tap + 1) * joined)
        left[0:512, lanes] = (
            body[dx : dx + 8, dy : dy + 8].reshape(512, joined).astype(jnp.bfloat16)
        )
        for p in range(2):
            left[512 + 64 * p : 576 + 64 * p, lanes] = (
                plane[p, dx : dx + 8, dy : dy + 8].reshape(64, joined).astype(jnp.bfloat16)
            )
    total = jnp.dot(left[...], right[...], preferred_element_type=jnp.float32)
    early[1:513] = total[0:512, 0:made]
    early[pl.ds(0, 64, stride=8), :] = total[512:576, 0:made]
    late[7:519] = total[0:512, 2 * made : 3 * made]
    late[pl.ds(15, 64, stride=8), :] = total[576:640, 2 * made : 3 * made]
    result = early[0:512] + total[0:512, made : 2 * made] + late[8:520]
    out[0] = jnp.maximum(result, 0.0).astype(jnp.bfloat16)


def refine(near, feats, own, before, after, conv_weight):
    bricks_dev, voxels, joined = feats.shape
    made = conv_weight.shape[2]
    return pl.pallas_call(
        refine_kernel,
        out_shape=jax.ShapeDtypeStruct((bricks_dev, voxels, made), jnp.bfloat16),
        grid_spec=pltpu.PrefetchScalarGridSpec(
            num_scalar_prefetch=1,
            grid=(bricks_dev,),
            in_specs=[
                pl.BlockSpec((1, voxels, joined), lambda b, s: (b, 0, 0)),
                anywhere(),
                anywhere(),
                anywhere(),
                pl.BlockSpec(conv_weight.shape, lambda b, s: (0, 0, 0)),
            ],
            out_specs=pl.BlockSpec((1, voxels, made), lambda b, s: (b, 0, 0)),
            scratch_shapes=[
                pltpu.VMEM((sum(a.shape[0] for a in (own, before, after)), 64, joined), own.dtype),
                pltpu.SemaphoreType.DMA((3,)),
                pltpu.VMEM((10, 10, 8, joined), jnp.float32),
                pltpu.VMEM((2, 10, 16, joined), jnp.float32),
                pltpu.VMEM((640, 9 * joined), jnp.bfloat16),
                pltpu.VMEM((9 * joined, 3 * made), jnp.bfloat16),
                pltpu.VMEM((520, made), jnp.float32),
                pltpu.VMEM((520, made), jnp.float32),
            ],
        ),
        compiler_params=pltpu.CompilerParams(vmem_limit_bytes=VMEM_LIMIT),
        name="refine",
    )(near, feats, own, before, after, conv_weight)


def general(parents, parent_dest, skip, skip_dest, neighbours, up_weight, conv_weight):
    bricks_dev = neighbours.shape[0]
    gy_count = lax.axis_size("gy")
    sent_p, sent_s = pack(parent_dest, skip_dest, parents, skip, bricks_dev, gy_count)
    came_p, came_s = exchange(sent_p, sent_s)
    voxels, channels = parents.shape[1:]
    spots = jnp.stack([came_p[:, voxels, 0], came_p[:, voxels, channels // 2]]).astype(jnp.int32)
    matches = spots[:, None, :] == jnp.arange(bricks_dev)[None, :, None]
    source = jnp.sum(jnp.where(matches, jnp.arange(gy_count)[None, None, :], 0), axis=2)
    feats, faces, to_before, to_after = build(
        source.astype(jnp.int32), neighbours, came_p, came_s, up_weight, bricks_dev
    )
    flat = (-1,) + faces.shape[2:]
    before, after = halo(to_before.reshape(flat), to_after.reshape(flat))
    return refine(neighbours, feats, faces.reshape(flat), before, after, conv_weight)


def per_device(parents, parent_dest, skip, skip_dest, neighbours, up_weight, conv_weight):
    count = neighbours.shape[0]
    n_gx, n_gy = lax.axis_size("gx"), lax.axis_size("gy")
    voxels = skip.shape[1]
    made = conv_weight.shape[2]
    bf16, f32 = jnp.bfloat16, jnp.float32
    pool = (8 * count + 1, 64, made)
    dma = pltpu.SemaphoreType.DMA
    width = 2 * made
    acc, even, odd, right, agreed = pl.pallas_call(
        functools.partial(kernel, n_gx, n_gy),
        out_shape=(
            pltpu.VMEM((count, voxels // 2, width), f32),
            pltpu.VMEM((count, 3, 800, made), bf16),
            pltpu.VMEM((count, 3, 640, made), bf16),
            pltpu.VMEM((36 * made, width), bf16),
            jax.ShapeDtypeStruct((1,), jnp.int32),
        ),
        in_specs=[smem(), smem(), smem()] + [anywhere()] * 4,
        out_specs=(vmem(), vmem(), vmem(), vmem(), smem()),
        scratch_shapes=[
            pltpu.VMEM(parents.shape, bf16),
            pltpu.VMEM(skip.shape, bf16),
            pltpu.VMEM(up_weight.shape, bf16),
            pltpu.VMEM(conv_weight.shape, bf16),
            pltpu.VMEM((n_gy,) + parents.shape[1:], bf16),
            pltpu.VMEM((n_gy, 304, skip.shape[2]), bf16),
            pltpu.VMEM((n_gy, 224, skip.shape[2]), bf16),
            pltpu.VMEM((n_gy,) + parents.shape[1:], bf16),
            pltpu.VMEM((n_gy, 304, skip.shape[2]), bf16),
            pltpu.VMEM((n_gy, 224, skip.shape[2]), bf16),
            pltpu.SMEM((2 * n_gy,), jnp.int32),
            pltpu.SMEM((n_gy, 2 * n_gy), jnp.int32),
            pltpu.SMEM((2 * n_gy,), jnp.int32),
            pltpu.SMEM((1,), jnp.int32),
            pltpu.SMEM((n_gy, 1), jnp.int32),
            pltpu.VMEM((voxels, skip.shape[2]), f32),
            pltpu.VMEM((304, skip.shape[2]), f32),
            pltpu.SMEM((1,), jnp.int32),
            pltpu.SMEM((n_gx, 1), jnp.int32),
            pltpu.SMEM((2 * count,), jnp.int32),
            pltpu.SMEM((26 * count,), jnp.int32),
            pltpu.VMEM((4, 128, 128), f32),
            pltpu.VMEM((count, voxels, made), f32),
            pltpu.VMEM((4, 64, made), f32),
            pltpu.VMEM((6 * count, 64, made), bf16),
            pltpu.VMEM(pool, bf16),
            pltpu.VMEM(pool, bf16),
            pltpu.VMEM((2, count, 64, made), bf16),
            pltpu.VMEM((2, count, 64, made), bf16),
            pltpu.VMEM((100 * PITCH, made), f32),
            pltpu.VMEM((count, 100 * PITCH, made), f32),
            pltpu.VMEM((3, 800, made), bf16),
            pltpu.VMEM((3, 640, made), bf16),
            pltpu.VMEM((36 * made, width), bf16),
            dma((4,)),
            dma((5, n_gy)),
            dma((5, n_gy)),
            dma((2, 2)),
            dma((2, 2)),
            dma((3,)),
            dma((n_gx,)),
            dma((n_gx,)),
        ],
        compiler_params=pltpu.CompilerParams(
            collective_id=0, has_side_effects=True, vmem_limit_bytes=40 * 2**20
        ),
        name="refine_level",
    )(parent_dest, skip_dest, neighbours, parents, skip, up_weight, conv_weight)
    return lax.switch(
        agreed[0],
        [
            lambda: general(
                parents, parent_dest, skip, skip_dest, neighbours, up_weight, conv_weight
            ),
            lambda: finish(acc, even, odd, right),
        ],
    )


def solution(mesh):
    placed = (
        P(("gx", "gy"), None, None),
        P(("gx", "gy")),
        P(("gx", "gy"), None, None),
        P(("gx", "gy")),
        P(("gx", "gy"), None),
        P(),
        P(),
    )
    return jax.shard_map(
        per_device,
        mesh=mesh,
        in_specs=placed,
        out_specs=P(("gx", "gy"), None, None),
        check_vma=False,
    )
```

```python
import functools

import jax
import jax.numpy as jnp
from jax import lax
from jax.experimental import pallas as pl
from jax.experimental.pallas import tpu as pltpu
from jax.sharding import PartitionSpec as P

steps = [(code // 9 - 1, code // 3 % 3 - 1, code % 3 - 1) for code in range(27) if code != 13]
direction_of = {step: k for k, step in enumerate(steps)}
face_of = [
    (1 if x < 0 else 0) if x and not z else (5 if z < 0 else 4) if z else (3 if y < 0 else 2)
    for x, y, z in steps
]
PITCH = 24
VMEM_LIMIT = 24 * 2**20
SHELL, INSIDE = 296, 216
MESH = pl.DeviceIdType.MESH


def smem():
    return pl.BlockSpec(memory_space=pltpu.SMEM)


def anywhere():
    return pl.BlockSpec(memory_space=pl.ANY)


def partner(me, step):
    other, bit = me, 1
    while bit <= step:
        if step & bit:
            other = other + bit * (1 - 2 * lax.rem(lax.div(me, bit), 2))
        bit *= 2
    return other


def column(u, v):
    return (u * 10 + v) * PITCH


def product(even, odd, right):
    parts = []
    for xx in range(4):
        for dy in range(3):
            for dz in range(3):
                if dy == 1:
                    rows = [odd[dz, (2 * s + xx) * 64 : (2 * s + xx) * 64 + 64] for s in range(4)]
                else:
                    at = [(2 * s + xx) * 80 + dy * 8 for s in range(4)]
                    rows = [even[dz, a : a + 64] for a in at]
                parts.append(jnp.concatenate(rows, axis=0))
    left = jnp.concatenate(parts, axis=1)
    return jnp.dot(left, right[...], preferred_element_type=jnp.float32)


def kernel(
    n_gx,
    n_gy,
    pdest_hbm,
    sdest_hbm,
    near_hbm,
    parents_hbm,
    skip_hbm,
    up_hbm,
    conv_hbm,
    acc,
    even_s,
    odd_s,
    right_s,
    agreed,
    pdest,
    sdest,
    near,
    parents,
    skip,
    up,
    conv,
    stage_p,
    stage_shell,
    stage_inside,
    recv_p,
    recv_shell,
    recv_inside,
    marks,
    land,
    chosen,
    origin,
    flag,
    flags,
    wide,
    strip,
    agree,
    agrees,
    face_pick,
    spots,
    spread,
    whole,
    ghost,
    own,
    pool_c,
    pool_s,
    halo_c,
    halo_s,
    body,
    body_s,
    even,
    odd,
    right,
    loads,
    sends,
    receives,
    halo_sends,
    halo_receives,
    own_copy,
    agree_sends,
    agree_receives,
):
    slots = parents.shape[0]
    count = near.shape[0]
    made = whole.shape[2]
    gx, me = lax.axis_index("gx"), lax.axis_index("gy")
    flat = gx * n_gy + me
    first = flat * count
    has_ahead, has_behind = flat < n_gx * n_gy - 1, flat > 0

    def coordinates(device):
        device = lax.max(device, 0)
        return (lax.div(device, n_gy), lax.rem(device, n_gy))

    ahead, behind = coordinates(flat + 1), coordinates(flat - 1)
    cross = list(range(n_gy // 2, n_gy))
    rest = list(range(2, n_gy // 2)) + [1]
    order = cross + rest

    barrier = pltpu.get_barrier_semaphore()
    wraps_ahead = has_ahead & (me == n_gy - 1)
    wraps_behind = has_behind & (me == 0)

    @pl.when(wraps_ahead)
    def _():
        pl.semaphore_signal(barrier, inc=1, device_id=ahead, device_id_type=MESH)

    @pl.when(wraps_behind)
    def _():
        pl.semaphore_signal(barrier, inc=1, device_id=behind, device_id_type=MESH)

    for step in order:
        pl.semaphore_signal(
            barrier, inc=1, device_id={"gy": partner(me, step)}, device_id_type=MESH
        )

    for step in range(1, n_gx):
        pl.semaphore_signal(
            barrier, inc=1, device_id={"gx": lax.rem(gx + step, n_gx)}, device_id_type=MESH
        )

    load = [
        pltpu.make_async_copy(parents_hbm, parents, loads.at[0]),
        pltpu.make_async_copy(skip_hbm, skip, loads.at[1]),
        pltpu.make_async_copy(up_hbm, up, loads.at[2]),
        pltpu.make_async_copy(conv_hbm, conv, loads.at[3]),
    ]
    tables_in = [
        pltpu.make_async_copy(pdest_hbm, pdest, loads.at[4]),
        pltpu.make_async_copy(sdest_hbm, sdest, loads.at[5]),
        pltpu.make_async_copy(near_hbm, near, loads.at[6]),
    ]
    for copy in tables_in + load:
        copy.start()
    for copy in tables_in:
        copy.wait()

    for which, dest in enumerate((pdest, sdest)):
        targets = [dest[s] for s in range(slots)]
        owners = [
            jnp.where(t >= 0, lax.rem(lax.div(lax.max(t, 0), count), n_gy), -1) for t in targets
        ]
        for d in range(n_gy):
            slot, mark = jnp.int32(0), jnp.int32(-1)
            for s in range(slots):
                here = owners[s] == d
                slot = jnp.where(here, s, slot)
                mark = jnp.where(here, targets[s], mark)
            marks[which * n_gy + d] = mark
            chosen[which * n_gy + d] = slot

    load[0].wait()
    for d in range(n_gy):
        stage_p[d] = parents[chosen[d]]
    load[1].wait()

    def split(d, carry):
        wide[...] = skip[chosen[n_gy + d]].astype(jnp.float32)
        columns = [wide[0:64], wide[448:512]]
        for x in range(1, 7):
            columns += [wide[x * 64 : x * 64 + 8], wide[x * 64 + 56 : x * 64 + 64]]
        stage_shell[d, 0:224] = jnp.concatenate(columns, axis=0).astype(stage_shell.dtype)
        for i in range(12):
            z, x = i // 6 * 7, i % 6 + 1
            strip[6 * i : 6 * i + 8] = wide[pl.ds(x * 64 + 8 + z, 8, stride=8), :]
        stage_shell[d, 224:304] = strip[0:80].astype(stage_shell.dtype)
        for i in range(36):
            at = (i // 6 + 1) * 64 + (i % 6 + 1) * 8 + 1
            strip[80 + 6 * i : 88 + 6 * i] = wide[at : at + 8]
        stage_inside[d] = strip[80:304].astype(stage_inside.dtype)
        return carry

    lax.fori_loop(0, n_gy, split, 0)

    pl.semaphore_wait(
        barrier, n_gx + n_gy - 2 + wraps_ahead.astype(jnp.int32) + wraps_behind.astype(jnp.int32)
    )

    def remote(source, landing, kind, step):
        return pltpu.make_async_remote_copy(
            src_ref=source,
            dst_ref=landing,
            send_sem=sends.at[kind, step],
            recv_sem=receives.at[kind, step],
            device_id={"gy": partner(me, step)},
            device_id_type=MESH,
        )

    mark_copies = [remote(marks, land.at[me], 0, s) for s in order]
    parent_copies = [remote(stage_p.at[partner(me, s)], recv_p.at[me], 1, s) for s in order]
    shell_copies, inside_copies = [
        [remote(stage.at[partner(me, s), pl.ds(0, size)], recv.at[me, pl.ds(0, size)], kind, s) for s in order]
        for kind, stage, recv, size in (
            (2, stage_shell, recv_shell, SHELL),
            (3, stage_inside, recv_inside, INSIDE),
        )
    ]
    flag_copies = [remote(flag, flags.at[me], 4, s) for s in order]
    mine = [
        pltpu.make_async_copy(stage.at[me], recv.at[me], own_copy.at[i])
        for i, (stage, recv) in enumerate(
            ((stage_p, recv_p), (stage_shell, recv_shell), (stage_inside, recv_inside))
        )
    ]
    early = max(1, len(cross) // 2)
    for copy in mark_copies + parent_copies + shell_copies[:early] + mine:
        copy.start()
    for i in range(2 * n_gy):
        land[me, i] = marks[i]

    last = 8 * count

    def tables(b, carry):
        ids = [near[b, k] for k in range(26)]
        offs = [i - first for i in ids]
        enough = carry
        for side in range(2):
            low, high = jnp.int32(6), jnp.int32(-1)
            for k in range(26):
                off = offs[k] if side else offs[k] + 2 * count
                there = (ids[k] >= 0) & (off >= count) & (off < 2 * count)
                low = jnp.where(there, lax.min(low, face_of[25 - k]), low)
                high = jnp.where(there, lax.max(high, face_of[25 - k]), high)
            face_pick[b * 2 + side] = lax.max(high, 0)
            enough = jnp.where((high >= 0) & (low != high), 0, enough)
        for k in range(26):
            off = offs[k]
            inside = (off >= 0) & (off < count)
            spot = jnp.where(inside, off * 6 + face_of[k], 6 * count + off)
            spot = jnp.where(off < 0, 7 * count + off, spot)
            spot = jnp.where(ids[k] >= 0, spot, last)
            spots[b * 26 + k] = lax.min(lax.max(spot, 0), last)
        return enough

    flag[0] = lax.fori_loop(0, count, tables, jnp.int32(1))
    for copy in flag_copies:
        copy.start()
    flags[me, 0] = flag[0]


    for copy in load[2:]:
        copy.wait()
    zero = jnp.zeros((made, made), conv.dtype)

    def arrange(yz, carry):
        for half, into in enumerate((right, right_s)):
            rows = slice(half * made, (half + 1) * made)
            for xx in range(4):
                at = pl.ds(pl.multiple_of((xx * 9 + yz) * made, made), made)
                into[at, 0:made] = conv[xx * 9 + yz, rows, :] if xx < 3 else zero
                into[at, made:] = conv[(xx - 1) * 9 + yz, rows, :] if xx > 0 else zero
        return carry

    lax.fori_loop(0, 9, arrange, 0)
    for pool in (pool_c, pool_s):
        pool[last] = jnp.zeros(pool.shape[1:], pool.dtype)
    spread[...] = jnp.zeros_like(spread)

    for copy in mark_copies + parent_copies:
        copy.wait_recv()
    mine[0].wait()
    for which in range(2):
        held = [land[d, which * n_gy + me] for d in range(n_gy)]
        for b in range(count):
            source = jnp.int32(0)
            for d in range(n_gy):
                source = jnp.where(held[d] == first + b, d, source)
            origin[which * count + b] = source

    def faces(b, pool):
        for f in range(6):
            edge = 7 * (f % 2)
            if f < 2:
                value = whole[b, edge * 64 : edge * 64 + 64]
            elif f < 4:
                value = jnp.concatenate(
                    [whole[b, x * 64 + edge * 8 : x * 64 + edge * 8 + 8] for x in range(8)], axis=0
                )
            else:
                value = whole[b, pl.ds(edge, 64, stride=8), :]
            value = value.astype(pool.dtype)
            own[b * 6 + f] = value
            pool[b * 6 + f] = value

    def faces_of_body(b, pool):
        for f in range(6):
            edge = 7 * (f % 2)
            if f < 2:
                rows = [body_s[b, pl.ds(column(edge + 1, y + 1) + 8, 8), :] for y in range(8)]
            elif f < 4:
                rows = [body_s[b, pl.ds(column(x + 1, edge + 1) + 8, 8), :] for x in range(8)]
            else:
                rows = [
                    body_s[b, pl.ds(column(x + 1, 1) + 8 + edge, 8, stride=PITCH), :]
                    for x in range(8)
                ]
            value = jnp.concatenate(rows, axis=0).astype(pool.dtype)
            own[b * 6 + f] = value
            pool[b * 6 + f] = value

    def send_halo(pool, halo, kind):
        def pack_halo(b, carry):
            for side in range(2):
                halo[side, b] = own[b * 6 + face_pick[b * 2 + side]]
            return carry

        lax.fori_loop(0, count, pack_halo, 0)
        down = pltpu.make_async_remote_copy(
            src_ref=halo.at[0],
            dst_ref=pool.at[pl.ds(7 * count, count)],
            send_sem=halo_sends.at[kind, 0],
            recv_sem=halo_receives.at[kind, 0],
            device_id=behind,
            device_id_type=MESH,
        )
        up_copy = pltpu.make_async_remote_copy(
            src_ref=halo.at[1],
            dst_ref=pool.at[pl.ds(6 * count, count)],
            send_sem=halo_sends.at[kind, 1],
            recv_sem=halo_receives.at[kind, 1],
            device_id=ahead,
            device_id_type=MESH,
        )

        @pl.when(has_ahead)
        def _():
            up_copy.start()

        @pl.when(has_behind)
        def _():
            down.start()

        return down, up_copy

    def wait_halo(copies):
        down, up_copy = copies

        @pl.when(has_ahead)
        def _():
            down.wait_recv()

        @pl.when(has_behind)
        def _():
            up_copy.wait_recv()

    def finish_halo(copies):
        down, up_copy = copies

        @pl.when(has_ahead)
        def _():
            up_copy.wait_send()

        @pl.when(has_behind)
        def _():
            down.wait_send()

    def upsample(b, carry):
        for half in range(2):
            values = recv_p[origin[b], :, half * 128 : (half + 1) * 128].astype(jnp.float32)
            for c in range(2):
                spread[c * 2 + half, pl.ds(c, 64, stride=2), :] = values
        rows = jnp.concatenate([spread[p] for p in range(4)], axis=1).astype(jnp.bfloat16)
        for a in range(2):
            for e in range(2):
                tap = a * 4 + e * 2
                weight = jnp.concatenate([up[tap], up[tap + 1]], axis=0)
                value = jnp.dot(rows, weight, preferred_element_type=jnp.float32)
                for i in range(4):
                    for j in range(4):
                        at = (2 * i + a) * 64 + (2 * j + e) * 8
                        whole[b, at : at + 8] = value[(i * 4 + j) * 8 : (i * 4 + j) * 8 + 8]

        faces(b, pool_c)
        return carry

    lax.fori_loop(0, count, upsample, 0)
    halo_copies = send_halo(pool_c, halo_c, 0)
    for copy in shell_copies[early:] + inside_copies:
        copy.start()

    def surround(b, pool, body):
        def taken(step):
            return pool.at[spots[b * 26 + direction_of[step]]]

        def part(step, low, high):
            return taken(step)[low:high].astype(jnp.float32)

        for ox in (-1, 1):
            u, ex = (0, 7) if ox < 0 else (9, 0)
            value = part((ox, 0, 0), 0, 64)
            for y in range(8):
                body[column(u, y + 1) + 8 : column(u, y + 1) + 16] = value[y * 8 : y * 8 + 8]
            for oy in (-1, 1):
                v, ey = (0, 7) if oy < 0 else (9, 0)
                low = ey * 8 // 16 * 16
                value = part((ox, oy, 0), low, low + 16)
                body[column(u, v) + 8 : column(u, v) + 16] = value[ey * 8 - low : ey * 8 - low + 8]
        for oy in (-1, 1):
            v = 0 if oy < 0 else 9
            value = part((0, oy, 0), 0, 64)
            for x in range(8):
                body[column(x + 1, v) + 8 : column(x + 1, v) + 16] = value[x * 8 : x * 8 + 8]
        for p, oz in enumerate((-1, 1)):
            z = 7 if oz < 0 else 16
            value = part((0, 0, oz), 0, 64)
            for x in range(8):
                body[pl.ds(column(x + 1, 1) + z, 8, stride=PITCH), :] = value[x * 8 : x * 8 + 8]
            for ox in (-1, 1):
                u, ex = (0, 7) if ox < 0 else (9, 0)
                low = ex * 8 // 16 * 16
                value = part((ox, 0, oz), low, low + 16)
                body[pl.ds(column(u, 1) + z, 8, stride=PITCH), :] = value[
                    ex * 8 - low : ex * 8 - low + 8
                ]
                for oy in (-1, 1):
                    v, ey = (0, 7) if oy < 0 else (9, 0)
                    value = part((ox, oy, oz), low, low + 16)
                    row = ex * 8 + ey - low
                    body[column(u, v) + z : column(u, v) + z + 1] = value[row : row + 1]
            for q, oy in enumerate((-1, 1)):
                v, ey = (0, 7) if oy < 0 else (9, 0)
                ghost[p * 2 + q] = part((0, oy, oz), 0, 64)
                body[pl.ds(column(1, v) + z, 8, stride=10 * PITCH), :] = ghost[
                    p * 2 + q, pl.ds(ey, 8, stride=8), :
                ]
    def shifts(body, even, odd):
        for dz in range(3):
            for u in range(10):
                blocks = [
                    body[column(u, v) + 7 + dz : column(u, v) + 15 + dz] for v in range(10)
                ]
                even[dz, u * 80 : u * 80 + 80] = jnp.concatenate(blocks, axis=0).astype(even.dtype)
                odd[dz, u * 64 : u * 64 + 64] = jnp.concatenate(blocks[1:9], axis=0).astype(
                    odd.dtype
                )

    wait_halo(halo_copies)

    def child_half(b, carry):
        for x in range(8):
            for y in range(8):
                at = column(x + 1, y + 1) + 8
                body[at : at + 8] = whole[b, x * 64 + y * 8 : x * 64 + y * 8 + 8]
        surround(b, pool_c, body)
        shifts(body, even, odd)
        acc[b] = product(even, odd, right)
        return carry

    lax.fori_loop(0, count, child_half, 0)

    for copy in shell_copies:
        copy.wait_recv()
    mine[1].wait()
    def outer_voxels(b, carry):
        outer = recv_shell[origin[count + b]].astype(jnp.float32)
        padded = body_s.at[b]
        for y in range(8):
            padded[column(1, y + 1) + 8 : column(1, y + 1) + 16] = outer[y * 8 : y * 8 + 8]
            padded[column(8, y + 1) + 8 : column(8, y + 1) + 16] = outer[64 + y * 8 : 72 + y * 8]
        for x in range(1, 7):
            at = 112 + x * 16
            padded[column(x + 1, 1) + 8 : column(x + 1, 1) + 16] = outer[at : at + 8]
            padded[column(x + 1, 8) + 8 : column(x + 1, 8) + 16] = outer[at + 8 : at + 16]
        strip[0:80] = outer[224:304]
        for i in range(12):
            at = column(i % 6 + 2, 2) + 8 + i // 6 * 7
            padded[pl.ds(at, 6, stride=PITCH), :] = strip[6 * i : 6 * i + 6]
        faces_of_body(b, pool_s)
        return carry

    lax.fori_loop(0, count, outer_voxels, 0)
    skip_halo = send_halo(pool_s, halo_s, 1)
    for copy in flag_copies:
        copy.wait_recv()
    enough = flags[0, 0]
    for d in range(1, n_gy):
        enough = lax.min(enough, flags[d, 0])
    agree[0] = enough
    agrees[gx, 0] = enough
    agree_copies = [
        pltpu.make_async_remote_copy(
            src_ref=agree,
            dst_ref=agrees.at[gx],
            send_sem=agree_sends.at[step],
            recv_sem=agree_receives.at[step],
            device_id={"gx": lax.rem(gx + step, n_gx)},
            device_id_type=MESH,
        )
        for step in range(1, n_gx)
    ]
    for copy in agree_copies:
        copy.start()
    wait_halo(skip_halo)
    def surround_skip(b, carry):
        surround(b, pool_s, body_s.at[b])
        return carry

    lax.fori_loop(0, count, surround_skip, 0)

    for copy in inside_copies:
        copy.wait_recv()
    mine[2].wait()
    def inner_voxels(b, carry):
        padded = body_s.at[b]
        strip[80:304] = recv_inside[origin[count + b]].astype(jnp.float32)
        for i in range(36):
            at = column(i // 6 + 2, i % 6 + 2) + 9
            padded[at : at + 6] = strip[80 + 6 * i : 86 + 6 * i]
        shifts(padded, even_s.at[b], odd_s.at[b])
        return carry

    lax.fori_loop(0, count, inner_voxels, 0)

    for copy in mark_copies + parent_copies + shell_copies + inside_copies + flag_copies:
        copy.wait_send()
    finish_halo(halo_copies)
    finish_halo(skip_halo)
    for copy in agree_copies:
        copy.wait()
    for x in range(n_gx):
        enough = lax.min(enough, agrees[x, 0])
    agreed[0] = enough

def finish_kernel(acc, even, odd, right, out, result, sems):
    copies = []
    for b in range(acc.shape[0]):
        made = acc.shape[2] // 2
        total = acc[b] + product(even.at[b], odd.at[b], right)
        total = jnp.maximum(total, 0.0).astype(result.dtype)
        for s in range(4):
            for p in range(2):
                at = (2 * s + p) * 64
                result[b, at : at + 64] = total[s * 64 : s * 64 + 64, p * made : (p + 1) * made]
        copies.append(pltpu.make_async_copy(result.at[b], out.at[b], sems.at[b]))
        copies[-1].start()
    for copy in copies:
        copy.wait()


def finish(acc, even, odd, right):
    count, made = acc.shape[0], acc.shape[2] // 2
    shape = (count, 2 * acc.shape[1], made)
    return pl.pallas_call(
        finish_kernel,
        out_shape=pltpu.HBM(shape, jnp.bfloat16),
        in_specs=[vmem()] * 4,
        out_specs=pl.BlockSpec(memory_space=pltpu.HBM),
        scratch_shapes=[
            pltpu.VMEM(shape, jnp.bfloat16),
            pltpu.SemaphoreType.DMA((count,)),
        ],
        compiler_params=pltpu.CompilerParams(vmem_limit_bytes=24 * 2**20),
        name="finish",
    )(acc, even, odd, right)


META = 8


def vmem():
    return pl.BlockSpec(memory_space=pltpu.VMEM)


def pack_kernel(
    gy_count, bricks_dev, pdest, sdest, parents, skip, out_p, out_s, land, sem_p, sem_s
):
    slots, voxels = parents.shape[0], parents.shape[1]
    for d in range(gy_count):
        land[0, d] = -1
        land[1, d] = -1

    def copies(s):
        tp, ts = pdest[s], sdest[s]
        op = lax.rem(lax.div(jnp.maximum(tp, 0), bricks_dev), gy_count)
        os = lax.rem(lax.div(jnp.maximum(ts, 0), bricks_dev), gy_count)
        cp = pltpu.make_async_copy(parents.at[s], out_p.at[op, pl.ds(0, voxels)], sem_p.at[s])
        cs = pltpu.make_async_copy(skip.at[s], out_s.at[os], sem_s.at[s])
        return (tp, op, cp), (ts, os, cs)

    for s in range(slots):
        for which, (t, o, c) in enumerate(copies(s)):

            @pl.when(t >= 0)
            def _():
                land[which, o] = lax.rem(t, bricks_dev)
                c.start()

    for d in range(gy_count):
        half = parents.shape[2] // 2
        for which in range(2):
            mark = jnp.full((META, half), land[which, d], jnp.int32).astype(jnp.float32)
            out_p[d, voxels : voxels + META, which * half : (which + 1) * half] = mark.astype(
                jnp.bfloat16
            )
    for s in range(slots):
        for t, o, c in copies(s):

            @pl.when(t >= 0)
            def _():
                c.wait()


def pack(parent_dest, skip_dest, parents, skip, bricks_dev, gy_count):
    slots, voxels, channels = parents.shape
    return pl.pallas_call(
        functools.partial(pack_kernel, gy_count, bricks_dev),
        out_shape=(
            jax.ShapeDtypeStruct((gy_count, voxels + META, channels), parents.dtype),
            jax.ShapeDtypeStruct((gy_count,) + skip.shape[1:], skip.dtype),
        ),
        in_specs=[smem(), smem(), anywhere(), anywhere()],
        out_specs=(vmem(), vmem()),
        scratch_shapes=[
            pltpu.SMEM((2, gy_count), jnp.int32),
            pltpu.SemaphoreType.DMA((slots,)),
            pltpu.SemaphoreType.DMA((slots,)),
        ],
        compiler_params=pltpu.CompilerParams(vmem_limit_bytes=VMEM_LIMIT),
        name="pack",
    )(parent_dest, skip_dest, parents, skip)


def exchange_kernel(gy_count, in_p, in_s, out_p, out_s, sends, receives, own):
    me = lax.axis_index("gy")
    mine = [
        pltpu.make_async_copy(in_p.at[me], out_p.at[me], own.at[0]),
        pltpu.make_async_copy(in_s.at[me], out_s.at[me], own.at[1]),
    ]
    for copy in mine:
        copy.start()
    barrier = pltpu.get_barrier_semaphore()
    shifts = sorted(range(1, gy_count), key=lambda s: abs(s - gy_count // 2))
    for shift in shifts:
        pl.semaphore_signal(
            barrier,
            inc=1,
            device_id={"gy": lax.rem(me + shift, gy_count)},
            device_id_type=pl.DeviceIdType.MESH,
        )
    pl.semaphore_wait(barrier, gy_count - 1)
    copies = []
    for which, (source, landing) in enumerate(((in_p, out_p), (in_s, out_s))):
        for shift in shifts:
            there = lax.rem(me + shift, gy_count)
            copy = pltpu.make_async_remote_copy(
                src_ref=source.at[there],
                dst_ref=landing.at[me],
                send_sem=sends.at[which, shift],
                recv_sem=receives.at[which, shift],
                device_id={"gy": there},
                device_id_type=pl.DeviceIdType.MESH,
            )
            copy.start()
            copies.append(copy)
    for copy in copies:
        copy.wait()
    for copy in mine:
        copy.wait()


def exchange(in_p, in_s):
    gy_count = in_p.shape[0]
    return pl.pallas_call(
        functools.partial(exchange_kernel, gy_count),
        out_shape=tuple(jax.ShapeDtypeStruct(a.shape, a.dtype) for a in (in_p, in_s)),
        in_specs=[anywhere(), anywhere()],
        out_specs=(anywhere(), anywhere()),
        scratch_shapes=[
            pltpu.SemaphoreType.DMA((2, gy_count)),
            pltpu.SemaphoreType.DMA((2, gy_count)),
            pltpu.SemaphoreType.DMA((2,)),
        ],
        compiler_params=pltpu.CompilerParams(
            collective_id=2, has_side_effects=True, vmem_limit_bytes=2**20
        ),
        name="exchange",
    )(in_p, in_s)


def halo_kernel(size, inner, to_before, to_after, from_before, from_after, sends, receives):
    me = lax.axis_index("gx") * inner + lax.axis_index("gy")

    def coordinates(device):
        device = lax.max(device, 0)
        return (lax.div(device, inner), lax.rem(device, inner))

    ahead, behind = coordinates(me + 1), coordinates(me - 1)
    has_ahead, has_behind = me < size - 1, me > 0
    barrier = pltpu.get_barrier_semaphore()
    mesh_id = pl.DeviceIdType.MESH

    @pl.when(has_ahead)
    def _():
        pl.semaphore_signal(barrier, inc=1, device_id=ahead, device_id_type=mesh_id)

    @pl.when(has_behind)
    def _():
        pl.semaphore_signal(barrier, inc=1, device_id=behind, device_id_type=mesh_id)

    pl.semaphore_wait(barrier, has_ahead.astype(jnp.int32) + has_behind.astype(jnp.int32))
    up = pltpu.make_async_remote_copy(
        src_ref=to_after,
        dst_ref=from_before,
        send_sem=sends.at[0],
        recv_sem=receives.at[0],
        device_id=ahead,
        device_id_type=mesh_id,
    )
    down = pltpu.make_async_remote_copy(
        src_ref=to_before,
        dst_ref=from_after,
        send_sem=sends.at[1],
        recv_sem=receives.at[1],
        device_id=behind,
        device_id_type=mesh_id,
    )

    @pl.when(has_ahead)
    def _():
        up.start()

    @pl.when(has_behind)
    def _():
        down.start()

    @pl.when(has_ahead)
    def _():
        up.wait_send()
        down.wait_recv()

    @pl.when(has_behind)
    def _():
        down.wait_send()
        up.wait_recv()


def halo(to_before, to_after):
    inner = lax.axis_size("gy")
    size = lax.axis_size("gx") * inner
    return pl.pallas_call(
        functools.partial(halo_kernel, size, inner),
        out_shape=(
            jax.ShapeDtypeStruct(to_after.shape, to_after.dtype),
            jax.ShapeDtypeStruct(to_before.shape, to_before.dtype),
        ),
        in_specs=[anywhere(), anywhere()],
        out_specs=(anywhere(), anywhere()),
        scratch_shapes=[pltpu.SemaphoreType.DMA((2,)), pltpu.SemaphoreType.DMA((2,))],
        compiler_params=pltpu.CompilerParams(
            collective_id=1, has_side_effects=True, vmem_limit_bytes=2**20
        ),
        name="halo",
    )(to_before, to_after)


def build_kernel(
    source, near, pay, skip, up, feats, faces, before, after, spread, whole, sent
):
    channels = up.shape[1]
    made = up.shape[2]

    @pl.when(pl.program_id(0) == 0)
    def _():
        spread[...] = jnp.zeros_like(spread)

    for half in range(channels // 128):
        values = pay[0, 0:64, half * 128 : (half + 1) * 128].astype(jnp.float32)
        for c in range(2):
            spread[c * (channels // 128) + half, pl.ds(c, 64, stride=2), :] = values
    rows = jnp.concatenate([spread[p] for p in range(spread.shape[0])], axis=1).astype(jnp.bfloat16)
    for a in range(2):
        for b in range(2):
            tap = a * 4 + b * 2
            weight = jnp.concatenate([up[tap], up[tap + 1]], axis=0)
            value = jnp.dot(rows, weight, preferred_element_type=jnp.float32)
            for i in range(4):
                for j in range(4):
                    at = (2 * i + a) * 64 + (2 * j + b) * 8
                    for p in range(made // 128):
                        whole[p, at : at + 8] = value[
                            (i * 4 + j) * 8 : (i * 4 + j) * 8 + 8, p * 128 : (p + 1) * 128
                        ]
    for p in range(made // 128, whole.shape[0]):
        at = p * 128 - made
        whole[p] = skip[0, :, at : at + 128].astype(jnp.float32)
    for p in range(whole.shape[0]):
        lanes = slice(p * 128, (p + 1) * 128)
        feats[0, :, lanes] = whole[p].astype(jnp.bfloat16)
        for side in range(2):
            edge = 7 * side
            faces[0, side, :, lanes] = whole[p, edge * 64 : edge * 64 + 64].astype(jnp.bfloat16)
            faces[0, 2 + side, :, lanes] = jnp.concatenate(
                [whole[p, x * 64 + edge * 8 : x * 64 + edge * 8 + 8] for x in range(8)], axis=0
            ).astype(jnp.bfloat16)
            faces[0, 4 + side, :, lanes] = whole[p, pl.ds(edge, 64, stride=8), :].astype(
                jnp.bfloat16
            )
    brick = pl.program_id(0)
    count = before.shape[1]
    first = (lax.axis_index("gx") * lax.axis_size("gy") + lax.axis_index("gy")) * count
    for m in range(2 * count):
        sent[m] = 0
    for k, face in enumerate(face_of[::-1]):
        n = near[brick, k]
        off = n - first
        spot = jnp.where(off < 0, off + count, jnp.where(off >= count, off, 2 * count))
        sent[jnp.where(n >= 0, spot, 2 * count)] = face
    for m in range(count):
        before[0, m] = faces[0, sent[m]]
        after[0, m] = faces[0, sent[count + m]]


def build(source, near, pay, skip, up_weight, bricks_dev):
    channels, made = up_weight.shape[1:]
    joined = made + skip.shape[2]
    return pl.pallas_call(
        build_kernel,
        out_shape=(
            jax.ShapeDtypeStruct((bricks_dev, 512, joined), jnp.bfloat16),
            jax.ShapeDtypeStruct((bricks_dev, 6, 64, joined), jnp.bfloat16),
            jax.ShapeDtypeStruct((bricks_dev, bricks_dev, 64, joined), jnp.bfloat16),
            jax.ShapeDtypeStruct((bricks_dev, bricks_dev, 64, joined), jnp.bfloat16),
        ),
        grid_spec=pltpu.PrefetchScalarGridSpec(
            num_scalar_prefetch=2,
            grid=(bricks_dev,),
            in_specs=[
                pl.BlockSpec((1,) + pay.shape[1:], lambda b, s, t: (s[0, b], 0, 0)),
                pl.BlockSpec((1,) + skip.shape[1:], lambda b, s, t: (s[1, b], 0, 0)),
                pl.BlockSpec(up_weight.shape, lambda b, s, t: (0, 0, 0)),
            ],
            out_specs=(
                pl.BlockSpec((1, 512, joined), lambda b, s, t: (b, 0, 0)),
                pl.BlockSpec((1, 6, 64, joined), lambda b, s, t: (b, 0, 0, 0)),
                pl.BlockSpec((1, bricks_dev, 64, joined), lambda b, s, t: (b, 0, 0, 0)),
                pl.BlockSpec((1, bricks_dev, 64, joined), lambda b, s, t: (b, 0, 0, 0)),
            ),
            scratch_shapes=[
                pltpu.VMEM((2 * channels // 128, 128, 128), jnp.float32),
                pltpu.VMEM((joined // 128, 512, 128), jnp.float32),
                pltpu.SMEM((2 * bricks_dev + 1,), jnp.int32),
            ],
        ),
        compiler_params=pltpu.CompilerParams(vmem_limit_bytes=VMEM_LIMIT),
        name="build",
    )(source, near, pay, skip, up_weight)


def refine_kernel(
    near,
    feats,
    own,
    before,
    after,
    weight,
    out,
    pool,
    sems,
    body,
    plane,
    left,
    right,
    early,
    late,
):
    brick = pl.program_id(0)
    joined, made = weight.shape[1:]

    @pl.when(brick == 0)
    def _():
        copies, first = [], 0
        for i, part in enumerate((own, before, after)):
            length = part.shape[0]
            copies.append(pltpu.make_async_copy(part, pool.at[pl.ds(first, length)], sems.at[i]))
            copies[-1].start()
            first += length
        for tap in range(9):
            for dz in range(3):
                right[tap * joined : (tap + 1) * joined, dz * made : (dz + 1) * made] = weight[
                    tap * 3 + dz
                ]
        for copy in copies:
            copy.wait()

    count = pl.num_programs(0)
    first = (lax.axis_index("gx") * lax.axis_size("gy") + lax.axis_index("gy")) * count
    ahead = own.shape[0] + count * count + brick
    behind = before.shape[0] - 2 * count * count

    def taken(step, start, length):
        k = direction_of[step]
        n = near[brick, k]
        off = n - first
        spot = jnp.where(off < 0, ahead + off * count, ahead + behind + off * count)
        spot = jnp.where((off >= 0) & (off < count), off * 6 + face_of[k], spot)
        spot = jnp.where(n >= 0, spot, 0)
        low = start // 16 * 16
        high = -(-(start + length) // 16) * 16
        value = pool[spot, low:high, :].astype(jnp.float32)
        return jnp.where(n >= 0, value[start - low : start - low + length], 0.0)

    body[1:9, 1:9] = feats[0].astype(jnp.float32).reshape(8, 8, 8, joined)
    for ox in (-1, 1):
        u = 0 if ox < 0 else 9
        body[u, 1:9] = taken((ox, 0, 0), 0, 64).reshape(8, 8, joined)
        for oy in (-1, 1):
            v, ey = (0, 7) if oy < 0 else (9, 0)
            body[u, v] = taken((ox, oy, 0), ey * 8, 8)
    for oy in (-1, 1):
        v = 0 if oy < 0 else 9
        body[1:9, v] = taken((0, oy, 0), 0, 64).reshape(8, 8, joined)
    for p, oz in enumerate((-1, 1)):
        plane[p, 1:9, 1:9] = taken((0, 0, oz), 0, 64).reshape(8, 8, joined)
        for ox in (-1, 1):
            u, ex = (0, 7) if ox < 0 else (9, 0)
            plane[p, u, 1:9] = taken((ox, 0, oz), ex * 8, 8)
            for oy in (-1, 1):
                v, ey = (0, 7) if oy < 0 else (9, 0)
                row = taken((ox, oy, oz), ex * 8, 8)
                plane[p, u, v : v + 1] = row[ey : ey + 1]
        for oy in (-1, 1):
            v, ey = (0, 7) if oy < 0 else (9, 0)
            value = taken((0, oy, oz), 0, 64).reshape(8, 8, joined)
            plane[p, 1:9, v : v + 1] = value[:, ey : ey + 1]

    for tap in range(9):
        dx, dy = tap // 3, tap % 3
        lanes = slice(tap * joined, (tap + 1) * joined)
        left[0:512, lanes] = (
            body[dx : dx + 8, dy : dy + 8].reshape(512, joined).astype(jnp.bfloat16)
        )
        for p in range(2):
            left[512 + 64 * p : 576 + 64 * p, lanes] = (
                plane[p, dx : dx + 8, dy : dy + 8].reshape(64, joined).astype(jnp.bfloat16)
            )
    total = jnp.dot(left[...], right[...], preferred_element_type=jnp.float32)
    early[1:513] = total[0:512, 0:made]
    early[pl.ds(0, 64, stride=8), :] = total[512:576, 0:made]
    late[7:519] = total[0:512, 2 * made : 3 * made]
    late[pl.ds(15, 64, stride=8), :] = total[576:640, 2 * made : 3 * made]
    result = early[0:512] + total[0:512, made : 2 * made] + late[8:520]
    out[0] = jnp.maximum(result, 0.0).astype(jnp.bfloat16)


def refine(near, feats, own, before, after, conv_weight):
    bricks_dev, voxels, joined = feats.shape
    made = conv_weight.shape[2]
    return pl.pallas_call(
        refine_kernel,
        out_shape=jax.ShapeDtypeStruct((bricks_dev, voxels, made), jnp.bfloat16),
        grid_spec=pltpu.PrefetchScalarGridSpec(
            num_scalar_prefetch=1,
            grid=(bricks_dev,),
            in_specs=[
                pl.BlockSpec((1, voxels, joined), lambda b, s: (b, 0, 0)),
                anywhere(),
                anywhere(),
                anywhere(),
                pl.BlockSpec(conv_weight.shape, lambda b, s: (0, 0, 0)),
            ],
            out_specs=pl.BlockSpec((1, voxels, made), lambda b, s: (b, 0, 0)),
            scratch_shapes=[
                pltpu.VMEM((sum(a.shape[0] for a in (own, before, after)), 64, joined), own.dtype),
                pltpu.SemaphoreType.DMA((3,)),
                pltpu.VMEM((10, 10, 8, joined), jnp.float32),
                pltpu.VMEM((2, 10, 16, joined), jnp.float32),
                pltpu.VMEM((640, 9 * joined), jnp.bfloat16),
                pltpu.VMEM((9 * joined, 3 * made), jnp.bfloat16),
                pltpu.VMEM((520, made), jnp.float32),
                pltpu.VMEM((520, made), jnp.float32),
            ],
        ),
        compiler_params=pltpu.CompilerParams(vmem_limit_bytes=VMEM_LIMIT),
        name="refine",
    )(near, feats, own, before, after, conv_weight)


def general(parents, parent_dest, skip, skip_dest, neighbours, up_weight, conv_weight):
    bricks_dev = neighbours.shape[0]
    gy_count = lax.axis_size("gy")
    sent_p, sent_s = pack(parent_dest, skip_dest, parents, skip, bricks_dev, gy_count)
    came_p, came_s = exchange(sent_p, sent_s)
    voxels, channels = parents.shape[1:]
    spots = jnp.stack([came_p[:, voxels, 0], came_p[:, voxels, channels // 2]]).astype(jnp.int32)
    matches = spots[:, None, :] == jnp.arange(bricks_dev)[None, :, None]
    source = jnp.sum(jnp.where(matches, jnp.arange(gy_count)[None, None, :], 0), axis=2)
    feats, faces, to_before, to_after = build(
        source.astype(jnp.int32), neighbours, came_p, came_s, up_weight, bricks_dev
    )
    flat = (-1,) + faces.shape[2:]
    before, after = halo(to_before.reshape(flat), to_after.reshape(flat))
    return refine(neighbours, feats, faces.reshape(flat), before, after, conv_weight)


def per_device(parents, parent_dest, skip, skip_dest, neighbours, up_weight, conv_weight):
    count = neighbours.shape[0]
    n_gx, n_gy = lax.axis_size("gx"), lax.axis_size("gy")
    voxels = skip.shape[1]
    made = conv_weight.shape[2]
    bf16, f32 = jnp.bfloat16, jnp.float32
    pool = (8 * count + 1, 64, made)
    dma = pltpu.SemaphoreType.DMA
    width = 2 * made
    acc, even, odd, right, agreed = pl.pallas_call(
        functools.partial(kernel, n_gx, n_gy),
        out_shape=(
            pltpu.VMEM((count, voxels // 2, width), f32),
            pltpu.VMEM((count, 3, 800, made), bf16),
            pltpu.VMEM((count, 3, 640, made), bf16),
            pltpu.VMEM((36 * made, width), bf16),
            jax.ShapeDtypeStruct((1,), jnp.int32),
        ),
        in_specs=[anywhere()] * 7,
        out_specs=(vmem(), vmem(), vmem(), vmem(), smem()),
        scratch_shapes=[
            pltpu.SMEM(parent_dest.shape, jnp.int32),
            pltpu.SMEM(skip_dest.shape, jnp.int32),
            pltpu.SMEM(neighbours.shape, jnp.int32),
            pltpu.VMEM(parents.shape, bf16),
            pltpu.VMEM(skip.shape, bf16),
            pltpu.VMEM(up_weight.shape, bf16),
            pltpu.VMEM(conv_weight.shape, bf16),
            pltpu.VMEM((n_gy,) + parents.shape[1:], bf16),
            pltpu.VMEM((n_gy, 304, skip.shape[2]), bf16),
            pltpu.VMEM((n_gy, 224, skip.shape[2]), bf16),
            pltpu.VMEM((n_gy,) + parents.shape[1:], bf16),
            pltpu.VMEM((n_gy, 304, skip.shape[2]), bf16),
            pltpu.VMEM((n_gy, 224, skip.shape[2]), bf16),
            pltpu.SMEM((2 * n_gy,), jnp.int32),
            pltpu.SMEM((n_gy, 2 * n_gy), jnp.int32),
            pltpu.SMEM((2 * n_gy,), jnp.int32),
            pltpu.SMEM((2 * count,), jnp.int32),
            pltpu.SMEM((1,), jnp.int32),
            pltpu.SMEM((n_gy, 1), jnp.int32),
            pltpu.VMEM((voxels, skip.shape[2]), f32),
            pltpu.VMEM((304, skip.shape[2]), f32),
            pltpu.SMEM((1,), jnp.int32),
            pltpu.SMEM((n_gx, 1), jnp.int32),
            pltpu.SMEM((2 * count,), jnp.int32),
            pltpu.SMEM((26 * count,), jnp.int32),
            pltpu.VMEM((4, 128, 128), f32),
            pltpu.VMEM((count, voxels, made), f32),
            pltpu.VMEM((4, 64, made), f32),
            pltpu.VMEM((6 * count, 64, made), bf16),
            pltpu.VMEM(pool, bf16),
            pltpu.VMEM(pool, bf16),
            pltpu.VMEM((2, count, 64, made), bf16),
            pltpu.VMEM((2, count, 64, made), bf16),
            pltpu.VMEM((100 * PITCH, made), f32),
            pltpu.VMEM((count, 100 * PITCH, made), f32),
            pltpu.VMEM((3, 800, made), bf16),
            pltpu.VMEM((3, 640, made), bf16),
            pltpu.VMEM((36 * made, width), bf16),
            dma((7,)),
            dma((5, n_gy)),
            dma((5, n_gy)),
            dma((2, 2)),
            dma((2, 2)),
            dma((3,)),
            dma((n_gx,)),
            dma((n_gx,)),
        ],
        compiler_params=pltpu.CompilerParams(
            collective_id=0, has_side_effects=True, vmem_limit_bytes=40 * 2**20
        ),
        name="refine_level",
    )(parent_dest, skip_dest, neighbours, parents, skip, up_weight, conv_weight)
    return lax.switch(
        agreed[0],
        [
            lambda: general(
                parents, parent_dest, skip, skip_dest, neighbours, up_weight, conv_weight
            ),
            lambda: finish(acc, even, odd, right),
        ],
    )


def solution(mesh):
    placed = (
        P(("gx", "gy"), None, None),
        P(("gx", "gy")),
        P(("gx", "gy"), None, None),
        P(("gx", "gy")),
        P(("gx", "gy"), None),
        P(),
        P(),
    )
    return jax.shard_map(
        per_device,
        mesh=mesh,
        in_specs=placed,
        out_specs=P(("gx", "gy"), None, None),
        check_vma=False,
    )
```

```python
import functools

import jax
import jax.numpy as jnp
from jax import lax
from jax.experimental import pallas as pl
from jax.experimental.pallas import tpu as pltpu
from jax.sharding import PartitionSpec as P

steps = [(code // 9 - 1, code // 3 % 3 - 1, code % 3 - 1) for code in range(27) if code != 13]
direction_of = {step: k for k, step in enumerate(steps)}
face_of = [
    (1 if x < 0 else 0) if x and not z else (5 if z < 0 else 4) if z else (3 if y < 0 else 2)
    for x, y, z in steps
]
PITCH = 24
VMEM_LIMIT = 24 * 2**20
SHELL, INSIDE = 296, 216
MESH = pl.DeviceIdType.MESH


def smem():
    return pl.BlockSpec(memory_space=pltpu.SMEM)


def anywhere():
    return pl.BlockSpec(memory_space=pl.ANY)


def partner(me, step):
    other, bit = me, 1
    while bit <= step:
        if step & bit:
            other = other + bit * (1 - 2 * lax.rem(lax.div(me, bit), 2))
        bit *= 2
    return other


def column(u, v):
    return (u * 10 + v) * PITCH


def product(even, odd, right):
    parts = []
    for xx in range(4):
        for dy in range(3):
            for dz in range(3):
                if dy == 1:
                    rows = [odd[dz, (2 * s + xx) * 64 : (2 * s + xx) * 64 + 64] for s in range(4)]
                else:
                    at = [(2 * s + xx) * 80 + dy * 8 for s in range(4)]
                    rows = [even[dz, a : a + 64] for a in at]
                parts.append(jnp.concatenate(rows, axis=0))
    left = jnp.concatenate(parts, axis=1)
    return jnp.dot(left, right[...], preferred_element_type=jnp.float32)


def kernel(
    n_gx,
    n_gy,
    pdest_hbm,
    sdest_hbm,
    near_hbm,
    parents_hbm,
    skip_hbm,
    up_hbm,
    conv_hbm,
    acc,
    even_s,
    odd_s,
    right_s,
    agreed,
    pdest,
    sdest,
    near,
    parents,
    skip,
    up,
    conv,
    stage_p,
    stage_shell,
    stage_inside,
    recv_p,
    recv_shell,
    recv_inside,
    marks,
    land,
    chosen,
    origin,
    flag,
    flags,
    wide,
    strip,
    agree,
    agrees,
    face_pick,
    spots,
    spread,
    whole,
    ghost,
    own,
    pool_c,
    pool_s,
    halo_c,
    halo_s,
    body,
    body_s,
    even,
    odd,
    right,
    loads,
    sends,
    receives,
    halo_sends,
    halo_receives,
    own_copy,
    agree_sends,
    agree_receives,
):
    slots = parents.shape[0]
    count = near.shape[0]
    made = whole.shape[2]
    gx, me = lax.axis_index("gx"), lax.axis_index("gy")
    flat = gx * n_gy + me
    first = flat * count
    has_ahead, has_behind = flat < n_gx * n_gy - 1, flat > 0

    def coordinates(device):
        device = lax.max(device, 0)
        return (lax.div(device, n_gy), lax.rem(device, n_gy))

    ahead, behind = coordinates(flat + 1), coordinates(flat - 1)
    cross = list(range(n_gy // 2, n_gy))
    rest = list(range(2, n_gy // 2)) + [1]
    order = cross + rest

    barrier = pltpu.get_barrier_semaphore()
    wraps_ahead = has_ahead & (me == n_gy - 1)
    wraps_behind = has_behind & (me == 0)

    @pl.when(wraps_ahead)
    def _():
        pl.semaphore_signal(barrier, inc=1, device_id=ahead, device_id_type=MESH)

    @pl.when(wraps_behind)
    def _():
        pl.semaphore_signal(barrier, inc=1, device_id=behind, device_id_type=MESH)

    for step in order:
        pl.semaphore_signal(
            barrier, inc=1, device_id={"gy": partner(me, step)}, device_id_type=MESH
        )

    for step in range(1, n_gx):
        pl.semaphore_signal(
            barrier, inc=1, device_id={"gx": lax.rem(gx + step, n_gx)}, device_id_type=MESH
        )

    load = [
        pltpu.make_async_copy(parents_hbm, parents, loads.at[0]),
        pltpu.make_async_copy(skip_hbm, skip, loads.at[1]),
        pltpu.make_async_copy(up_hbm, up, loads.at[2]),
        pltpu.make_async_copy(conv_hbm, conv, loads.at[3]),
    ]
    tables_in = [
        pltpu.make_async_copy(pdest_hbm, pdest, loads.at[4]),
        pltpu.make_async_copy(sdest_hbm, sdest, loads.at[5]),
        pltpu.make_async_copy(near_hbm, near, loads.at[6]),
    ]
    for copy in tables_in + load:
        copy.start()
    for copy in tables_in:
        copy.wait()

    for which, dest in enumerate((pdest, sdest)):
        targets = [dest[s] for s in range(slots)]
        owners = [
            jnp.where(t >= 0, lax.rem(lax.div(lax.max(t, 0), count), n_gy), -1) for t in targets
        ]
        for d in range(n_gy):
            slot, mark = jnp.int32(0), jnp.int32(-1)
            for s in range(slots):
                here = owners[s] == d
                slot = jnp.where(here, s, slot)
                mark = jnp.where(here, targets[s], mark)
            marks[which * n_gy + d] = mark
            chosen[which * n_gy + d] = slot

    load[0].wait()
    for d in range(n_gy):
        stage_p[d] = parents[chosen[d]]
    load[1].wait()

    def split(d, carry):
        wide[...] = skip[chosen[n_gy + d]].astype(jnp.float32)
        columns = [wide[0:64], wide[448:512]]
        for x in range(1, 7):
            columns += [wide[x * 64 : x * 64 + 8], wide[x * 64 + 56 : x * 64 + 64]]
        stage_shell[d, 0:224] = jnp.concatenate(columns, axis=0).astype(stage_shell.dtype)
        for i in range(12):
            z, x = i // 6 * 7, i % 6 + 1
            strip[6 * i : 6 * i + 8] = wide[pl.ds(x * 64 + 8 + z, 8, stride=8), :]
        stage_shell[d, 224:304] = strip[0:80].astype(stage_shell.dtype)
        for i in range(36):
            at = (i // 6 + 1) * 64 + (i % 6 + 1) * 8 + 1
            strip[80 + 6 * i : 88 + 6 * i] = wide[at : at + 8]
        stage_inside[d] = strip[80:304].astype(stage_inside.dtype)
        return carry

    lax.fori_loop(0, n_gy, split, 0)

    pl.semaphore_wait(
        barrier, n_gx + n_gy - 2 + wraps_ahead.astype(jnp.int32) + wraps_behind.astype(jnp.int32)
    )

    def remote(source, landing, kind, step):
        return pltpu.make_async_remote_copy(
            src_ref=source,
            dst_ref=landing,
            send_sem=sends.at[kind, step],
            recv_sem=receives.at[kind, step],
            device_id={"gy": partner(me, step)},
            device_id_type=MESH,
        )

    mark_copies = [remote(marks, land.at[me], 0, s) for s in order]
    parent_copies = [remote(stage_p.at[partner(me, s)], recv_p.at[me], 1, s) for s in order]
    shell_copies, inside_copies = [
        [remote(stage.at[partner(me, s), pl.ds(0, size)], recv.at[me, pl.ds(0, size)], kind, s) for s in order]
        for kind, stage, recv, size in (
            (2, stage_shell, recv_shell, SHELL),
            (3, stage_inside, recv_inside, INSIDE),
        )
    ]
    flag_copies = [remote(flag, flags.at[me], 4, s) for s in order]
    mine = [
        pltpu.make_async_copy(stage.at[me], recv.at[me], own_copy.at[i])
        for i, (stage, recv) in enumerate(
            ((stage_p, recv_p), (stage_shell, recv_shell), (stage_inside, recv_inside))
        )
    ]
    far, early = len(cross), max(1, len(cross) * 3 // 4)
    for copy in mark_copies + parent_copies + shell_copies[far:] + shell_copies[:early] + mine:
        copy.start()
    for i in range(2 * n_gy):
        land[me, i] = marks[i]

    last = 8 * count

    def tables(b, carry):
        ids = [near[b, k] for k in range(26)]
        offs = [i - first for i in ids]
        enough = carry
        for side in range(2):
            low, high = jnp.int32(6), jnp.int32(-1)
            for k in range(26):
                off = offs[k] if side else offs[k] + 2 * count
                there = (ids[k] >= 0) & (off >= count) & (off < 2 * count)
                low = jnp.where(there, lax.min(low, face_of[25 - k]), low)
                high = jnp.where(there, lax.max(high, face_of[25 - k]), high)
            face_pick[b * 2 + side] = lax.max(high, 0)
            enough = jnp.where((high >= 0) & (low != high), 0, enough)
        for k in range(26):
            off = offs[k]
            inside = (off >= 0) & (off < count)
            spot = jnp.where(inside, off * 6 + face_of[k], 6 * count + off)
            spot = jnp.where(off < 0, 7 * count + off, spot)
            spot = jnp.where(ids[k] >= 0, spot, last)
            spots[b * 26 + k] = lax.min(lax.max(spot, 0), last)
        return enough

    flag[0] = lax.fori_loop(0, count, tables, jnp.int32(1))
    for copy in flag_copies:
        copy.start()
    flags[me, 0] = flag[0]


    for copy in load[2:]:
        copy.wait()
    zero = jnp.zeros((made, made), conv.dtype)

    def arrange(yz, carry):
        for half, into in enumerate((right, right_s)):
            rows = slice(half * made, (half + 1) * made)
            for xx in range(4):
                at = pl.ds(pl.multiple_of((xx * 9 + yz) * made, made), made)
                into[at, 0:made] = conv[xx * 9 + yz, rows, :] if xx < 3 else zero
                into[at, made:] = conv[(xx - 1) * 9 + yz, rows, :] if xx > 0 else zero
        return carry

    lax.fori_loop(0, 9, arrange, 0)
    for pool in (pool_c, pool_s):
        pool[last] = jnp.zeros(pool.shape[1:], pool.dtype)
    spread[...] = jnp.zeros_like(spread)

    for copy in mark_copies + parent_copies:
        copy.wait_recv()
    mine[0].wait()
    for which in range(2):
        held = [land[d, which * n_gy + me] for d in range(n_gy)]
        for b in range(count):
            source = jnp.int32(0)
            for d in range(n_gy):
                source = jnp.where(held[d] == first + b, d, source)
            origin[which * count + b] = source

    def faces(b, pool):
        for f in range(6):
            edge = 7 * (f % 2)
            if f < 2:
                value = whole[b, edge * 64 : edge * 64 + 64]
            elif f < 4:
                value = jnp.concatenate(
                    [whole[b, x * 64 + edge * 8 : x * 64 + edge * 8 + 8] for x in range(8)], axis=0
                )
            else:
                value = whole[b, pl.ds(edge, 64, stride=8), :]
            value = value.astype(pool.dtype)
            own[b * 6 + f] = value
            pool[b * 6 + f] = value

    def faces_of_body(b, pool):
        for f in range(6):
            edge = 7 * (f % 2)
            if f < 2:
                rows = [body_s[b, pl.ds(column(edge + 1, y + 1) + 8, 8), :] for y in range(8)]
            elif f < 4:
                rows = [body_s[b, pl.ds(column(x + 1, edge + 1) + 8, 8), :] for x in range(8)]
            else:
                rows = [
                    body_s[b, pl.ds(column(x + 1, 1) + 8 + edge, 8, stride=PITCH), :]
                    for x in range(8)
                ]
            value = jnp.concatenate(rows, axis=0).astype(pool.dtype)
            own[b * 6 + f] = value
            pool[b * 6 + f] = value

    def send_halo(pool, halo, kind):
        def pack_halo(b, carry):
            for side in range(2):
                halo[side, b] = own[b * 6 + face_pick[b * 2 + side]]
            return carry

        lax.fori_loop(0, count, pack_halo, 0)
        down = pltpu.make_async_remote_copy(
            src_ref=halo.at[0],
            dst_ref=pool.at[pl.ds(7 * count, count)],
            send_sem=halo_sends.at[kind, 0],
            recv_sem=halo_receives.at[kind, 0],
            device_id=behind,
            device_id_type=MESH,
        )
        up_copy = pltpu.make_async_remote_copy(
            src_ref=halo.at[1],
            dst_ref=pool.at[pl.ds(6 * count, count)],
            send_sem=halo_sends.at[kind, 1],
            recv_sem=halo_receives.at[kind, 1],
            device_id=ahead,
            device_id_type=MESH,
        )

        @pl.when(has_ahead)
        def _():
            up_copy.start()

        @pl.when(has_behind)
        def _():
            down.start()

        return down, up_copy

    def wait_halo(copies):
        down, up_copy = copies

        @pl.when(has_ahead)
        def _():
            down.wait_recv()

        @pl.when(has_behind)
        def _():
            up_copy.wait_recv()

    def finish_halo(copies):
        down, up_copy = copies

        @pl.when(has_ahead)
        def _():
            up_copy.wait_send()

        @pl.when(has_behind)
        def _():
            down.wait_send()

    def upsample(b, carry):
        for half in range(2):
            values = recv_p[origin[b], :, half * 128 : (half + 1) * 128].astype(jnp.float32)
            for c in range(2):
                spread[c * 2 + half, pl.ds(c, 64, stride=2), :] = values
        rows = jnp.concatenate([spread[p] for p in range(4)], axis=1).astype(jnp.bfloat16)
        for a in range(2):
            for e in range(2):
                tap = a * 4 + e * 2
                weight = jnp.concatenate([up[tap], up[tap + 1]], axis=0)
                value = jnp.dot(rows, weight, preferred_element_type=jnp.float32)
                for i in range(4):
                    for j in range(4):
                        at = (2 * i + a) * 64 + (2 * j + e) * 8
                        whole[b, at : at + 8] = value[(i * 4 + j) * 8 : (i * 4 + j) * 8 + 8]

        faces(b, pool_c)
        return carry

    lax.fori_loop(0, count, upsample, 0)
    halo_copies = send_halo(pool_c, halo_c, 0)
    for copy in shell_copies[early:far] + inside_copies[far:] + inside_copies[:far]:
        copy.start()

    def surround(b, pool, body):
        def taken(step):
            return pool.at[spots[b * 26 + direction_of[step]]]

        def part(step, low, high):
            return taken(step)[low:high].astype(jnp.float32)

        for ox in (-1, 1):
            u, ex = (0, 7) if ox < 0 else (9, 0)
            value = part((ox, 0, 0), 0, 64)
            for y in range(8):
                body[column(u, y + 1) + 8 : column(u, y + 1) + 16] = value[y * 8 : y * 8 + 8]
            for oy in (-1, 1):
                v, ey = (0, 7) if oy < 0 else (9, 0)
                low = ey * 8 // 16 * 16
                value = part((ox, oy, 0), low, low + 16)
                body[column(u, v) + 8 : column(u, v) + 16] = value[ey * 8 - low : ey * 8 - low + 8]
        for oy in (-1, 1):
            v = 0 if oy < 0 else 9
            value = part((0, oy, 0), 0, 64)
            for x in range(8):
                body[column(x + 1, v) + 8 : column(x + 1, v) + 16] = value[x * 8 : x * 8 + 8]
        for p, oz in enumerate((-1, 1)):
            z = 7 if oz < 0 else 16
            value = part((0, 0, oz), 0, 64)
            for x in range(8):
                body[pl.ds(column(x + 1, 1) + z, 8, stride=PITCH), :] = value[x * 8 : x * 8 + 8]
            for ox in (-1, 1):
                u, ex = (0, 7) if ox < 0 else (9, 0)
                low = ex * 8 // 16 * 16
                value = part((ox, 0, oz), low, low + 16)
                body[pl.ds(column(u, 1) + z, 8, stride=PITCH), :] = value[
                    ex * 8 - low : ex * 8 - low + 8
                ]
                for oy in (-1, 1):
                    v, ey = (0, 7) if oy < 0 else (9, 0)
                    value = part((ox, oy, oz), low, low + 16)
                    row = ex * 8 + ey - low
                    body[column(u, v) + z : column(u, v) + z + 1] = value[row : row + 1]
            for q, oy in enumerate((-1, 1)):
                v, ey = (0, 7) if oy < 0 else (9, 0)
                ghost[p * 2 + q] = part((0, oy, oz), 0, 64)
                body[pl.ds(column(1, v) + z, 8, stride=10 * PITCH), :] = ghost[
                    p * 2 + q, pl.ds(ey, 8, stride=8), :
                ]
    def shifts(body, even, odd):
        for dz in range(3):
            for u in range(10):
                blocks = [
                    body[column(u, v) + 7 + dz : column(u, v) + 15 + dz] for v in range(10)
                ]
                even[dz, u * 80 : u * 80 + 80] = jnp.concatenate(blocks, axis=0).astype(even.dtype)
                odd[dz, u * 64 : u * 64 + 64] = jnp.concatenate(blocks[1:9], axis=0).astype(
                    odd.dtype
                )

    wait_halo(halo_copies)

    def child_half(b, carry):
        for x in range(8):
            for y in range(8):
                at = column(x + 1, y + 1) + 8
                body[at : at + 8] = whole[b, x * 64 + y * 8 : x * 64 + y * 8 + 8]
        surround(b, pool_c, body)
        shifts(body, even, odd)
        acc[b] = product(even, odd, right)
        return carry

    lax.fori_loop(0, count, child_half, 0)

    for copy in shell_copies:
        copy.wait_recv()
    mine[1].wait()
    def outer_voxels(b, carry):
        outer = recv_shell[origin[count + b]].astype(jnp.float32)
        padded = body_s.at[b]
        for y in range(8):
            padded[column(1, y + 1) + 8 : column(1, y + 1) + 16] = outer[y * 8 : y * 8 + 8]
            padded[column(8, y + 1) + 8 : column(8, y + 1) + 16] = outer[64 + y * 8 : 72 + y * 8]
        for x in range(1, 7):
            at = 112 + x * 16
            padded[column(x + 1, 1) + 8 : column(x + 1, 1) + 16] = outer[at : at + 8]
            padded[column(x + 1, 8) + 8 : column(x + 1, 8) + 16] = outer[at + 8 : at + 16]
        strip[0:80] = outer[224:304]
        for i in range(12):
            at = column(i % 6 + 2, 2) + 8 + i // 6 * 7
            padded[pl.ds(at, 6, stride=PITCH), :] = strip[6 * i : 6 * i + 6]
        faces_of_body(b, pool_s)
        return carry

    lax.fori_loop(0, count, outer_voxels, 0)
    skip_halo = send_halo(pool_s, halo_s, 1)
    for copy in flag_copies:
        copy.wait_recv()
    enough = flags[0, 0]
    for d in range(1, n_gy):
        enough = lax.min(enough, flags[d, 0])
    agree[0] = enough
    agrees[gx, 0] = enough
    agree_copies = [
        pltpu.make_async_remote_copy(
            src_ref=agree,
            dst_ref=agrees.at[gx],
            send_sem=agree_sends.at[step],
            recv_sem=agree_receives.at[step],
            device_id={"gx": lax.rem(gx + step, n_gx)},
            device_id_type=MESH,
        )
        for step in range(1, n_gx)
    ]
    for copy in agree_copies:
        copy.start()
    wait_halo(skip_halo)
    def surround_skip(b, carry):
        surround(b, pool_s, body_s.at[b])
        return carry

    lax.fori_loop(0, count, surround_skip, 0)

    for copy in inside_copies:
        copy.wait_recv()
    mine[2].wait()
    def inner_voxels(b, carry):
        padded = body_s.at[b]
        strip[80:304] = recv_inside[origin[count + b]].astype(jnp.float32)
        for i in range(36):
            at = column(i // 6 + 2, i % 6 + 2) + 9
            padded[at : at + 6] = strip[80 + 6 * i : 86 + 6 * i]
        shifts(padded, even_s.at[b], odd_s.at[b])
        return carry

    lax.fori_loop(0, count, inner_voxels, 0)

    for copy in mark_copies + parent_copies + shell_copies + inside_copies + flag_copies:
        copy.wait_send()
    finish_halo(halo_copies)
    finish_halo(skip_halo)
    for copy in agree_copies:
        copy.wait()
    for x in range(n_gx):
        enough = lax.min(enough, agrees[x, 0])
    agreed[0] = enough

def finish_kernel(acc, even, odd, right, out, result, sems):
    copies = []
    for b in range(acc.shape[0]):
        made = acc.shape[2] // 2
        total = acc[b] + product(even.at[b], odd.at[b], right)
        total = jnp.maximum(total, 0.0).astype(result.dtype)
        for s in range(4):
            for p in range(2):
                at = (2 * s + p) * 64
                result[b, at : at + 64] = total[s * 64 : s * 64 + 64, p * made : (p + 1) * made]
        copies.append(pltpu.make_async_copy(result.at[b], out.at[b], sems.at[b]))
        copies[-1].start()
    for copy in copies:
        copy.wait()


def finish(acc, even, odd, right):
    count, made = acc.shape[0], acc.shape[2] // 2
    shape = (count, 2 * acc.shape[1], made)
    return pl.pallas_call(
        finish_kernel,
        out_shape=pltpu.HBM(shape, jnp.bfloat16),
        in_specs=[vmem()] * 4,
        out_specs=pl.BlockSpec(memory_space=pltpu.HBM),
        scratch_shapes=[
            pltpu.VMEM(shape, jnp.bfloat16),
            pltpu.SemaphoreType.DMA((count,)),
        ],
        compiler_params=pltpu.CompilerParams(vmem_limit_bytes=24 * 2**20),
        name="finish",
    )(acc, even, odd, right)


META = 8


def vmem():
    return pl.BlockSpec(memory_space=pltpu.VMEM)


def pack_kernel(
    gy_count, bricks_dev, pdest, sdest, parents, skip, out_p, out_s, land, sem_p, sem_s
):
    slots, voxels = parents.shape[0], parents.shape[1]
    for d in range(gy_count):
        land[0, d] = -1
        land[1, d] = -1

    def copies(s):
        tp, ts = pdest[s], sdest[s]
        op = lax.rem(lax.div(jnp.maximum(tp, 0), bricks_dev), gy_count)
        os = lax.rem(lax.div(jnp.maximum(ts, 0), bricks_dev), gy_count)
        cp = pltpu.make_async_copy(parents.at[s], out_p.at[op, pl.ds(0, voxels)], sem_p.at[s])
        cs = pltpu.make_async_copy(skip.at[s], out_s.at[os], sem_s.at[s])
        return (tp, op, cp), (ts, os, cs)

    for s in range(slots):
        for which, (t, o, c) in enumerate(copies(s)):

            @pl.when(t >= 0)
            def _():
                land[which, o] = lax.rem(t, bricks_dev)
                c.start()

    for d in range(gy_count):
        half = parents.shape[2] // 2
        for which in range(2):
            mark = jnp.full((META, half), land[which, d], jnp.int32).astype(jnp.float32)
            out_p[d, voxels : voxels + META, which * half : (which + 1) * half] = mark.astype(
                jnp.bfloat16
            )
    for s in range(slots):
        for t, o, c in copies(s):

            @pl.when(t >= 0)
            def _():
                c.wait()


def pack(parent_dest, skip_dest, parents, skip, bricks_dev, gy_count):
    slots, voxels, channels = parents.shape
    return pl.pallas_call(
        functools.partial(pack_kernel, gy_count, bricks_dev),
        out_shape=(
            jax.ShapeDtypeStruct((gy_count, voxels + META, channels), parents.dtype),
            jax.ShapeDtypeStruct((gy_count,) + skip.shape[1:], skip.dtype),
        ),
        in_specs=[smem(), smem(), anywhere(), anywhere()],
        out_specs=(vmem(), vmem()),
        scratch_shapes=[
            pltpu.SMEM((2, gy_count), jnp.int32),
            pltpu.SemaphoreType.DMA((slots,)),
            pltpu.SemaphoreType.DMA((slots,)),
        ],
        compiler_params=pltpu.CompilerParams(vmem_limit_bytes=VMEM_LIMIT),
        name="pack",
    )(parent_dest, skip_dest, parents, skip)


def exchange_kernel(gy_count, in_p, in_s, out_p, out_s, sends, receives, own):
    me = lax.axis_index("gy")
    mine = [
        pltpu.make_async_copy(in_p.at[me], out_p.at[me], own.at[0]),
        pltpu.make_async_copy(in_s.at[me], out_s.at[me], own.at[1]),
    ]
    for copy in mine:
        copy.start()
    barrier = pltpu.get_barrier_semaphore()
    shifts = sorted(range(1, gy_count), key=lambda s: abs(s - gy_count // 2))
    for shift in shifts:
        pl.semaphore_signal(
            barrier,
            inc=1,
            device_id={"gy": lax.rem(me + shift, gy_count)},
            device_id_type=pl.DeviceIdType.MESH,
        )
    pl.semaphore_wait(barrier, gy_count - 1)
    copies = []
    for which, (source, landing) in enumerate(((in_p, out_p), (in_s, out_s))):
        for shift in shifts:
            there = lax.rem(me + shift, gy_count)
            copy = pltpu.make_async_remote_copy(
                src_ref=source.at[there],
                dst_ref=landing.at[me],
                send_sem=sends.at[which, shift],
                recv_sem=receives.at[which, shift],
                device_id={"gy": there},
                device_id_type=pl.DeviceIdType.MESH,
            )
            copy.start()
            copies.append(copy)
    for copy in copies:
        copy.wait()
    for copy in mine:
        copy.wait()


def exchange(in_p, in_s):
    gy_count = in_p.shape[0]
    return pl.pallas_call(
        functools.partial(exchange_kernel, gy_count),
        out_shape=tuple(jax.ShapeDtypeStruct(a.shape, a.dtype) for a in (in_p, in_s)),
        in_specs=[anywhere(), anywhere()],
        out_specs=(anywhere(), anywhere()),
        scratch_shapes=[
            pltpu.SemaphoreType.DMA((2, gy_count)),
            pltpu.SemaphoreType.DMA((2, gy_count)),
            pltpu.SemaphoreType.DMA((2,)),
        ],
        compiler_params=pltpu.CompilerParams(
            collective_id=2, has_side_effects=True, vmem_limit_bytes=2**20
        ),
        name="exchange",
    )(in_p, in_s)


def halo_kernel(size, inner, to_before, to_after, from_before, from_after, sends, receives):
    me = lax.axis_index("gx") * inner + lax.axis_index("gy")

    def coordinates(device):
        device = lax.max(device, 0)
        return (lax.div(device, inner), lax.rem(device, inner))

    ahead, behind = coordinates(me + 1), coordinates(me - 1)
    has_ahead, has_behind = me < size - 1, me > 0
    barrier = pltpu.get_barrier_semaphore()
    mesh_id = pl.DeviceIdType.MESH

    @pl.when(has_ahead)
    def _():
        pl.semaphore_signal(barrier, inc=1, device_id=ahead, device_id_type=mesh_id)

    @pl.when(has_behind)
    def _():
        pl.semaphore_signal(barrier, inc=1, device_id=behind, device_id_type=mesh_id)

    pl.semaphore_wait(barrier, has_ahead.astype(jnp.int32) + has_behind.astype(jnp.int32))
    up = pltpu.make_async_remote_copy(
        src_ref=to_after,
        dst_ref=from_before,
        send_sem=sends.at[0],
        recv_sem=receives.at[0],
        device_id=ahead,
        device_id_type=mesh_id,
    )
    down = pltpu.make_async_remote_copy(
        src_ref=to_before,
        dst_ref=from_after,
        send_sem=sends.at[1],
        recv_sem=receives.at[1],
        device_id=behind,
        device_id_type=mesh_id,
    )

    @pl.when(has_ahead)
    def _():
        up.start()

    @pl.when(has_behind)
    def _():
        down.start()

    @pl.when(has_ahead)
    def _():
        up.wait_send()
        down.wait_recv()

    @pl.when(has_behind)
    def _():
        down.wait_send()
        up.wait_recv()


def halo(to_before, to_after):
    inner = lax.axis_size("gy")
    size = lax.axis_size("gx") * inner
    return pl.pallas_call(
        functools.partial(halo_kernel, size, inner),
        out_shape=(
            jax.ShapeDtypeStruct(to_after.shape, to_after.dtype),
            jax.ShapeDtypeStruct(to_before.shape, to_before.dtype),
        ),
        in_specs=[anywhere(), anywhere()],
        out_specs=(anywhere(), anywhere()),
        scratch_shapes=[pltpu.SemaphoreType.DMA((2,)), pltpu.SemaphoreType.DMA((2,))],
        compiler_params=pltpu.CompilerParams(
            collective_id=1, has_side_effects=True, vmem_limit_bytes=2**20
        ),
        name="halo",
    )(to_before, to_after)


def build_kernel(
    source, near, pay, skip, up, feats, faces, before, after, spread, whole, sent
):
    channels = up.shape[1]
    made = up.shape[2]

    @pl.when(pl.program_id(0) == 0)
    def _():
        spread[...] = jnp.zeros_like(spread)

    for half in range(channels // 128):
        values = pay[0, 0:64, half * 128 : (half + 1) * 128].astype(jnp.float32)
        for c in range(2):
            spread[c * (channels // 128) + half, pl.ds(c, 64, stride=2), :] = values
    rows = jnp.concatenate([spread[p] for p in range(spread.shape[0])], axis=1).astype(jnp.bfloat16)
    for a in range(2):
        for b in range(2):
            tap = a * 4 + b * 2
            weight = jnp.concatenate([up[tap], up[tap + 1]], axis=0)
            value = jnp.dot(rows, weight, preferred_element_type=jnp.float32)
            for i in range(4):
                for j in range(4):
                    at = (2 * i + a) * 64 + (2 * j + b) * 8
                    for p in range(made // 128):
                        whole[p, at : at + 8] = value[
                            (i * 4 + j) * 8 : (i * 4 + j) * 8 + 8, p * 128 : (p + 1) * 128
                        ]
    for p in range(made // 128, whole.shape[0]):
        at = p * 128 - made
        whole[p] = skip[0, :, at : at + 128].astype(jnp.float32)
    for p in range(whole.shape[0]):
        lanes = slice(p * 128, (p + 1) * 128)
        feats[0, :, lanes] = whole[p].astype(jnp.bfloat16)
        for side in range(2):
            edge = 7 * side
            faces[0, side, :, lanes] = whole[p, edge * 64 : edge * 64 + 64].astype(jnp.bfloat16)
            faces[0, 2 + side, :, lanes] = jnp.concatenate(
                [whole[p, x * 64 + edge * 8 : x * 64 + edge * 8 + 8] for x in range(8)], axis=0
            ).astype(jnp.bfloat16)
            faces[0, 4 + side, :, lanes] = whole[p, pl.ds(edge, 64, stride=8), :].astype(
                jnp.bfloat16
            )
    brick = pl.program_id(0)
    count = before.shape[1]
    first = (lax.axis_index("gx") * lax.axis_size("gy") + lax.axis_index("gy")) * count
    for m in range(2 * count):
        sent[m] = 0
    for k, face in enumerate(face_of[::-1]):
        n = near[brick, k]
        off = n - first
        spot = jnp.where(off < 0, off + count, jnp.where(off >= count, off, 2 * count))
        sent[jnp.where(n >= 0, spot, 2 * count)] = face
    for m in range(count):
        before[0, m] = faces[0, sent[m]]
        after[0, m] = faces[0, sent[count + m]]


def build(source, near, pay, skip, up_weight, bricks_dev):
    channels, made = up_weight.shape[1:]
    joined = made + skip.shape[2]
    return pl.pallas_call(
        build_kernel,
        out_shape=(
            jax.ShapeDtypeStruct((bricks_dev, 512, joined), jnp.bfloat16),
            jax.ShapeDtypeStruct((bricks_dev, 6, 64, joined), jnp.bfloat16),
            jax.ShapeDtypeStruct((bricks_dev, bricks_dev, 64, joined), jnp.bfloat16),
            jax.ShapeDtypeStruct((bricks_dev, bricks_dev, 64, joined), jnp.bfloat16),
        ),
        grid_spec=pltpu.PrefetchScalarGridSpec(
            num_scalar_prefetch=2,
            grid=(bricks_dev,),
            in_specs=[
                pl.BlockSpec((1,) + pay.shape[1:], lambda b, s, t: (s[0, b], 0, 0)),
                pl.BlockSpec((1,) + skip.shape[1:], lambda b, s, t: (s[1, b], 0, 0)),
                pl.BlockSpec(up_weight.shape, lambda b, s, t: (0, 0, 0)),
            ],
            out_specs=(
                pl.BlockSpec((1, 512, joined), lambda b, s, t: (b, 0, 0)),
                pl.BlockSpec((1, 6, 64, joined), lambda b, s, t: (b, 0, 0, 0)),
                pl.BlockSpec((1, bricks_dev, 64, joined), lambda b, s, t: (b, 0, 0, 0)),
                pl.BlockSpec((1, bricks_dev, 64, joined), lambda b, s, t: (b, 0, 0, 0)),
            ),
            scratch_shapes=[
                pltpu.VMEM((2 * channels // 128, 128, 128), jnp.float32),
                pltpu.VMEM((joined // 128, 512, 128), jnp.float32),
                pltpu.SMEM((2 * bricks_dev + 1,), jnp.int32),
            ],
        ),
        compiler_params=pltpu.CompilerParams(vmem_limit_bytes=VMEM_LIMIT),
        name="build",
    )(source, near, pay, skip, up_weight)


def refine_kernel(
    near,
    feats,
    own,
    before,
    after,
    weight,
    out,
    pool,
    sems,
    body,
    plane,
    left,
    right,
    early,
    late,
):
    brick = pl.program_id(0)
    joined, made = weight.shape[1:]

    @pl.when(brick == 0)
    def _():
        copies, first = [], 0
        for i, part in enumerate((own, before, after)):
            length = part.shape[0]
            copies.append(pltpu.make_async_copy(part, pool.at[pl.ds(first, length)], sems.at[i]))
            copies[-1].start()
            first += length
        for tap in range(9):
            for dz in range(3):
                right[tap * joined : (tap + 1) * joined, dz * made : (dz + 1) * made] = weight[
                    tap * 3 + dz
                ]
        for copy in copies:
            copy.wait()

    count = pl.num_programs(0)
    first = (lax.axis_index("gx") * lax.axis_size("gy") + lax.axis_index("gy")) * count
    ahead = own.shape[0] + count * count + brick
    behind = before.shape[0] - 2 * count * count

    def taken(step, start, length):
        k = direction_of[step]
        n = near[brick, k]
        off = n - first
        spot = jnp.where(off < 0, ahead + off * count, ahead + behind + off * count)
        spot = jnp.where((off >= 0) & (off < count), off * 6 + face_of[k], spot)
        spot = jnp.where(n >= 0, spot, 0)
        low = start // 16 * 16
        high = -(-(start + length) // 16) * 16
        value = pool[spot, low:high, :].astype(jnp.float32)
        return jnp.where(n >= 0, value[start - low : start - low + length], 0.0)

    body[1:9, 1:9] = feats[0].astype(jnp.float32).reshape(8, 8, 8, joined)
    for ox in (-1, 1):
        u = 0 if ox < 0 else 9
        body[u, 1:9] = taken((ox, 0, 0), 0, 64).reshape(8, 8, joined)
        for oy in (-1, 1):
            v, ey = (0, 7) if oy < 0 else (9, 0)
            body[u, v] = taken((ox, oy, 0), ey * 8, 8)
    for oy in (-1, 1):
        v = 0 if oy < 0 else 9
        body[1:9, v] = taken((0, oy, 0), 0, 64).reshape(8, 8, joined)
    for p, oz in enumerate((-1, 1)):
        plane[p, 1:9, 1:9] = taken((0, 0, oz), 0, 64).reshape(8, 8, joined)
        for ox in (-1, 1):
            u, ex = (0, 7) if ox < 0 else (9, 0)
            plane[p, u, 1:9] = taken((ox, 0, oz), ex * 8, 8)
            for oy in (-1, 1):
                v, ey = (0, 7) if oy < 0 else (9, 0)
                row = taken((ox, oy, oz), ex * 8, 8)
                plane[p, u, v : v + 1] = row[ey : ey + 1]
        for oy in (-1, 1):
            v, ey = (0, 7) if oy < 0 else (9, 0)
            value = taken((0, oy, oz), 0, 64).reshape(8, 8, joined)
            plane[p, 1:9, v : v + 1] = value[:, ey : ey + 1]

    for tap in range(9):
        dx, dy = tap // 3, tap % 3
        lanes = slice(tap * joined, (tap + 1) * joined)
        left[0:512, lanes] = (
            body[dx : dx + 8, dy : dy + 8].reshape(512, joined).astype(jnp.bfloat16)
        )
        for p in range(2):
            left[512 + 64 * p : 576 + 64 * p, lanes] = (
                plane[p, dx : dx + 8, dy : dy + 8].reshape(64, joined).astype(jnp.bfloat16)
            )
    total = jnp.dot(left[...], right[...], preferred_element_type=jnp.float32)
    early[1:513] = total[0:512, 0:made]
    early[pl.ds(0, 64, stride=8), :] = total[512:576, 0:made]
    late[7:519] = total[0:512, 2 * made : 3 * made]
    late[pl.ds(15, 64, stride=8), :] = total[576:640, 2 * made : 3 * made]
    result = early[0:512] + total[0:512, made : 2 * made] + late[8:520]
    out[0] = jnp.maximum(result, 0.0).astype(jnp.bfloat16)


def refine(near, feats, own, before, after, conv_weight):
    bricks_dev, voxels, joined = feats.shape
    made = conv_weight.shape[2]
    return pl.pallas_call(
        refine_kernel,
        out_shape=jax.ShapeDtypeStruct((bricks_dev, voxels, made), jnp.bfloat16),
        grid_spec=pltpu.PrefetchScalarGridSpec(
            num_scalar_prefetch=1,
            grid=(bricks_dev,),
            in_specs=[
                pl.BlockSpec((1, voxels, joined), lambda b, s: (b, 0, 0)),
                anywhere(),
                anywhere(),
                anywhere(),
                pl.BlockSpec(conv_weight.shape, lambda b, s: (0, 0, 0)),
            ],
            out_specs=pl.BlockSpec((1, voxels, made), lambda b, s: (b, 0, 0)),
            scratch_shapes=[
                pltpu.VMEM((sum(a.shape[0] for a in (own, before, after)), 64, joined), own.dtype),
                pltpu.SemaphoreType.DMA((3,)),
                pltpu.VMEM((10, 10, 8, joined), jnp.float32),
                pltpu.VMEM((2, 10, 16, joined), jnp.float32),
                pltpu.VMEM((640, 9 * joined), jnp.bfloat16),
                pltpu.VMEM((9 * joined, 3 * made), jnp.bfloat16),
                pltpu.VMEM((520, made), jnp.float32),
                pltpu.VMEM((520, made), jnp.float32),
            ],
        ),
        compiler_params=pltpu.CompilerParams(vmem_limit_bytes=VMEM_LIMIT),
        name="refine",
    )(near, feats, own, before, after, conv_weight)


def general(parents, parent_dest, skip, skip_dest, neighbours, up_weight, conv_weight):
    bricks_dev = neighbours.shape[0]
    gy_count = lax.axis_size("gy")
    sent_p, sent_s = pack(parent_dest, skip_dest, parents, skip, bricks_dev, gy_count)
    came_p, came_s = exchange(sent_p, sent_s)
    voxels, channels = parents.shape[1:]
    spots = jnp.stack([came_p[:, voxels, 0], came_p[:, voxels, channels // 2]]).astype(jnp.int32)
    matches = spots[:, None, :] == jnp.arange(bricks_dev)[None, :, None]
    source = jnp.sum(jnp.where(matches, jnp.arange(gy_count)[None, None, :], 0), axis=2)
    feats, faces, to_before, to_after = build(
        source.astype(jnp.int32), neighbours, came_p, came_s, up_weight, bricks_dev
    )
    flat = (-1,) + faces.shape[2:]
    before, after = halo(to_before.reshape(flat), to_after.reshape(flat))
    return refine(neighbours, feats, faces.reshape(flat), before, after, conv_weight)


def per_device(parents, parent_dest, skip, skip_dest, neighbours, up_weight, conv_weight):
    count = neighbours.shape[0]
    n_gx, n_gy = lax.axis_size("gx"), lax.axis_size("gy")
    voxels = skip.shape[1]
    made = conv_weight.shape[2]
    bf16, f32 = jnp.bfloat16, jnp.float32
    pool = (8 * count + 1, 64, made)
    dma = pltpu.SemaphoreType.DMA
    width = 2 * made
    acc, even, odd, right, agreed = pl.pallas_call(
        functools.partial(kernel, n_gx, n_gy),
        out_shape=(
            pltpu.VMEM((count, voxels // 2, width), f32),
            pltpu.VMEM((count, 3, 800, made), bf16),
            pltpu.VMEM((count, 3, 640, made), bf16),
            pltpu.VMEM((36 * made, width), bf16),
            jax.ShapeDtypeStruct((1,), jnp.int32),
        ),
        in_specs=[anywhere()] * 7,
        out_specs=(vmem(), vmem(), vmem(), vmem(), smem()),
        scratch_shapes=[
            pltpu.SMEM(parent_dest.shape, jnp.int32),
            pltpu.SMEM(skip_dest.shape, jnp.int32),
            pltpu.SMEM(neighbours.shape, jnp.int32),
            pltpu.VMEM(parents.shape, bf16),
            pltpu.VMEM(skip.shape, bf16),
            pltpu.VMEM(up_weight.shape, bf16),
            pltpu.VMEM(conv_weight.shape, bf16),
            pltpu.VMEM((n_gy,) + parents.shape[1:], bf16),
            pltpu.VMEM((n_gy, 304, skip.shape[2]), bf16),
            pltpu.VMEM((n_gy, 224, skip.shape[2]), bf16),
            pltpu.VMEM((n_gy,) + parents.shape[1:], bf16),
            pltpu.VMEM((n_gy, 304, skip.shape[2]), bf16),
            pltpu.VMEM((n_gy, 224, skip.shape[2]), bf16),
            pltpu.SMEM((2 * n_gy,), jnp.int32),
            pltpu.SMEM((n_gy, 2 * n_gy), jnp.int32),
            pltpu.SMEM((2 * n_gy,), jnp.int32),
            pltpu.SMEM((2 * count,), jnp.int32),
            pltpu.SMEM((1,), jnp.int32),
            pltpu.SMEM((n_gy, 1), jnp.int32),
            pltpu.VMEM((voxels, skip.shape[2]), f32),
            pltpu.VMEM((304, skip.shape[2]), f32),
            pltpu.SMEM((1,), jnp.int32),
            pltpu.SMEM((n_gx, 1), jnp.int32),
            pltpu.SMEM((2 * count,), jnp.int32),
            pltpu.SMEM((26 * count,), jnp.int32),
            pltpu.VMEM((4, 128, 128), f32),
            pltpu.VMEM((count, voxels, made), f32),
            pltpu.VMEM((4, 64, made), f32),
            pltpu.VMEM((6 * count, 64, made), bf16),
            pltpu.VMEM(pool, bf16),
            pltpu.VMEM(pool, bf16),
            pltpu.VMEM((2, count, 64, made), bf16),
            pltpu.VMEM((2, count, 64, made), bf16),
            pltpu.VMEM((100 * PITCH, made), f32),
            pltpu.VMEM((count, 100 * PITCH, made), f32),
            pltpu.VMEM((3, 800, made), bf16),
            pltpu.VMEM((3, 640, made), bf16),
            pltpu.VMEM((36 * made, width), bf16),
            dma((7,)),
            dma((5, n_gy)),
            dma((5, n_gy)),
            dma((2, 2)),
            dma((2, 2)),
            dma((3,)),
            dma((n_gx,)),
            dma((n_gx,)),
        ],
        compiler_params=pltpu.CompilerParams(
            collective_id=0, has_side_effects=True, vmem_limit_bytes=40 * 2**20
        ),
        name="refine_level",
    )(parent_dest, skip_dest, neighbours, parents, skip, up_weight, conv_weight)
    return lax.switch(
        agreed[0],
        [
            lambda: general(
                parents, parent_dest, skip, skip_dest, neighbours, up_weight, conv_weight
            ),
            lambda: finish(acc, even, odd, right),
        ],
    )


def solution(mesh):
    placed = (
        P(("gx", "gy"), None, None),
        P(("gx", "gy")),
        P(("gx", "gy"), None, None),
        P(("gx", "gy")),
        P(("gx", "gy"), None),
        P(),
        P(),
    )
    return jax.shard_map(
        per_device,
        mesh=mesh,
        in_specs=placed,
        out_specs=P(("gx", "gy"), None, None),
        check_vma=False,
    )
```
